32 devices in a mesh: dp: 16 (over z, y, core), mp: 2 (over x).
Axes of the slice: x: 2, y: 2, z: 4, core: 2. Of those that a mesh axis runs over, the one named last changes fastest.
Arguments:
- tokens: bfloat16 [2048, 2048], P(('dp', 'mp')), may hold values from -6 to 6
- lengths: int32 [22], replicated, may hold values from 1 to 1024, 2048 in all
- w_in: bfloat16 [2048, 2048], P('dp'), may hold values from -0.125 to 0.125
- w_forget: bfloat16 [2048, 2048], P('dp'), may hold values from -0.125 to 0.125
- w_gate: bfloat16 [2048, 2048], P('dp'), may hold values from -0.125 to 0.125
- w_out: bfloat16 [2048, 2048], P('dp'), may hold values from -0.125 to 0.125
- attn_gain: bfloat16 [2048], P('dp'), may hold values from 0.5 to 1.5
- mix_gain: bfloat16 [2048], P('dp'), may hold values from 0.5 to 1.5
- bound_table: bfloat16 [24, 2048], P(None, 'dp'), may hold values from -14 to 3
- ff_gate: bfloat16 [2048, 5632], P('dp', 'mp'), may hold values from -0.125 to 0.125
- ff_up: bfloat16 [2048, 5632], P('dp', 'mp'), may hold values from -0.125 to 0.125
- ff_down: bfloat16 [5632, 2048], P('mp', 'dp'), may hold values from -0.078125 to 0.078125
- mlp_gain: bfloat16 [2048], P('dp'), may hold values from 0.5 to 1.5
- out_grad: bfloat16 [2048, 2048], P(('dp', 'mp')), may hold values from -6 to 6
Outputs:
- result: bfloat16 [2048, 2048], P(('dp', 'mp'))
- token_grad: float32 [2048, 2048], P(('dp', 'mp'))
- grad_w_in: float32 [2048, 2048], P('dp')
- grad_w_forget: float32 [2048, 2048], P('dp')
- grad_w_gate: float32 [2048, 2048], P('dp')
- grad_w_out: float32 [2048, 2048], P('dp')
- grad_attn_gain: float32 [2048], P('dp')
- grad_mix_gain: float32 [2048], P('dp')
- grad_bound_table: float32 [24, 2048], P(None, 'dp')
- grad_ff_gate: float32 [2048, 5632], P('dp', 'mp')
- grad_ff_up: float32 [2048, 5632], P('dp', 'mp')
- grad_ff_down: float32 [5632, 2048], P('mp', 'dp')
- grad_mlp_gain: float32 [2048], P('dp')
The draws below stay inside these ranges and needn't reach their ends.
Inputs may be any that keep to these rules, and one draw needn't show every extreme that they name: lengths of 22 sequences packed end to end; they sum to 2048 and the longest is 1024.
All inputs are finite; a program needn't handle non-finite values.
Results may differ from the reference program's by a relative error of at most 0.0085.
Values may be sent and summed in bfloat16 or wider, within the bound.
No kernel may reach another device: no remote copies, remote signals or barrier semaphores. Data moves between devices by JAX's collectives and lax.ppermute only.
A program may use at most 384 MiB of HBM per device.

```python
import math
from functools import partial
import jax
import jax.numpy as jnp
import numpy as np
from jax import lax

D = 2048
FF = 5632
LAYERS = 24
LAYER = 12
NSEQ = 22
TOKENS = 2048
MAXLEN = 1024


def draw_bound_table(key, part):
    first_key, second_key = jax.random.split(key, 2)
    log_low, log_high = (-8.5, -2.5)
    log_rate = jax.random.uniform(first_key, (1, D), jnp.float32, log_low, log_high)
    noise = jax.random.normal(second_key, (LAYERS, D), jnp.float32)
    rows = jnp.arange(LAYERS)[:, None]
    active = jnp.logical_and(rows >= 1, rows <= LAYER)
    scale_fix = jnp.log(jnp.float32(LAYER) / jnp.float32(LAYERS - LAYER))
    values = jnp.where(active, 0.5 * noise, log_rate + scale_fix + 0.3 * noise)
    return jnp.clip(values, -14.0, 3.0).astype(jnp.bfloat16)


def raised(array, rng, source, target, parts, factor):
    def block_of(dim):
        return (jnp.arange(array.shape[dim]) // (array.shape[dim] // parts)).reshape((-1,) + (1,) * (array.ndim - 1 - dim))

    one_side = jax.random.permutation(rng, parts)[block_of(target)]
    other_side = (block_of(target) + parts // 2) % parts
    return jnp.where((block_of(source) == one_side) | (block_of(source) == other_side), factor * array, array)


def steps_of(own_key, shape, shards, least, top_value):
    level = 1.0
    for dim, shards_of in shards:
        draws = jax.random.uniform(jax.random.fold_in(jax.random.fold_in(own_key, 6), dim), (shards_of,), jnp.float32, least / len(shards), top_value / len(shards))
        level = level * jnp.repeat(jnp.exp(draws), shape[dim] // shards_of).reshape((-1,) + (1,) * (len(shape) - 1 - dim))
    return level


def length_profile(count, total, most, slope):
    weights = [(1 << 20) // math.isqrt(grade ** slope) + 1 for grade in range(2, count + 1)]
    spare, given = total - most - (count - 1), [1] * (count - 1)
    while spare > 0:
        movable = [i for i in range(count - 1) if given[i] < most]
        whole, budget = sum([weights[i] for i in movable]), spare
        for i in movable:
            more = min(most - given[i], max(1, budget * weights[i] // whole), spare)
            given[i] = given[i] + more
            spare = spare - more
    return np.array([most] + given)


def ragged_sizes(own_key, count, total, reach, lean):
    if count == 2:
        one = jax.random.randint(own_key, (), max(1, total - reach), min(reach, total - 1) + 1)
        return jnp.stack([one, total - one])
    sizes = jnp.asarray(length_profile(count, total, reach, lean), jnp.int32)
    twos = (count - 1) // 2
    source_of, receiver = sizes[1:1 + 2 * twos:2], sizes[2:2 + 2 * twos:2]
    room = jnp.minimum(source_of - 1, reach - receiver)
    shifted = jax.random.randint(jax.random.fold_in(own_key, 1), (twos,), 0, 1 << 20) % (room + 1)
    sizes = sizes.at[1:1 + 2 * twos:2].set(source_of - shifted).at[2:2 + 2 * twos:2].set(receiver + shifted)
    return sizes[jax.random.permutation(jax.random.fold_in(own_key, 2), count)]


def centred(key, extent, deviation, limit, shards=(), kind=jnp.bfloat16):
    array = jax.random.normal(key, extent, jnp.float32) * deviation
    if len(shards) > 0:
        array = steps_of(key, extent, shards, -0.22, 0.18) * array
    return jnp.clip(array, min=-limit, max=limit).astype(kind)


def gaussian_with(key, extent, spread, most, cuts, heavy, kind=jnp.bfloat16):
    entries = spread * jax.random.normal(key, extent, jnp.float32)
    if cuts:
        entries = entries * steps_of(key, extent, cuts, -0.22, 0.18)
    return jnp.clip(raised(entries, jax.random.fold_in(key, 3), *heavy), -most, most).astype(kind)


def setup_inputs(seed: int = 0) -> dict:
    seeds = jax.random.split(jax.random.key(seed), 15)
    return {
        "tokens": gaussian_with(seeds[0], (TOKENS, D), 1.0, 6.0, ((0, 32),), (0, 1, 32, 2.75)),
        "lengths": ragged_sizes(seeds[1], NSEQ, TOKENS, MAXLEN, 2).astype(jnp.int32),
        "w_in": centred(seeds[2], (D, D), D ** -0.5, 0.125, ((0, 16),)),
        "w_forget": centred(seeds[3], (D, D), D ** -0.5, 0.125, ((0, 16),)),
        "w_gate": centred(seeds[4], (D, D), D ** -0.5, 0.125, ((0, 16),)),
        "w_out": centred(seeds[5], (D, D), D ** -0.5, 0.125, ((0, 16),)),
        "attn_gain": jnp.clip(1.0 + 0.1 * jax.random.normal(seeds[6], (D,), jnp.float32), 0.5, 1.5).astype(jnp.bfloat16),
        "mix_gain": jnp.clip(1.0 + 0.1 * jax.random.normal(seeds[7], (D,), jnp.float32), 0.5, 1.5).astype(jnp.bfloat16),
        "bound_table": draw_bound_table(jax.random.fold_in(seeds[14], 71), 0),
        "ff_gate": centred(seeds[9], (D, FF), D ** -0.5, 0.125, ((0, 16), (1, 2))),
        "ff_up": centred(seeds[10], (D, FF), D ** -0.5, 0.125, ((0, 16), (1, 2))),
        "ff_down": centred(seeds[11], (FF, D), FF ** -0.5, 0.078125, ((0, 2), (1, 16))),
        "mlp_gain": jnp.clip(1.0 + 0.1 * jax.random.normal(seeds[12], (D,), jnp.float32), 0.5, 1.5).astype(jnp.bfloat16),
        "out_grad": gaussian_with(seeds[13], (TOKENS, D), 1.0, 6.0, ((0, 32),), (0, 1, 32, 2.75)),
    }


epsilon = 1e-06

@jax.custom_vjp
def low(v):
    return lax.optimization_barrier(v.astype(jnp.bfloat16)).astype(jnp.float32)

@jax.custom_vjp
def low_back(v):
    return v

def low_keep(v):
    return (low(v), None)

def low_pass(kept, grad):
    return (grad,)

def back_keep(v):
    return (v, None)

def back_low(kept, grad):
    return (low(grad),)
low.defvjp(low_keep, low_pass)
low_back.defvjp(back_keep, back_low)

def product(left, right):
    return jnp.dot(left, right, precision=lax.Precision.HIGHEST, preferred_element_type=jnp.float32)

def rms_norm(value, gain):
    return value * lax.rsqrt(lax.optimization_barrier(jnp.mean(value * value, axis=-1, keepdims=True)) + epsilon) * gain

def combine(earlier, later):
    return (earlier[0] * later[0], later[0] * earlier[1] + later[1])

def block_step(weights, carry, inputs):
    w_in, w_forget, w_gate, w_out, attn_gain, mix_gain, bound, ff_gate, ff_up, ff_down, mlp_gain = weights
    rows, keep = inputs
    normed = low(rms_norm(rows, attn_gain))
    inner = low_back(product(normed, w_in))
    forget_raw = low_back(product(normed, w_forget))
    gate_raw = low_back(product(normed, w_gate))
    forget = bound + (1.0 - bound) * jax.nn.sigmoid(forget_raw)
    drive = jax.nn.silu(inner) * (1.0 - forget)
    decay = forget * keep[:, None]
    decay_all, state_all = lax.associative_scan(combine, (decay, drive), axis=0)
    states = decay_all * carry[None, :] + state_all
    mixed_in = low(rms_norm(states, mix_gain) * jax.nn.silu(gate_raw))
    mixed = low_back(product(mixed_in, w_out))
    resid = rows + mixed
    hidden_in = low(rms_norm(resid, mlp_gain))
    gate_ff = low_back(product(hidden_in, ff_gate))
    up_ff = low_back(product(hidden_in, ff_up))
    act = low(jax.nn.silu(gate_ff) * up_ff)
    output = resid + product(act, ff_down)
    return (states[-1], output)

def reference(tokens, lengths, w_in, w_forget, w_gate, w_out, attn_gain, mix_gain, bound_table, ff_gate, ff_up, ff_down, mlp_gain, out_grad):
    starts = (jnp.cumsum(lengths) - lengths).astype(jnp.int32)
    position = jnp.arange(TOKENS, dtype=jnp.int32)
    opening = jnp.any(position[:, None] == starts[None, :], axis=1)
    keep = 1.0 - opening.astype(jnp.float32)
    width = math.gcd(TOKENS, 4096)
    count = TOKENS // width

    def forward(tokens_f, w_in_f, w_forget_f, w_gate_f, w_out_f, attn_f, mix_f, table_f, gate_f, up_f, down_f, mlp_f):
        soft = jax.nn.softmax(table_f, axis=0)
        bound = lax.optimization_barrier(jnp.sum(soft[1:LAYER + 1], axis=0))
        weights = (w_in_f, w_forget_f, w_gate_f, w_out_f, attn_f, mix_f, bound, gate_f, up_f, down_f, mlp_f)
        stepper = jax.checkpoint(partial(block_step, weights))
        start_state = jnp.zeros((D,), jnp.float32)
        final_state, outputs = lax.scan(stepper, start_state, (tokens_f.reshape(count, width, D), keep.reshape(count, width)))
        return outputs.reshape(TOKENS, D)
    inputs = (tokens.astype(jnp.float32), w_in.astype(jnp.float32), w_forget.astype(jnp.float32), w_gate.astype(jnp.float32), w_out.astype(jnp.float32), attn_gain.astype(jnp.float32), mix_gain.astype(jnp.float32), bound_table.astype(jnp.float32), ff_gate.astype(jnp.float32), ff_up.astype(jnp.float32), ff_down.astype(jnp.float32), mlp_gain.astype(jnp.float32))
    output, pullback = jax.vjp(forward, *inputs)
    grads = pullback(out_grad.astype(jnp.float32))
    return (output.astype(jnp.bfloat16), grads[0], grads[1], grads[2], grads[3], grads[4], grads[5], grads[6], grads[7], grads[8], grads[9], grads[10], grads[11])
```

```python
import jax
import jax.numpy as jnp
from jax import lax
from jax.sharding import PartitionSpec as P

LAYER = 12


epsilon = 1e-06


def entering(value, axis, join, neutral, backward):
    count, mine = (lax.axis_size(axis), lax.axis_index(axis))
    pieces = jax.tree.map(lambda part: lax.all_gather(part, axis), value)
    if backward:
        pieces = jax.tree.map(lambda part: part[::-1], pieces)
        mine = count - 1 - mine
    running = jax.tree.map(
        lambda part, zero: jnp.full_like(part, 0) + jnp.asarray(zero, part.dtype), value, neutral
    )

    def turn(position, running):
        longer = join(running, jax.tree.map(lambda part: part[position], pieces))
        return jax.tree.map(lambda new, old: jnp.where(position < mine, new, old), longer, running)

    return lax.fori_loop(0, count - 1, turn, running)


def contract_rows(left, right):
    return lax.dot_general(
        left, right, (((0,), (0,)), ((), ())), preferred_element_type=jnp.float32
    )


def times_transposed(left, right):
    return lax.dot_general(
        left, right, (((1,), (1,)), ((), ())), preferred_element_type=jnp.float32
    )


def combine(earlier, later):
    return (earlier[0] * later[0], later[0] * earlier[1] + later[1])


def inverse_rms(value):
    return lax.rsqrt(jnp.mean(value * value, axis=-1, keepdims=True) + epsilon)


def sigmoid_slope(raw, sig):
    return sig * (1.0 + raw * (1.0 - sig))


def per_device(
    tokens,
    lengths,
    w_in,
    w_forget,
    w_gate,
    w_out,
    attn_gain,
    mix_gain,
    bound_table,
    ff_gate,
    ff_up,
    ff_down,
    mlp_gain,
    out_grad,
):
    whole = lax.all_gather(tokens, "mp", axis=0, tiled=True)
    mixer = (
        lax.all_gather(w_in, "dp", axis=0, tiled=True),
        lax.all_gather(w_forget, "dp", axis=0, tiled=True),
        lax.all_gather(w_gate, "dp", axis=0, tiled=True),
        lax.all_gather(w_out, "dp", axis=0, tiled=True),
        lax.all_gather(attn_gain, "dp", axis=0, tiled=True),
        lax.all_gather(mix_gain, "dp", axis=0, tiled=True),
        lax.all_gather(bound_table, "dp", axis=1, tiled=True),
    )
    dense = (
        lax.all_gather(ff_gate, "dp", axis=0, tiled=True),
        lax.all_gather(ff_up, "dp", axis=0, tiled=True),
        lax.all_gather(ff_down, "dp", axis=1, tiled=True),
        lax.all_gather(mlp_gain, "dp", axis=0, tiled=True),
    )
    row_count = whole.shape[0]
    half_rows = row_count // lax.axis_size("mp")
    width = whole.shape[1]
    layer_rows = bound_table.shape[0]
    mp_index = lax.axis_index("mp")
    slot = jnp.arange(lengths.shape[0])
    starts = jnp.sum(jnp.where(slot[None, :] < slot[:, None], lengths[None, :], 0), axis=1)
    position = lax.axis_index("dp") * row_count + jnp.arange(row_count, dtype=jnp.int32)
    opening = jnp.any(position[:, None] == starts[None, :], axis=1)
    keep = (1.0 - opening.astype(jnp.float32))[:, None]
    table_f = mixer[6].astype(jnp.float32)
    soft = jax.nn.softmax(table_f, axis=0)
    bound = jnp.sum(soft[1 : LAYER + 1], axis=0)
    attn_g = mixer[4].astype(jnp.float32)
    mix_g = mixer[5].astype(jnp.float32)
    mlp_g = dense[3].astype(jnp.float32)
    tokens_wide = whole.astype(jnp.float32)
    inv_tokens = inverse_rms(tokens_wide)
    tokens_hat = tokens_wide * inv_tokens
    normed = (tokens_hat * attn_g).astype(jnp.bfloat16)
    inner = jnp.dot(normed, mixer[0], preferred_element_type=jnp.float32)
    forget_raw = jnp.dot(normed, mixer[1], preferred_element_type=jnp.float32)
    gate_raw = jnp.dot(normed, mixer[2], preferred_element_type=jnp.float32)
    sig_forget = jax.nn.sigmoid(forget_raw)
    forget = bound + (1.0 - bound) * sig_forget
    sig_inner = jax.nn.sigmoid(inner)
    silu_inner = inner * sig_inner
    drive = silu_inner * (1.0 - forget)
    decay = forget * keep
    decay_all, state_all = lax.associative_scan(combine, (decay, drive), axis=0)
    ones_vec = jnp.ones((width,), jnp.float32)
    zeros_vec = jnp.zeros((width,), jnp.float32)
    carry_in = entering(
        (decay_all[-1], state_all[-1]), "dp", combine, (ones_vec, zeros_vec), False
    )[1]
    states = decay_all * carry_in[None, :] + state_all
    inv_states = inverse_rms(states)
    states_hat = states * inv_states
    sig_gate = jax.nn.sigmoid(gate_raw)
    silu_gate = gate_raw * sig_gate
    mixed_in = (states_hat * mix_g * silu_gate).astype(jnp.bfloat16)
    resid = tokens_wide + jnp.dot(mixed_in, mixer[3], preferred_element_type=jnp.float32)
    inv_resid = inverse_rms(resid)
    resid_hat = resid * inv_resid
    hidden_in = (resid_hat * mlp_g).astype(jnp.bfloat16)
    gate_ff = jnp.dot(hidden_in, dense[0], preferred_element_type=jnp.float32)
    up_ff = jnp.dot(hidden_in, dense[1], preferred_element_type=jnp.float32)
    sig_ff = jax.nn.sigmoid(gate_ff)
    silu_ff = gate_ff * sig_ff
    act = (silu_ff * up_ff).astype(jnp.bfloat16)
    partial_out = jnp.dot(act, dense[2], preferred_element_type=jnp.float32)
    glu_out = lax.psum_scatter(
        partial_out.astype(jnp.bfloat16), "mp", scatter_dimension=0, tiled=True
    ).astype(jnp.float32)
    own_resid = lax.dynamic_slice_in_dim(resid, mp_index * half_rows, half_rows, 0)
    result = (own_resid + glu_out).astype(jnp.bfloat16)
    grad_whole = lax.all_gather(out_grad, "mp", axis=0, tiled=True)
    grad_wide = grad_whole.astype(jnp.float32)
    d_act = times_transposed(grad_whole, dense[2])
    grad_down = contract_rows(act, grad_whole)
    d_gate_ff = (d_act * up_ff * sigmoid_slope(gate_ff, sig_ff)).astype(jnp.bfloat16)
    d_up_ff = (d_act * silu_ff).astype(jnp.bfloat16)
    grad_gate_ff = contract_rows(hidden_in, d_gate_ff)
    grad_up_ff = contract_rows(hidden_in, d_up_ff)
    d_hidden_part = times_transposed(d_gate_ff, dense[0]) + times_transposed(d_up_ff, dense[1])
    d_hidden = lax.psum(d_hidden_part, "mp")
    grad_mlp = jnp.sum(d_hidden * resid_hat, axis=0)
    glu_grads = (
        lax.psum_scatter(grad_gate_ff, "dp", scatter_dimension=0, tiled=True),
        lax.psum_scatter(grad_up_ff, "dp", scatter_dimension=0, tiled=True),
        lax.psum_scatter(grad_down, "dp", scatter_dimension=1, tiled=True),
        lax.psum_scatter(grad_mlp, "dp", scatter_dimension=0, tiled=True),
    )
    scaled_hidden = d_hidden * mlp_g
    d_resid = grad_wide + inv_resid * (
        scaled_hidden - resid_hat * jnp.mean(scaled_hidden * resid_hat, axis=-1, keepdims=True)
    )
    d_mixed = d_resid.astype(jnp.bfloat16)
    grad_out = contract_rows(mixed_in, d_mixed)
    d_mixin = times_transposed(d_mixed, mixer[3])
    grad_mix = jnp.sum(d_mixin * states_hat * silu_gate, axis=0)
    d_gate_raw = (d_mixin * states_hat * mix_g * sigmoid_slope(gate_raw, sig_gate)).astype(
        jnp.bfloat16
    )
    scaled_states = d_mixin * mix_g * silu_gate
    d_states = inv_states * (
        scaled_states - states_hat * jnp.mean(scaled_states * states_hat, axis=-1, keepdims=True)
    )
    decay_next = jnp.concatenate([decay[1:], jnp.ones((1, width), jnp.float32)], axis=0)
    tail_all, adjoint_local = lax.associative_scan(
        combine, (decay_next, d_states), reverse=True, axis=0
    )
    first_decay = decay[0]
    incoming = entering(
        (first_decay * tail_all[0], first_decay * adjoint_local[0]),
        "dp",
        combine,
        (ones_vec, zeros_vec),
        True,
    )[1]
    adjoint = adjoint_local + tail_all * incoming[None, :]
    prev_states = jnp.concatenate([carry_in[None, :], states[:-1]], axis=0)
    d_forget = adjoint * prev_states * keep - adjoint * silu_inner
    d_inner = (adjoint * (1.0 - forget) * sigmoid_slope(inner, sig_inner)).astype(jnp.bfloat16)
    d_forget_raw = (d_forget * (1.0 - bound) * sig_forget * (1.0 - sig_forget)).astype(jnp.bfloat16)
    d_bound = jnp.sum(d_forget * (1.0 - sig_forget), axis=0)
    row_ids = jnp.arange(layer_rows)[:, None]
    member = jnp.logical_and(row_ids >= 1, row_ids <= LAYER).astype(jnp.float32)
    grad_table = soft * (member - bound[None, :]) * d_bound[None, :]
    grad_in = contract_rows(normed, d_inner)
    grad_forget = contract_rows(normed, d_forget_raw)
    grad_gate = contract_rows(normed, d_gate_raw)
    d_normed = (
        times_transposed(d_inner, mixer[0])
        + times_transposed(d_forget_raw, mixer[1])
        + times_transposed(d_gate_raw, mixer[2])
    )
    grad_attn = jnp.sum(d_normed * tokens_hat, axis=0)
    scaled_normed = d_normed * attn_g
    d_tokens = d_resid + inv_tokens * (
        scaled_normed - tokens_hat * jnp.mean(scaled_normed * tokens_hat, axis=-1, keepdims=True)
    )
    token_grad = lax.dynamic_slice_in_dim(d_tokens, mp_index * half_rows, half_rows, 0)
    mixer_grads = (
        lax.psum_scatter(grad_in, "dp", scatter_dimension=0, tiled=True),
        lax.psum_scatter(grad_forget, "dp", scatter_dimension=0, tiled=True),
        lax.psum_scatter(grad_gate, "dp", scatter_dimension=0, tiled=True),
        lax.psum_scatter(grad_out, "dp", scatter_dimension=0, tiled=True),
        lax.psum_scatter(grad_attn, "dp", scatter_dimension=0, tiled=True),
        lax.psum_scatter(grad_mix, "dp", scatter_dimension=0, tiled=True),
        lax.psum_scatter(grad_table, "dp", scatter_dimension=1, tiled=True),
    )
    return (
        result,
        token_grad,
        mixer_grads[0],
        mixer_grads[1],
        mixer_grads[2],
        mixer_grads[3],
        mixer_grads[4],
        mixer_grads[5],
        mixer_grads[6],
        glu_grads[0],
        glu_grads[1],
        glu_grads[2],
        glu_grads[3],
    )


def solution(mesh):
    return jax.shard_map(
        per_device,
        mesh=mesh,
        in_specs=(
            P(("dp", "mp"), None),
            P(),
            P("dp", None),
            P("dp", None),
            P("dp", None),
            P("dp", None),
            P("dp"),
            P("dp"),
            P(None, "dp"),
            P("dp", "mp"),
            P("dp", "mp"),
            P("mp", "dp"),
            P("dp"),
            P(("dp", "mp"), None),
        ),
        out_specs=(
            P(("dp", "mp"), None),
            P(("dp", "mp"), None),
            P("dp", None),
            P("dp", None),
            P("dp", None),
            P("dp", None),
            P("dp"),
            P("dp"),
            P(None, "dp"),
            P("dp", "mp"),
            P("dp", "mp"),
            P("mp", "dp"),
            P("dp"),
        ),
        check_vma=False,
    )
```

```python
import jax
import jax.numpy as jnp
from jax import lax
from jax.experimental import pallas as pl
from jax.experimental.pallas import tpu as pltpu
from jax.sharding import Mesh, PartitionSpec as P

LAYER = 12
Z, C, X = 4, 2, 2
epsilon = 1e-06
BF, F32 = jnp.bfloat16, jnp.float32


def swap(value, axis):
    return lax.ppermute(value, axis, [(0, 1), (1, 0)])


def across_z(value, step):
    return lax.ppermute(value, "z", [(i, i ^ step) for i in range(Z)])


def dot(left, right):
    return jnp.dot(left, right, preferred_element_type=F32)


def contract_rows(left, right):
    return lax.dot_general(left, right, (((0,), (0,)), ((), ())), preferred_element_type=F32)


def times_transposed(left, right):
    return lax.dot_general(left, right, (((1,), (1,)), ((), ())), preferred_element_type=F32)


def inverse_rms(value):
    return lax.rsqrt(jnp.mean(value * value, axis=-1, keepdims=True) + epsilon)


def sigmoid_slope(raw, sig):
    return sig * (1.0 + raw * (1.0 - sig))


def gather_rows(own):
    mine = jnp.concatenate([own] + [across_z(own, k) for k in range(1, Z)], axis=0)
    return jnp.concatenate([mine, swap(mine, "c")], axis=0)


def scatter_rows(partial):
    half = partial.shape[0] // C
    rows = half // Z
    both = partial[:half].astype(F32) + swap(partial[half:], "c").astype(F32)
    total = both[:rows]
    for k in range(1, Z):
        total = total + across_z(both[k * rows : (k + 1) * rows].astype(BF), k).astype(F32)
    return total


def forward_kernel(decay_ref, drive_ref, state_ref, through_ref):
    chunks = 8
    length = decay_ref.shape[0] // chunks

    def step(t, carry):
        state, through = carry
        at = pl.ds(t, chunks, stride=length)
        decay = decay_ref[at, :]
        state = decay * state + drive_ref[at, :]
        through = decay * through
        state_ref[at, :] = state
        through_ref[at, :] = through
        return state, through

    shape = (chunks, decay_ref.shape[1])
    lax.fori_loop(0, length, step, (jnp.zeros(shape, F32), jnp.ones(shape, F32)), unroll=8)


def backward_kernel(decay_ref, grad_ref, adjoint_ref, after_ref, first_ref):
    chunks = 8
    length = decay_ref.shape[0] // chunks

    def step(t, carry):
        coming, after = carry
        at = pl.ds(length - 1 - t, chunks, stride=length)
        decay = decay_ref[at, :]
        adjoint = grad_ref[at, :] + coming
        adjoint_ref[at, :] = adjoint
        after_ref[at, :] = after
        return decay * adjoint, decay * after

    shape = (chunks, decay_ref.shape[1])
    coming, _ = lax.fori_loop(
        0, length, step, (jnp.zeros(shape, F32), jnp.ones(shape, F32)), unroll=8
    )
    first_ref[...] = coming


LANES = 128


def scan_call(kernel, inputs, outputs):
    feats = inputs[0].shape[1]

    def spec(rows):
        return pl.BlockSpec((rows, LANES), lambda i: (0, i))

    return pl.pallas_call(
        kernel,
        grid=(feats // LANES,),
        in_specs=[spec(v.shape[0]) for v in inputs],
        out_specs=[spec(n) for n in outputs],
        out_shape=[jax.ShapeDtypeStruct((n, feats), F32) for n in outputs],
    )(*inputs)


def entry_kernel(order_ref, through_ref, last_ref, entry_ref):
    def step(n, running):
        row = pl.ds(order_ref[n], 1)
        entry_ref[row, :] = running
        return through_ref[row, :] * running + last_ref[row, :]

    lax.fori_loop(0, order_ref.shape[0], step, jnp.zeros((1, last_ref.shape[1]), F32))


def per_device(
    tokens, lengths, w_in, w_forget, w_gate, w_out, attn_gain, mix_gain, bound_table,
    ff_gate, ff_up, ff_down, mlp_gain, out_grad,
):
    Y = lax.axis_size("y")
    pair = Y == 2
    z, y, c, x = (lax.axis_index(a) for a in "zycx")
    rows, width = tokens.shape
    sub = w_in.shape[0]
    feats = Y * sub
    block = ff_gate.shape[1] // (Z * C)
    chunks = Z * C
    group = rows * chunks

    def y_first(value):
        parts = value.reshape(value.shape[0], Z, Y, C * sub)
        parts = [parts[:, :, k].reshape(value.shape[0], Z * C * sub) for k in range(Y)]
        if pair:
            first, second = parts
            return jnp.concatenate(
                [jnp.where(y == 0, first, second), jnp.where(y == 0, second, first)], axis=1
            )
        return jnp.concatenate(parts, axis=1)

    def z_first(value):
        parts = jnp.split(value, Y, axis=1)
        if pair:
            first, second = parts
            parts = [jnp.where(y == 0, first, second), jnp.where(y == 0, second, first)]
        parts = [p.reshape(-1, Z, C * sub) for p in parts]
        return jnp.stack(parts, axis=2).reshape(value.shape[0], width)

    def over_y(value):
        if pair:
            return [value, swap(value, "y")]
        return [lax.all_gather(value, "y", axis=0, tiled=True)]

    def y_sum(pieces):
        if pair:
            return pieces[0].astype(BF).astype(F32) + swap(pieces[1].astype(BF), "y").astype(F32)
        return lax.psum_scatter(pieces[0].astype(BF), "y", scatter_dimension=0, tiled=True).astype(F32)

    def in_order(value):
        if pair:
            other = swap(value, "y")
            return jnp.concatenate(
                [jnp.where(y == 0, value, other), jnp.where(y == 0, other, value)], axis=0
            )
        return lax.all_gather(value, "y", axis=0, tiled=True)

    def own_sum(value):
        if pair:
            first, second = jnp.split(value, 2, axis=0)
            mine = jnp.where(y == 0, first, second).astype(BF)
            sent = jnp.where(y == 0, second, first).astype(BF)
            return mine.astype(F32) + swap(sent, "y").astype(F32)
        return lax.psum_scatter(value.astype(BF), "y", scatter_dimension=0, tiled=True).astype(F32)

    def x_sum(value):
        value = value.astype(BF)
        return value.astype(F32) + swap(value, "x").astype(F32)

    def spread(value):
        return lax.all_to_all(value, ("z", "c"), 0, 0, tiled=True)

    tokens_rho = y_first(tokens)
    tokens_all = gather_rows(tokens_rho)
    grad_all = gather_rows(y_first(out_grad))

    def to_blocks(weight):
        return weight.reshape(sub, Z, Y, C, sub).transpose(1, 3, 0, 2, 4).reshape(chunks, sub, feats)

    mixer = jnp.concatenate([to_blocks(w) for w in (w_in, w_forget, w_gate)], axis=2)
    mixer = over_y(spread(mixer).reshape(chunks * sub, 3 * feats))
    out_rows = in_order(w_out)
    table_f = bound_table.astype(F32)
    soft = jax.nn.softmax(table_f, axis=0)
    own_bound = jnp.sum(soft[1 : LAYER + 1], axis=0)
    small = in_order(jnp.stack([own_bound, mix_gain.astype(F32)])[None])
    bound = small[:, 0].reshape(1, feats)
    mix_g = small[:, 1].reshape(1, feats)
    gains = lax.all_gather(
        jnp.stack([attn_gain, mlp_gain]), ("z", "y", "c"), axis=1, tiled=True
    ).astype(F32)
    attn_g, mlp_g = gains[:1], gains[1:]

    def columns(weight):
        return spread(weight.reshape(sub, chunks, block).transpose(1, 0, 2)).reshape(chunks * sub, block)

    def halves(own, x_last):
        if not pair:
            full = over_y(own)
            return [full, [swap(full[0], "x")]]
        if x_last:
            near = over_y(own)
            return [near, [swap(p, "x") for p in near]]
        side = swap(own, "x")
        return [over_y(own), over_y(side)]

    gate_w = halves(columns(ff_gate), True)
    up_w = halves(columns(ff_up), False)
    down_w = spread(ff_down.reshape(chunks, block, sub)).transpose(0, 2, 1).reshape(chunks * sub, block)
    down_w = halves(down_w, True)

    def k_parts(value):
        return jnp.split(value, 2, axis=1) if pair else [value]

    def into(value, weights):
        return sum(dot(v, w) for v, w in zip(k_parts(value), weights, strict=True))

    starts_slot = jnp.arange(lengths.shape[0])
    starts = jnp.sum(jnp.where(starts_slot[None, :] < starts_slot[:, None], lengths[None, :], 0), axis=1)
    slot = jnp.arange(chunks)
    chunk = ((z ^ (slot % Z)) * Y + y) * (C * X) + (c ^ (slot // Z)) * X + x
    position = (chunk[:, None] * rows + jnp.arange(rows)[None, :]).reshape(group)
    keep = 1.0 - jnp.any(position[:, None] == starts[None, :], axis=1).astype(F32)[:, None]
    count = Z * Y * C * X
    number = jnp.arange(count)
    xn, cn = number % X, number // X % C
    yn, zn = number // (X * C) % Y, number // (X * C * Y)
    party = (yn ^ y) * X + (xn ^ x) if pair else yn * X + xn
    order = (party * chunks + (cn ^ c) * Z + (zn ^ z)).astype(jnp.int32)

    def parties(value):
        if pair:
            side = swap(value, "x")
            return jnp.concatenate([value, side, swap(value, "y"), lax.ppermute(
                value, ("y", "x"), [(i, 3 - i) for i in range(4)])], axis=0)
        return lax.all_gather(value, ("y", "x"), axis=0, tiled=True)

    def entries(order, through, last):
        total = pl.pallas_call(
            entry_kernel,
            out_shape=jax.ShapeDtypeStruct(last.shape, F32),
            in_specs=[pl.BlockSpec(memory_space=pltpu.SMEM)] + [pl.BlockSpec(memory_space=pltpu.VMEM)] * 2,
            out_specs=pl.BlockSpec(memory_space=pltpu.VMEM),
        )(order, through, last)
        if pair:
            return total[:chunks]
        return lax.dynamic_slice_in_dim(total, (y * X + x) * chunks, chunks, 0)

    wide = tokens_all.astype(F32)
    normed = (wide * inverse_rms(wide) * y_first(attn_g)).astype(BF)
    projected = into(normed, mixer)
    inner, forget_raw, gate_raw = jnp.split(projected, 3, axis=1)
    sig_forget = jax.nn.sigmoid(forget_raw)
    forget = bound + (1.0 - bound) * sig_forget
    sig_inner = jax.nn.sigmoid(inner)
    silu_inner = inner * sig_inner
    drive = silu_inner * (1.0 - forget)
    decay = forget * keep
    local, through = scan_call(forward_kernel, [decay, drive], [group, group])

    def per_chunk(value):
        return value.reshape(chunks, rows, feats)

    def flat(value):
        return value.reshape(group, feats)

    all_edges = parties(jnp.stack([per_chunk(through)[:, -1], per_chunk(local)[:, -1]], axis=1))
    all_through = all_edges[:, 0]
    entry = entries(order, all_through, all_edges[:, 1])
    states3 = per_chunk(local) + per_chunk(through) * entry[:, None, :]
    states = flat(states3)
    previous = flat(jnp.concatenate([entry[:, None, :], states3[:, :-1]], axis=1))
    sig_gate = jax.nn.sigmoid(gate_raw)
    silu_gate = gate_raw * sig_gate
    raw_mix = states * (mix_g * silu_gate)
    squares = jnp.sum(states * states, axis=1, keepdims=True)

    def lanes(*columns):
        split = []
        for column in columns:
            high = lax.reduce_precision(column, 8, 7)
            split += [high, column - high]
        split.append(jnp.zeros((columns[0].shape[0], 128 - len(split)), F32))
        return jnp.concatenate(split, axis=1).astype(BF)

    def unlane(value, at):
        return value[:, 2 * at : 2 * at + 1].astype(F32) + value[:, 2 * at + 1 : 2 * at + 2].astype(F32)

    summed = scatter_rows(
        jnp.concatenate([dot(raw_mix.astype(BF), out_rows).astype(BF), lanes(squares)], axis=1)
    )
    own_q = lax.rsqrt(unlane(summed[:, width:], 0) * (1.0 / width) + epsilon)
    mixed = own_q * summed[:, :width]
    resid = tokens.astype(F32) + mixed
    inv_resid = inverse_rms(resid)
    resid_hat = resid * inv_resid
    hidden = gather_rows(y_first((resid_hat * mlp_g).astype(BF)))

    gate_ff = [into(hidden, w) for w in gate_w]
    up_ff = [into(hidden, w) for w in up_w]
    sig_ff = [jax.nn.sigmoid(g) for g in gate_ff]
    silu_ff = [g * s for g, s in zip(gate_ff, sig_ff)]
    act = [(s * u).astype(BF) for s, u in zip(silu_ff, up_ff)]

    def back(values, weights):
        parts = []
        for k in range(len(weights[0])):
            parts.append(sum(times_transposed(v, w[k]) for v, w in zip(values, weights)))
        return jnp.concatenate([p.astype(BF) for p in parts], axis=1)

    d_act = [into(grad_all, w) for w in down_w]
    d_gate_ff = [
        (d * u * sigmoid_slope(g, s)).astype(BF) for d, u, g, s in zip(d_act, up_ff, gate_ff, sig_ff)
    ]
    d_up_ff = [(d * s).astype(BF) for d, s in zip(d_act, silu_ff)]
    d_hidden = z_first(scatter_rows(back(d_gate_ff + d_up_ff, gate_w + up_w)))
    glu_out = z_first(scatter_rows(back(act, down_w)))
    result = (resid + glu_out).astype(BF)

    def glu_total(source, grads, x_first):
        pieces = [[contract_rows(s, g) for s in k_parts(source)] for g in grads]
        if x_first or not pair:
            near = [
                own.astype(BF).astype(F32) + swap(other.astype(BF), "x").astype(F32)
                for own, other in zip(*pieces)
            ]
            return y_sum(near)
        near = [y_sum(p) for p in pieces]
        return near[0].astype(BF).astype(F32) + swap(near[1].astype(BF), "x").astype(F32)

    def columns_back(value):
        value = spread(value.astype(BF).reshape(chunks, sub, block))
        return value.transpose(1, 0, 2).reshape(sub, chunks * block).astype(F32)

    grad_gate_ff = columns_back(glu_total(hidden, d_gate_ff, True))
    grad_up_ff = columns_back(glu_total(hidden, d_up_ff, False))
    grad_down = glu_total(grad_all, act, True)
    grad_down = spread(grad_down.astype(BF).reshape(chunks, sub, block).transpose(0, 2, 1))
    grad_down = grad_down.reshape(chunks * block, sub).astype(F32)

    scaled_hidden = d_hidden * mlp_g
    d_resid = out_grad.astype(F32) + inv_resid * (
        scaled_hidden - resid_hat * jnp.mean(scaled_hidden * resid_hat, axis=-1, keepdims=True)
    )
    own_d_mixed = d_resid.astype(BF)
    own_mean = jnp.mean(own_d_mixed.astype(F32) * mixed, axis=-1, keepdims=True)
    sent = gather_rows(jnp.concatenate([own_d_mixed, lanes(own_q, own_mean)], axis=1))
    d_mixed = sent[:, :width]
    inv_states, mean_states = unlane(sent[:, width:], 0), unlane(sent[:, width:], 1)
    states_hat = states * inv_states
    mixed_in = (states_hat * mix_g * silu_gate).astype(BF)
    grad_out = x_sum(own_sum(contract_rows(mixed_in, d_mixed)))
    d_mixin = times_transposed(d_mixed, out_rows)
    d_gate_raw = (d_mixin * states_hat * mix_g * sigmoid_slope(gate_raw, sig_gate)).astype(BF)
    d_states = inv_states * (d_mixin * mix_g * silu_gate - states_hat * mean_states)
    adjoint_local, after, first = scan_call(
        backward_kernel, [decay, d_states], [group, group, chunks]
    )
    coming = entries(order[::-1], all_through, parties(first))
    adjoint = flat(per_chunk(adjoint_local) + per_chunk(after) * coming[:, None, :])
    d_forget = adjoint * previous * keep - adjoint * silu_inner
    d_inner = (adjoint * (1.0 - forget) * sigmoid_slope(inner, sig_inner)).astype(BF)
    d_forget_raw = (d_forget * (1.0 - bound) * sig_forget * (1.0 - sig_forget)).astype(BF)
    d_raw = jnp.concatenate([d_inner, d_forget_raw, d_gate_raw], axis=1)
    d_normed = z_first(
        scatter_rows(
            jnp.concatenate([times_transposed(d_raw, w).astype(BF) for w in mixer], axis=1)
        )
    )

    part_bound = jnp.sum(d_forget * (1.0 - sig_forget), axis=0)
    if pair:
        first_half, second_half = jnp.split(part_bound, 2)
        d_bound = jnp.where(y == 0, first_half, second_half) + swap(
            jnp.where(y == 0, second_half, first_half), "y"
        )
    else:
        d_bound = lax.psum_scatter(part_bound, "y", scatter_dimension=0, tiled=True)
    d_bound = d_bound + swap(d_bound, "x")
    row_ids = jnp.arange(bound_table.shape[0])[:, None]
    member = jnp.logical_and(row_ids >= 1, row_ids <= LAYER).astype(F32)
    grad_table = soft * (member - own_bound[None, :]) * d_bound[None, :]

    grad_mixer = y_sum([contract_rows(s, d_raw) for s in k_parts(normed)])
    grad_mixer = spread(x_sum(grad_mixer).astype(BF).reshape(chunks, sub, 3 * feats))
    grad_mixer = grad_mixer.reshape(Z, C, sub, 3, Y, sub).transpose(3, 2, 0, 4, 1, 5)
    grad_mixer = grad_mixer.reshape(3, sub, width).astype(F32)
    grad_in, grad_forget, grad_gate = grad_mixer[0], grad_mixer[1], grad_mixer[2]

    def along(weight, grad):
        return jnp.sum(weight.astype(F32) * grad, axis=1)

    grad_attn = along(w_in, grad_in) + along(w_forget, grad_forget) + along(w_gate, grad_gate)
    grad_attn = grad_attn / attn_gain.astype(F32)
    grad_mix = along(w_out, grad_out) / mix_gain.astype(F32)
    grad_mlp = along(ff_gate, grad_gate_ff) + along(ff_up, grad_up_ff)
    grad_mlp = (grad_mlp + swap(grad_mlp, "x")) / mlp_gain.astype(F32)

    own_wide = tokens.astype(F32)
    inv_tokens = inverse_rms(own_wide)
    tokens_hat = own_wide * inv_tokens
    scaled_normed = d_normed * attn_g
    token_grad = d_resid + inv_tokens * (
        scaled_normed - tokens_hat * jnp.mean(scaled_normed * tokens_hat, axis=-1, keepdims=True)
    )
    return (
        result, token_grad, grad_in, grad_forget, grad_gate, grad_out, grad_attn, grad_mix,
        grad_table, grad_gate_ff, grad_up_ff, grad_down, grad_mlp,
    )


def solution(mesh):
    dp, mp = mesh.devices.shape
    grid = Mesh(mesh.devices.reshape(Z, dp // (Z * C), C, mp), ("z", "y", "c", "x"))
    dp_axes = ("z", "y", "c")
    every = ("z", "y", "c", "x")
    mat, row, gain = P(dp_axes, None), P(every, None), P(dp_axes)
    table, glu, glu_down = P(None, dp_axes), P(dp_axes, "x"), P("x", dp_axes)
    return jax.shard_map(
        per_device,
        mesh=grid,
        in_specs=(
            row, P(), mat, mat, mat, mat, gain, gain, table, glu, glu, glu_down, gain, row,
        ),
        out_specs=(
            row, row, mat, mat, mat, mat, gain, gain, table, glu, glu, glu_down, gain,
        ),
        check_vma=False,
    )
```

```python
import functools

import jax
import jax.numpy as jnp
from jax import lax
from jax.experimental import pallas as pl
from jax.experimental.pallas import tpu as pltpu
from jax.sharding import Mesh, PartitionSpec as P

LAYER = 12
Z, C, X = 4, 2, 2
CHUNKS = Z * C
LANES = 128
epsilon = 1e-06
BF, F32 = jnp.bfloat16, jnp.float32


def swap(value, axis):
    return lax.ppermute(value, axis, [(0, 1), (1, 0)])


def across_z(value, step):
    return lax.ppermute(value, "z", [(i, i ^ step) for i in range(Z)])


def dot(left, right):
    return jnp.dot(left, right, preferred_element_type=F32)


def contract_rows(left, right):
    return lax.dot_general(left, right, (((0,), (0,)), ((), ())), preferred_element_type=F32)


def times_transposed(left, right):
    return lax.dot_general(left, right, (((1,), (1,)), ((), ())), preferred_element_type=F32)


def mean_last(value):
    return jnp.mean(value, axis=-1, keepdims=True)


def inverse_rms(value):
    return lax.rsqrt(mean_last(value * value) + epsilon)


def sigmoid_slope(raw, sig):
    return sig * (1.0 + raw * (1.0 - sig))


def call(kernel, outs, *ins, smem=0, scratch=(), flops=0):
    specs = [pl.BlockSpec(memory_space=pltpu.SMEM)] * smem
    specs += [pl.BlockSpec(memory_space=pltpu.VMEM)] * (len(ins) - smem)
    shapes = [jax.ShapeDtypeStruct(s, t) for s, t in outs]
    moved = sum(v.size * v.dtype.itemsize for v in list(ins) + shapes)
    return pl.pallas_call(
        kernel,
        out_shape=shapes,
        in_specs=specs,
        out_specs=[pl.BlockSpec(memory_space=pltpu.VMEM)] * len(outs),
        scratch_shapes=list(scratch),
        compiler_params=pltpu.CompilerParams(vmem_limit_bytes=40 << 20),
        cost_estimate=pl.CostEstimate(flops=flops, bytes_accessed=moved, transcendentals=0),
    )(*ins)


def stat_block(columns):
    rows = columns[0].shape[0]
    lane = lax.broadcasted_iota(jnp.int32, (rows, LANES), 1)
    block = jnp.zeros((rows, LANES), F32)
    for k, column in enumerate(columns):
        high = column.astype(BF).astype(F32)
        block = jnp.where(lane == 2 * k, high, block)
        block = jnp.where(lane == 2 * k + 1, column - high, block)
    return block


def stat(block, k):
    lane = lax.broadcasted_iota(jnp.int32, block.shape, 1)
    picked = jnp.where((lane == 2 * k) | (lane == 2 * k + 1), block.astype(F32), 0.0)
    return jnp.sum(picked, axis=1, keepdims=True)


def reorder_kernel(back, y_ref, *refs):
    y = y_ref[0]
    half = len(refs) // 2
    for in_ref, out_ref in zip(refs[:half], refs[half:]):
        width = in_ref.shape[1] // CHUNKS
        for k in range(2):
            there = k + y - 2 * k * y
            for z in range(Z):
                near = slice((k * Z + z) * width, (k * Z + z + 1) * width)
                far = pl.ds(pl.multiple_of((z * 2 + there) * width, width), width)
                if back:
                    out_ref[:, far] = in_ref[:, near]
                else:
                    out_ref[:, near] = in_ref[:, far]


def mixer_blocks_kernel(*refs):
    out_ref = refs[-1]
    for m, w_ref in enumerate(refs[:-1]):
        for z in range(Z):
            for y in range(2):
                for c in range(C):
                    at, to = ((z * 2 + y) * C + c) * LANES, (m * 2 + y) * LANES
                    out_ref[z * C + c, :, to : to + LANES] = w_ref[:, at : at + LANES]


def mixer_grads_kernel(blocks_ref, w_in, w_forget, w_gate, grad_in, grad_forget, grad_gate, along_ref):
    total = jnp.zeros((w_in.shape[0], 1), F32)
    for m, (w_ref, g_ref) in enumerate(((w_in, grad_in), (w_forget, grad_forget), (w_gate, grad_gate))):
        for z in range(Z):
            for y in range(2):
                for c in range(C):
                    to, at = ((z * 2 + y) * C + c) * LANES, (m * 2 + y) * LANES
                    piece = blocks_ref[z * C + c, :, at : at + LANES].astype(F32)
                    g_ref[:, to : to + LANES] = piece
                    weight = w_ref[:, to : to + LANES].astype(F32)
                    total = total + jnp.sum(piece * weight, axis=1, keepdims=True)
    along_ref[...] = jnp.broadcast_to(total, along_ref.shape)


def glu_blocks_kernel(gate_ref, up_ref, down_ref, out_ref):
    block = down_ref.shape[0] // CHUNKS
    for s in range(CHUNKS):
        at = slice(s * block, (s + 1) * block)
        out_ref[s, :block] = gate_ref[:, at].astype(F32).T.astype(BF)
        out_ref[s, block : 2 * block] = up_ref[:, at].astype(F32).T.astype(BF)
        out_ref[s, 2 * block :] = down_ref[at, :]


def glu_grads_kernel(blocks_ref, w_gate, w_up, grad_gate, grad_up, grad_down, along_ref):
    block = grad_down.shape[0] // CHUNKS
    total = jnp.zeros((w_gate.shape[0], 1), F32)
    for s in range(CHUNKS):
        at = slice(s * block, (s + 1) * block)
        for m, (w_ref, g_ref) in enumerate(((w_gate, grad_gate), (w_up, grad_up))):
            piece = blocks_ref[s, m * block : (m + 1) * block].astype(F32).T
            g_ref[:, at] = piece
            total = total + jnp.sum(piece * w_ref[:, at].astype(F32), axis=1, keepdims=True)
        grad_down[at, :] = blocks_ref[s, 2 * block :].astype(F32)
    along_ref[...] = jnp.broadcast_to(total, along_ref.shape)


def mixer_forward_kernel(parts, *refs):
    gain, near, far, bound, keep = refs[:5]
    weights = refs[5 : 5 + parts]
    normed, raw, decay, local, through, edge, drive = refs[5 + parts :]
    group, feats = raw.shape[0], bound.shape[1]
    rows = group // CHUNKS
    for k, source in enumerate((near, far)):

        @pl.loop(0, source.shape[0] // 32)
        def _(i, source=source, base=k * source.shape[0]):
            value = source[pl.ds(i * 32, 32), :].astype(F32)
            normed[pl.ds(base + i * 32, 32), :] = (value * inverse_rms(value) * gain[...]).astype(BF)

    @pl.loop(0, 4)
    def _(i):
        at = pl.ds(i * (group // 4), group // 4)
        total, begin = None, 0
        for w in weights:
            part = dot(normed[at, begin : begin + w.shape[0]], w[...])
            total = part if total is None else total + part
            begin += w.shape[0]
        raw[at, :] = total

    count = feats // LANES

    @pl.loop(0, CHUNKS)
    def _(i):
        at = pl.ds(i * rows, rows)
        for j in range(count):
            lanes = slice(j * LANES, (j + 1) * LANES)
            inner = raw[at, lanes]
            forget_raw = raw[at, feats + j * LANES : feats + (j + 1) * LANES]
            low = bound[:, lanes]
            forget = low + (1.0 - low) * jax.nn.sigmoid(forget_raw)
            drive[j, at, :] = inner * jax.nn.sigmoid(inner) * (1.0 - forget)
            decay[j, at, :] = forget * keep[at, :]

    def step(t, carry):
        out = []
        at = pl.ds(t, CHUNKS, stride=rows)
        for j in range(count):
            state, passed = carry[2 * j], carry[2 * j + 1]
            here = decay[j, at, :]
            state = here * state + drive[j, at, :]
            passed = here * passed
            local[j, at, :] = state
            through[j, at, :] = passed
            out += [state, passed]
        return tuple(out)

    zero, one = jnp.zeros((CHUNKS, LANES), F32), jnp.ones((CHUNKS, LANES), F32)
    last = lax.fori_loop(0, rows, step, (zero, one) * count, unroll=8)
    for j in range(count):
        edge[:CHUNKS, j * LANES : (j + 1) * LANES] = last[2 * j + 1]
        edge[CHUNKS:, j * LANES : (j + 1) * LANES] = last[2 * j]


def entries(order, backwards, count, passed, last, entry):
    def step(n, running):
        row = pl.ds(order[count - 1 - n if backwards else n], 1)
        entry[row, :] = running
        return passed[row, :] * running + last[row, :]

    lax.fori_loop(0, count, step, jnp.zeros((1, last.shape[1]), F32))


def collect(parties, at, to):
    base = 0
    for p in parties:
        for g in range(p.shape[0] // (at[1] * CHUNKS)):
            begin = (g * at[1] + at[0]) * CHUNKS
            to[base : base + CHUNKS, :] = p[begin : begin + CHUNKS, :]
            base += CHUNKS


def mixer_out_kernel(parties, count, order, *refs):
    edges = refs[:parties]
    local, through, raw, mix_gain, out_w = refs[parties : parties + 5]
    states, entry_own, keep, send, passed, last, entry, mixed, squares = refs[parties + 5 :]
    group, feats = raw.shape[0], mix_gain.shape[1]
    width = out_w.shape[1]
    rows = group // CHUNKS
    collect(edges, (0, 2), passed)
    collect(edges, (1, 2), last)
    entries(order, False, count, passed, last, entry)
    base = order[count]
    entry_own[...] = entry[pl.ds(pl.multiple_of(base, CHUNKS), CHUNKS), :]
    for s in range(CHUNKS):
        at = slice(s * rows, (s + 1) * rows)
        total = jnp.zeros((rows, LANES), F32)
        for j in range(feats // LANES):
            lanes = slice(j * LANES, (j + 1) * LANES)
            state = local[j, at, :] + through[j, at, :] * entry_own[s : s + 1, lanes]
            gate = raw[at, 2 * feats + j * LANES : 2 * feats + (j + 1) * LANES]
            mixed[at, lanes] = (state * (mix_gain[:, lanes] * (gate * jax.nn.sigmoid(gate)))).astype(BF)
            states[j, at, :] = state
            total = total + state * state
        squares[at, :] = stat_block([jnp.sum(total, axis=1, keepdims=True)])
    half = group // 2
    keep[:, width:] = squares[:half, :]
    send[:, width:] = squares[half:, :].astype(BF)

    for k in range(2):
        part = slice(k * half // 2, (k + 1) * half // 2)
        keep[part, :width] = dot(mixed[part, :], out_w[...])
        part2 = slice(half + k * half // 2, half + (k + 1) * half // 2)
        send[part, :width] = dot(mixed[part2, :], out_w[...]).astype(BF)


def shares_kernel(keep, got, own, *others):
    rows = own.shape[0]
    own[...] = keep[:rows, :] + got[:rows, :].astype(F32)
    for k, other in enumerate(others):
        at = slice((k + 1) * rows, (k + 2) * rows)
        other[...] = (keep[at, :] + got[at, :].astype(F32)).astype(BF)


def total_of(refs, at, lanes):
    total = refs[0][at, lanes]
    for r in refs[1:]:
        total = total + r[at, lanes].astype(F32)
    return total


STEP = 16


def resid_kernel(own, a, b, c, tokens, gain, resid, hidden, scale):
    width = tokens.shape[1]

    @pl.loop(0, tokens.shape[0] // STEP)
    def _(i):
        at = pl.ds(i * STEP, STEP)
        q = lax.rsqrt(stat(total_of((own, a, b, c), at, slice(width, None)), 0) / width + epsilon)
        value = tokens[at, :].astype(F32) + q * total_of((own, a, b, c), at, slice(0, width))
        resid[at, :] = value
        hidden[at, :] = (value * inverse_rms(value) * gain[...]).astype(BF)
        scale[at, :] = jnp.broadcast_to(q, (STEP, LANES))


def glu_kernel(first, *refs):
    h_near, h_far, d_near, d_far, weight = refs[:5]
    if first:
        d_gate, d_up, act, total = refs[5:]
    else:
        before, d_gate, d_up, act, keep, send = refs[5:]
    half, block = h_near.shape[0], d_gate.shape[1]
    rows = half // 2
    w_gate, w_up, w_down = (slice(k * block, (k + 1) * block) for k in range(3))
    for k, (h, d) in enumerate(((h_near, d_near), (h_far, d_far))):
        for i in range(half // rows):
            at, to = slice(i * rows, (i + 1) * rows), slice(k * half + i * rows, k * half + (i + 1) * rows)
            gate = times_transposed(h[at, :], weight[w_gate, :])
            up = times_transposed(h[at, :], weight[w_up, :])
            d_act = times_transposed(d[at, :], weight[w_down, :])
            sig = jax.nn.sigmoid(gate)
            silu = gate * sig
            act[to, :] = (silu * up).astype(BF)
            d_gate[to, :] = (d_act * up * sigmoid_slope(gate, sig)).astype(BF)
            d_up[to, :] = (d_act * silu).astype(BF)
            value = dot(d_gate[to, :], weight[w_gate, :]) + dot(d_up[to, :], weight[w_up, :])
            if first:
                total[to, :] = value
            elif k == 0:
                keep[at, :] = before[to, :] + value
            else:
                send[at, :] = (before[to, :] + value).astype(BF)


def glu_out_kernel(act0, act1, w0, w1, keep, send):
    half, block = keep.shape[0], act0.shape[1]
    down = slice(2 * block, 3 * block)
    rows = half // 2
    for k in range(4):
        at = slice(k * rows, (k + 1) * rows)
        to = slice(k % 2 * rows, (k % 2 + 1) * rows)
        value = dot(act0[at, :], w0[down, :]) + dot(act1[at, :], w1[down, :])
        if k < 2:
            keep[to, :] = value
        else:
            send[to, :] = value.astype(BF)


def glu_weights_kernel(parts, d_gate, d_up, act, h_near, h_far, d_near, d_far, *outs):
    half, block = h_near.shape[0], d_gate.shape[1]
    part = h_near.shape[1] // parts
    for m, (left, near, far) in enumerate(
        ((d_gate, h_near, h_far), (d_up, h_near, h_far), (act, d_near, d_far))
    ):
        for k in range(parts):
            cols = slice(k * part, (k + 1) * part)
            value = contract_rows(left[:half, :], near[:, cols])
            value = value + contract_rows(left[half:, :], far[:, cols])
            outs[k][m * block : (m + 1) * block, :] = value.astype(BF)


def d_resid_kernel(own, a, b, c, resid, tokens, grad, gain, scale, d_resid, piece):
    width = tokens.shape[1]

    @pl.loop(0, tokens.shape[0] // STEP)
    def _(i):
        at = pl.ds(i * STEP, STEP)
        d_hidden = total_of((own, a, b, c), at, slice(None)) * gain[...]
        value = resid[at, :]
        inv = inverse_rms(value)
        hat = value * inv
        d_value = grad[at, :].astype(F32) + inv * (d_hidden - hat * mean_last(d_hidden * hat))
        d_resid[at, :] = d_value
        low = d_value.astype(BF)
        piece[at, :width] = low
        mean = mean_last(low.astype(F32) * (value - tokens[at, :].astype(F32)))
        piece[at, width:] = stat_block([scale[at, :1], mean]).astype(BF)


def mixer_back_kernel(near, far, out_w, raw, states, mix_gain, decay, *refs):
    mixed, d_gate_raw, local, after, first, d_mixin, d_states = refs
    width = out_w.shape[1]
    group, feats = raw.shape[0], mix_gain.shape[1]
    rows, half = group // CHUNKS, group // 2
    count = feats // LANES
    for k, source in enumerate((near, far)):
        d_mixin[k * half : (k + 1) * half, :] = times_transposed(source[:, :width], out_w[...])
        for s in range(Z):
            part, at = slice(s * rows, (s + 1) * rows), slice(k * half + s * rows, k * half + (s + 1) * rows)
            stats = source[part, width:]
            q, mean = stat(stats, 0), stat(stats, 1)
            for j in range(count):
                lanes = slice(j * LANES, (j + 1) * LANES)
                hat = states[j, at, :] * q
                gate = raw[at, 2 * feats + j * LANES : 2 * feats + (j + 1) * LANES]
                sig = jax.nn.sigmoid(gate)
                silu = gate * sig
                gain = mix_gain[:, lanes]
                d = d_mixin[at, lanes] * gain
                mixed[at, lanes] = (hat * gain * silu).astype(BF)
                d_gate_raw[at, lanes] = (d * hat * sigmoid_slope(gate, sig)).astype(BF)
                d_states[j, at, :] = q * (d * silu - hat * mean)

    def step(t, carry):
        out = []
        at = pl.ds(rows - 1 - t, CHUNKS, stride=rows)
        for j in range(count):
            coming, passed = carry[2 * j], carry[2 * j + 1]
            here = decay[j, at, :]
            adjoint = d_states[j, at, :] + coming
            local[j, at, :] = adjoint
            after[j, at, :] = passed
            out += [here * adjoint, here * passed]
        return tuple(out)

    zero, one = jnp.zeros((CHUNKS, LANES), F32), jnp.ones((CHUNKS, LANES), F32)
    last = lax.fori_loop(0, rows, step, (zero, one) * count, unroll=8)
    for j in range(count):
        first[:, j * LANES : (j + 1) * LANES] = last[2 * j]


def d_mixer_kernel(parties, parts, count, order, *refs):
    edges, firsts = refs[:parties], refs[parties : 2 * parties]
    refs = refs[2 * parties :]
    local, after, states, entry_own, raw, keep_mask, bound, d_gate_raw = refs[:8]
    weights = refs[8 : 8 + parts]
    d_raw, d_bound, keep, send, passed, last, entry = refs[8 + parts :]
    group, feats = raw.shape[0], bound.shape[1]
    rows, half = group // CHUNKS, group // 2
    collect(edges, (0, 2), passed)
    collect(firsts, (0, 1), last)
    entries(order, True, count, passed, last, entry)
    base = pl.multiple_of(order[count], CHUNKS)
    top = lax.broadcasted_iota(jnp.int32, (rows, LANES), 0) == 0
    for j in range(feats // LANES):
        lanes = slice(j * LANES, (j + 1) * LANES)
        coming = entry[pl.ds(base, CHUNKS), lanes]
        low = bound[:, lanes]
        total = jnp.zeros((1, LANES), F32)
        for s in range(CHUNKS):
            at = slice(s * rows, (s + 1) * rows)
            adjoint = local[j, at, :] + after[j, at, :] * coming[s : s + 1, :]
            previous = jnp.where(top, entry_own[s : s + 1, lanes], pltpu.roll(states[j, at, :], 1, 0))
            inner = raw[at, lanes]
            sig_inner = jax.nn.sigmoid(inner)
            sig = jax.nn.sigmoid(raw[at, feats + j * LANES : feats + (j + 1) * LANES])
            open_part = (1.0 - low) * (1.0 - sig)
            d_forget = adjoint * (previous * keep_mask[at, :] - inner * sig_inner)
            d_inner = adjoint * open_part * sigmoid_slope(inner, sig_inner)
            d_raw[at, lanes] = d_inner.astype(BF)
            d_raw[at, feats + j * LANES : feats + (j + 1) * LANES] = (d_forget * open_part * sig).astype(BF)
            total = total + jnp.sum(d_forget * (1.0 - sig), axis=0, keepdims=True)
        d_bound[:, lanes] = total
    d_raw[:, 2 * feats :] = d_gate_raw[...]
    begin = 0
    for w in weights:
        cols = slice(begin, begin + w.shape[0])
        for k in range(2):
            part, part2 = slice(k * half // 2, (k + 1) * half // 2), slice(half + k * half // 2, half + (k + 1) * half // 2)
            keep[part, cols] = times_transposed(d_raw[part, :], w[...])
            send[part, cols] = times_transposed(d_raw[part2, :], w[...]).astype(BF)
        begin += w.shape[0]


def token_grad_kernel(own, a, b, c, tokens, d_resid, gain, out):
    @pl.loop(0, tokens.shape[0] // STEP)
    def _(i):
        at = pl.ds(i * STEP, STEP)
        value = tokens[at, :].astype(F32)
        inv = inverse_rms(value)
        hat = value * inv
        d = total_of((own, a, b, c), at, slice(None)) * gain[...]
        out[at, :] = d_resid[at, :] + inv * (d - hat * mean_last(d * hat))


def result_kernel(own, a, b, c, resid, out):
    @pl.loop(0, resid.shape[0] // STEP)
    def _(i):
        at = pl.ds(i * STEP, STEP)
        out[at, :] = (resid[at, :] + total_of((own, a, b, c), at, slice(None))).astype(BF)


def gather_rows(own):
    near = jnp.concatenate([own] + [across_z(own, k) for k in range(1, Z)], axis=0)
    return near, swap(near, "c")


def scatter_rows(keep, send):
    rows, width = keep.shape[0] // Z, keep.shape[1]
    shapes = [((rows, width), F32)] + [((rows, width), BF)] * (Z - 1)
    own, *others = call(shares_kernel, shapes, keep, swap(send, "c"))
    return [own] + [across_z(v, k + 1) for k, v in enumerate(others)]


def per_device(
    tokens, lengths, w_in, w_forget, w_gate, w_out, attn_gain, mix_gain, bound_table,
    ff_gate, ff_up, ff_down, mlp_gain, out_grad,
):
    Y = lax.axis_size("y")
    pair = Y == 2
    parts = 2 if pair else 1
    z, y, c, x = (lax.axis_index(a) for a in "zycx")
    rows, width = tokens.shape
    sub = w_in.shape[0]
    feats = Y * sub
    block = ff_gate.shape[1] // CHUNKS
    tall = 3 * block
    group = rows * CHUNKS
    half = group // 2
    near_y = y[None].astype(jnp.int32)

    def y_first(*values):
        if pair:
            return call(
                functools.partial(reorder_kernel, False),
                [(v.shape, v.dtype) for v in values], near_y, *values, smem=1,
            )
        return [
            v.reshape(v.shape[0], Z, Y, C * sub).transpose(0, 2, 1, 3).reshape(v.shape) for v in values
        ]

    def z_first(*values):
        if pair:
            return call(
                functools.partial(reorder_kernel, True),
                [(v.shape, v.dtype) for v in values], near_y, *values, smem=1,
            )
        return [
            v.reshape(v.shape[0], Y, Z, C * sub).transpose(0, 2, 1, 3).reshape(v.shape) for v in values
        ]

    def over_y(value):
        if pair:
            return [value, swap(value, "y")]
        return [lax.all_gather(value, "y", axis=0, tiled=True)]

    def in_order(value):
        if pair:
            other = swap(value, "y")
            return jnp.concatenate(
                [jnp.where(y == 0, value, other), jnp.where(y == 0, other, value)], axis=0
            )
        return lax.all_gather(value, "y", axis=0, tiled=True)

    def spread(value):
        return lax.all_to_all(value, ("z", "c"), 0, 0, tiled=True)

    def both(own, sent, axis):
        return own.astype(BF).astype(F32) + swap(sent.astype(BF), axis).astype(F32)

    gains = jnp.stack([attn_gain, mlp_gain])
    if pair:
        gains = jnp.stack([gains, swap(gains, "y")])
        gains = jnp.stack([gains] + [across_z(gains, k) for k in range(1, Z)])
        gains = jnp.stack([gains, swap(gains, "c")]).reshape(CHUNKS, 4 * sub)
        slot = jnp.arange(CHUNKS)
        source = (slot % C ^ c) * Z + (slot // C ^ z)
        pick = (source[:, None] == slot[None, :]).astype(BF)
        gains = dot(pick, gains).reshape(CHUNKS, 2, 2, sub)
        attn_g, mlp_g = (gains[:, :, k].transpose(1, 0, 2).reshape(1, width) for k in range(2))
    else:
        gains = lax.all_gather(gains, ("z", "y", "c"), axis=1, tiled=True).astype(F32)
        attn_g, mlp_g = y_first(gains[:1], gains[1:])

    tokens_y, grad_y = y_first(tokens, out_grad)
    tokens_near, tokens_far = gather_rows(tokens_y)

    if pair:
        (mixer,) = call(mixer_blocks_kernel, [((CHUNKS, sub, 3 * feats), BF)], w_in, w_forget, w_gate)
    else:
        mixer = jnp.concatenate(
            [
                w.reshape(sub, Z, Y, C, sub).transpose(1, 3, 0, 2, 4).reshape(CHUNKS, sub, feats)
                for w in (w_in, w_forget, w_gate)
            ],
            axis=2,
        )
    mixer = over_y(spread(mixer).reshape(CHUNKS * sub, 3 * feats))
    (out_rows,) = y_first(in_order(w_out))
    table_f = bound_table.astype(F32)
    soft = jax.nn.softmax(table_f, axis=0)
    own_bound = jnp.sum(soft[1 : LAYER + 1], axis=0)
    small = in_order(jnp.stack([own_bound, mix_gain.astype(F32)])[None])
    bound = small[:, 0].reshape(1, feats)
    mix_g = small[:, 1].reshape(1, feats)

    if pair:
        (glu,) = call(glu_blocks_kernel, [((CHUNKS, tall, sub), BF)], ff_gate, ff_up, ff_down)
    else:
        glu = jnp.concatenate(
            [w.T.reshape(CHUNKS, block, sub) for w in (ff_gate, ff_up)] + [ff_down.reshape(CHUNKS, block, sub)],
            axis=1,
        )
    glu = spread(glu)
    cut = tall // 2

    def assemble(pieces):
        return jnp.concatenate([p.transpose(1, 0, 2).reshape(p.shape[1], -1) for p in pieces], axis=1)

    if pair:
        side, up_y = swap(glu, "x"), swap(glu, "y")
        corner = jnp.concatenate([swap(up_y[:, :cut], "x"), swap(side[:, cut:], "y")], axis=1)
        glu_w = [assemble([glu, up_y]), assemble([side, corner])]
    else:
        every = assemble(over_y(glu))
        glu_w = [every, swap(every, "x")]

    slot = jnp.arange(lengths.shape[0])
    starts = jnp.sum(jnp.where(slot[None, :] < slot[:, None], lengths[None, :], 0), axis=1)
    slot = jnp.arange(CHUNKS)
    chunk = ((z ^ (slot % Z)) * Y + y) * (C * X) + (c ^ (slot // Z)) * X + x
    position = (chunk[:, None] * rows + jnp.arange(rows)[None, :]).reshape(group)
    keep = 1.0 - jnp.any(position[:, None] == starts[None, :], axis=1).astype(F32)[:, None]
    count = Z * Y * C * X
    number = jnp.arange(count)
    xn, cn = number % X, number // X % C
    yn, zn = number // (X * C) % Y, number // (X * C * Y)
    party = (yn ^ y) * X + (xn ^ x) if pair else yn * X + xn
    order = party * CHUNKS + (cn ^ c) * Z + (zn ^ z)
    base = 0 * y if pair else (y * X + x) * CHUNKS
    order = jnp.concatenate([order, base[None]]).astype(jnp.int32)

    def parties(value):
        if pair:
            corner = lax.ppermute(value, ("y", "x"), [(i, 3 - i) for i in range(4)])
            return [value, swap(value, "x"), swap(value, "y"), corner]
        return [lax.all_gather(value, ("y", "x"), axis=0, tiled=True)]

    crowd = 4 if pair else 1
    featured = ((feats // LANES, group, LANES), F32)
    normed, raw, decay, local, through, edge = call(
        functools.partial(mixer_forward_kernel, parts),
        [((group, width), BF), ((group, 3 * feats), F32)] + [featured] * 3 + [((2 * CHUNKS, feats), F32)],
        attn_g, tokens_near, tokens_far, bound, keep, *mixer,
        scratch=[pltpu.VMEM(*featured)], flops=2 * group * width * 3 * feats,
    )
    edges = parties(edge)
    carries = [pltpu.VMEM((Y * X * CHUNKS, feats), F32)] * 3
    states, entry, keep_rows, send_rows = call(
        functools.partial(mixer_out_kernel, crowd, count),
        [featured, ((CHUNKS, feats), F32), ((half, width + LANES), F32), ((half, width + LANES), BF)],
        order, *edges, local, through, raw, mix_g, out_rows,
        smem=1, scratch=carries + [pltpu.VMEM((group, feats), BF), pltpu.VMEM((group, LANES), F32)],
        flops=2 * group * width * feats,
    )
    resid, hidden, scale = call(
        resid_kernel,
        [((rows, width), F32), ((rows, width), BF), ((rows, LANES), F32)],
        *scatter_rows(keep_rows, send_rows), tokens_y, mlp_g,
    )
    hidden_near, hidden_far = gather_rows(hidden)
    grad_near, grad_far = gather_rows(grad_y)
    wide = [hidden_near, hidden_far, grad_near, grad_far]
    thin = ((group, block), BF)
    glu_flops = 2 * group * width * block
    d_gate0, d_up0, act0, d_hidden = call(
        functools.partial(glu_kernel, True), [thin] * 3 + [((group, width), F32)],
        *wide, glu_w[0], flops=5 * glu_flops,
    )
    d_gate1, d_up1, act1, keep_rows, send_rows = call(
        functools.partial(glu_kernel, False), [thin] * 3 + [((half, width), F32), ((half, width), BF)],
        *wide, glu_w[1], d_hidden, flops=5 * glu_flops,
    )
    d_resid, piece = call(
        d_resid_kernel, [((rows, width), F32), ((rows, width + LANES), BF)],
        *scatter_rows(keep_rows, send_rows), resid, tokens_y, grad_y, mlp_g, scale,
    )
    d_mixed_near, d_mixed_far = gather_rows(piece)

    grads = [
        call(
            functools.partial(glu_weights_kernel, parts), [((tall, width // parts), BF)] * parts,
            *left, *wide, flops=3 * glu_flops,
        )
        for left in ((d_gate0, d_up0, act0), (d_gate1, d_up1, act1))
    ]

    def to_blocks(value):
        return value.reshape(value.shape[0], -1, sub).transpose(1, 0, 2)

    if pair:
        upper = [both(grads[0][k][:cut], grads[1][k][:cut], "x") for k in range(2)]
        lower = [both(grads[k][0][cut:], grads[k][1][cut:], "y") for k in range(2)]
        glu_grad = jnp.concatenate([both(*upper, "y"), both(*lower, "x")], axis=0)
        glu_grad = to_blocks(glu_grad.astype(BF))
    else:
        glu_grad = to_blocks(both(grads[0][0], grads[1][0], "x").astype(BF))
        glu_grad = lax.psum_scatter(glu_grad, "y", scatter_dimension=0, tiled=True)
    glu_grad = spread(glu_grad)

    mixed_in, d_gate_raw, adjoint, after, first = call(
        mixer_back_kernel,
        [((group, feats), BF)] * 2 + [featured] * 2 + [((CHUNKS, feats), F32)],
        d_mixed_near, d_mixed_far, out_rows, raw, states, mix_g, decay,
        scratch=[pltpu.VMEM((group, feats), F32), pltpu.VMEM(*featured)],
        flops=2 * group * width * feats,
    )
    d_raw, part_bound, keep_rows, send_rows = call(
        functools.partial(d_mixer_kernel, crowd, parts, count),
        [((group, 3 * feats), BF), ((1, feats), F32), ((half, width), F32), ((half, width), BF)],
        order, *edges, *parties(first), adjoint, after, states, entry, raw, keep, bound, d_gate_raw, *mixer,
        smem=1, scratch=carries, flops=2 * group * width * 3 * feats,
    )

    act0, act1, _ = lax.optimization_barrier((act0, act1, d_mixed_far))
    keep_out, send_out = call(
        glu_out_kernel, [((half, width), F32), ((half, width), BF)],
        act0, act1, *glu_w, flops=2 * glu_flops,
    )
    (result_y,) = call(result_kernel, [((rows, width), BF)], *scatter_rows(keep_out, send_out), resid)

    (token_grad_y,) = call(
        token_grad_kernel, [((rows, width), F32)],
        *scatter_rows(keep_rows, send_rows), tokens_y, d_resid, attn_g,
    )
    result, token_grad = z_first(result_y, token_grad_y)

    grad_out = contract_rows(mixed_in[:half], d_mixed_near[:, :width])
    grad_out = grad_out + contract_rows(mixed_in[half:], d_mixed_far[:, :width])
    (grad_out,) = z_first(grad_out.astype(BF))
    if pair:
        top, bottom = jnp.split(grad_out, 2, axis=0)
        grad_out = both(jnp.where(y == 0, top, bottom), jnp.where(y == 0, bottom, top), "y")
    else:
        grad_out = lax.psum_scatter(grad_out, "y", scatter_dimension=0, tiled=True)
    grad_out = both(grad_out, grad_out, "x")

    part_bound = part_bound.reshape(feats)
    if pair:
        top, bottom = jnp.split(part_bound, 2)
        d_bound = jnp.where(y == 0, top, bottom) + swap(jnp.where(y == 0, bottom, top), "y")
    else:
        d_bound = lax.psum_scatter(part_bound, "y", scatter_dimension=0, tiled=True)
    d_bound = d_bound + swap(d_bound, "x")
    row_ids = jnp.arange(bound_table.shape[0])[:, None]
    member = jnp.logical_and(row_ids >= 1, row_ids <= LAYER).astype(F32)
    grad_table = soft * (member - own_bound[None, :]) * d_bound[None, :]

    if pair:
        span = width // 2
        mixer_grad = both(*(contract_rows(normed[:, k * span : (k + 1) * span], d_raw) for k in range(2)), "y")
    else:
        mixer_grad = lax.psum_scatter(
            contract_rows(normed, d_raw).astype(BF), "y", scatter_dimension=0, tiled=True
        )
    mixer_grad = both(mixer_grad, mixer_grad, "x").astype(BF)
    mixer_grad = spread(mixer_grad.reshape(CHUNKS, sub, 3 * feats))

    def along(weight, grad):
        return jnp.sum(weight.astype(F32) * grad, axis=1)

    square, glued = ((sub, width), F32), ((sub, CHUNKS * block), F32)
    if pair:
        grad_in, grad_forget, grad_gate, grad_attn = call(
            mixer_grads_kernel, [square] * 3 + [((sub, LANES), F32)], mixer_grad, w_in, w_forget, w_gate
        )
        grad_gate_ff, grad_up_ff, grad_down, grad_mlp = call(
            glu_grads_kernel, [glued] * 2 + [((CHUNKS * block, sub), F32), ((sub, LANES), F32)],
            glu_grad, ff_gate, ff_up,
        )
        grad_attn, grad_mlp = grad_attn[:, 0], grad_mlp[:, 0]
    else:
        mixer_grad = mixer_grad.reshape(Z, C, sub, 3, Y, sub).transpose(3, 2, 0, 4, 1, 5)
        grad_in, grad_forget, grad_gate = mixer_grad.reshape(3, sub, width).astype(F32)
        grad_attn = along(w_in, grad_in) + along(w_forget, grad_forget) + along(w_gate, grad_gate)
        pieces = jnp.split(glu_grad.astype(F32), 3, axis=1)
        grad_gate_ff, grad_up_ff = (p.reshape(CHUNKS * block, sub).T for p in pieces[:2])
        grad_down = pieces[2].reshape(CHUNKS * block, sub)
        grad_mlp = along(ff_gate, grad_gate_ff) + along(ff_up, grad_up_ff)
    grad_attn = grad_attn / attn_gain.astype(F32)
    grad_mix = along(w_out, grad_out) / mix_gain.astype(F32)
    grad_mlp = (grad_mlp + swap(grad_mlp, "x")) / mlp_gain.astype(F32)
    return (
        result, token_grad, grad_in, grad_forget, grad_gate, grad_out, grad_attn, grad_mix,
        grad_table, grad_gate_ff, grad_up_ff, grad_down, grad_mlp,
    )


def solution(mesh):
    dp, mp = mesh.devices.shape
    grid = Mesh(mesh.devices.reshape(Z, dp // CHUNKS, C, mp), ("z", "y", "c", "x"))
    dp_axes = ("z", "y", "c")
    every = ("z", "y", "c", "x")
    mat, row, gain = P(dp_axes, None), P(every, None), P(dp_axes)
    table, glu, glu_down = P(None, dp_axes), P(dp_axes, "x"), P("x", dp_axes)
    return jax.shard_map(
        per_device,
        mesh=grid,
        in_specs=(
            row, P(), mat, mat, mat, mat, gain, gain, table, glu, glu, glu_down, gain, row,
        ),
        out_specs=(
            row, row, mat, mat, mat, mat, gain, gain, table, glu, glu, glu_down, gain,
        ),
        check_vma=False,
    )
```

```python
import functools

import jax
import jax.numpy as jnp
from jax import lax
from jax.experimental import pallas as pl
from jax.experimental.pallas import tpu as pltpu
from jax.sharding import Mesh, PartitionSpec as P

LAYER = 12
Z, C, X = 4, 2, 2
CHUNKS = Z * C
LANES = 128
epsilon = 1e-06
VMEM_LIMIT = 56 << 20
BF, F32 = jnp.bfloat16, jnp.float32


def swap(value, axis):
    return lax.ppermute(value, axis, [(0, 1), (1, 0)])


def dot(left, right):
    return jnp.dot(left, right, preferred_element_type=F32)


def contract_rows(left, right):
    return lax.dot_general(left, right, (((0,), (0,)), ((), ())), preferred_element_type=F32)


def times_transposed(left, right):
    return lax.dot_general(left, right, (((1,), (1,)), ((), ())), preferred_element_type=F32)


def mean_last(value):
    return jnp.mean(value, axis=-1, keepdims=True)


def inverse_rms(value):
    return lax.rsqrt(mean_last(value * value) + epsilon)


def sigmoid_slope(raw, sig):
    return sig * (1.0 + raw * (1.0 - sig))


class Copies:
    def __init__(self, inputs, outputs):
        self.inputs, self.outputs, self.waited, self.flushed = inputs, outputs, set(), set()
        for copy in inputs:
            copy.start()

    def wait(self, *numbers):
        for k in numbers:
            if k not in self.waited:
                self.waited.add(k)
                self.inputs[k].wait()

    def flush(self, *numbers):
        for k in numbers:
            if k not in self.flushed:
                self.flushed.add(k)
                self.outputs[k].start()


def call(kernel, outs, *ins, smem=0, scratch=(), late=None):
    n_in, n_out = len(ins) - smem, len(outs)

    def body(*refs):
        scalars, refs = refs[:smem], refs[smem:]
        far_in, far_out, refs = refs[:n_in], refs[n_in : n_in + n_out], refs[n_in + n_out :]
        near_in, near_out, refs = refs[:n_in], refs[n_in : n_in + n_out], refs[n_in + n_out :]
        *own, in_sems, out_sems = refs
        copies = Copies(
            [pltpu.make_async_copy(f, n, in_sems.at[k]) for k, (f, n) in enumerate(zip(far_in, near_in))],
            [pltpu.make_async_copy(n, f, out_sems.at[k]) for k, (f, n) in enumerate(zip(far_out, near_out))],
        )
        copies.wait(*range(n_in if late is None else late))
        kernel(*([] if late is None else [copies]), *scalars, *near_in, *near_out, *own)
        copies.wait(*range(n_in))
        copies.flush(*range(n_out))
        for copy in copies.outputs:
            copy.wait()

    shapes = [jax.ShapeDtypeStruct(s, t) for s, t in outs]
    near = [pltpu.VMEM(v.shape, v.dtype) for v in list(ins[smem:]) + shapes]
    return pl.pallas_call(
        body,
        out_shape=shapes,
        in_specs=[pl.BlockSpec(memory_space=pltpu.SMEM)] * smem + [pl.BlockSpec(memory_space=pl.ANY)] * n_in,
        out_specs=[pl.BlockSpec(memory_space=pl.ANY)] * n_out,
        scratch_shapes=near
        + list(scratch)
        + [pltpu.SemaphoreType.DMA((n_in,)), pltpu.SemaphoreType.DMA((n_out,))],
        compiler_params=pltpu.CompilerParams(vmem_limit_bytes=VMEM_LIMIT),
        cost_estimate=pl.CostEstimate(flops=0, bytes_accessed=1024, transcendentals=0),
    )(*ins)


def stat_block(columns, first=0):
    rows = columns[0].shape[0]
    lane = lax.broadcasted_iota(jnp.int32, (rows, LANES), 1) - first
    block = jnp.zeros((rows, LANES), F32)
    for k, column in enumerate(columns):
        high = column.astype(BF).astype(F32)
        block = jnp.where(lane == 2 * k, high, block)
        block = jnp.where(lane == 2 * k + 1, column - high, block)
    return block


def stat(block, k):
    lane = lax.broadcasted_iota(jnp.int32, block.shape, 1)
    picked = jnp.where((lane == 2 * k) | (lane == 2 * k + 1), block.astype(F32), 0.0)
    return jnp.sum(picked, axis=1, keepdims=True)


def reorder_kernel(back, y_ref, *refs):
    y = y_ref[0]
    half = len(refs) // 2
    for in_ref, out_ref in zip(refs[:half], refs[half:]):
        width = in_ref.shape[1] // CHUNKS
        for k in range(2):
            there = k + y - 2 * k * y
            for z in range(Z):
                near = slice((k * Z + z) * width, (k * Z + z + 1) * width)
                far = pl.ds(pl.multiple_of((z * 2 + there) * width, width), width)
                if back:
                    out_ref[:, far] = in_ref[:, near]
                else:
                    out_ref[:, near] = in_ref[:, far]


def token_piece_kernel(y_ref, tokens, gains, piece):
    width = tokens.shape[1]
    reorder_kernel(False, y_ref, tokens, piece.at[:, :width])
    row = lax.broadcasted_iota(jnp.int32, (tokens.shape[0], LANES), 0)
    block = jnp.zeros((tokens.shape[0], LANES), F32)
    for k in range(gains.shape[0]):
        block = jnp.where(row == k, gains[k : k + 1, :], block)
    piece[:, width:] = block.astype(BF)


def mixer_blocks_kernel(x_ref, *refs):
    *weights, out_ref = refs
    half = len(weights)
    x = x_ref[0]
    for z in range(Z):
        for c in range(C):
            for k in range(half):
                pieces = []
                for j in (k, half + k):
                    at = ((z * 2 + j % 2) * C + c) * LANES
                    pieces.append(weights[j // 2][:, at : at + LANES])
                out_ref[z * C + c, :, k * LANES : (k + 1) * LANES] = jnp.where(x == 0, *pieces)


def mixer_grads_kernel(
    x_ref, mine, theirs, w_in, w_forget, w_gate, grad_in, grad_forget, grad_gate, along_ref
):
    x = x_ref[0]
    total = jnp.zeros((w_in.shape[0], 1), F32)
    for m, (w_ref, g_ref) in enumerate(((w_in, grad_in), (w_forget, grad_forget), (w_gate, grad_gate))):
        for z in range(Z):
            for y in range(2):
                for c in range(C):
                    to, j = ((z * 2 + y) * C + c) * LANES, m * 2 + y
                    at = j % 3 * LANES
                    piece = jnp.where(
                        x == j // 3,
                        mine[z * C + c, :, at : at + LANES],
                        theirs[z * C + c, :, at : at + LANES],
                    ).astype(F32)
                    g_ref[:, to : to + LANES] = piece
                    weight = w_ref[:, to : to + LANES].astype(F32)
                    total = total + jnp.sum(piece * weight, axis=1, keepdims=True)
    along_ref[...] = jnp.broadcast_to(total, along_ref.shape)


def glu_blocks_kernel(gate_ref, up_ref, down_ref, out_ref):
    block = down_ref.shape[0] // CHUNKS
    for s in range(CHUNKS):
        at = slice(s * block, (s + 1) * block)
        out_ref[s, :block] = gate_ref[:, at].astype(F32).T.astype(BF)
        out_ref[s, block : 2 * block] = up_ref[:, at].astype(F32).T.astype(BF)
        out_ref[s, 2 * block :] = down_ref[at, :]


def glu_grads_kernel(blocks_ref, w_gate, w_up, grad_gate, grad_up, grad_down, along_ref):
    block = blocks_ref.shape[1] // 3
    total = jnp.zeros((w_gate.shape[0], 1), F32)
    for s in range(CHUNKS):
        at = slice(s * block, (s + 1) * block)
        for m, (w_ref, g_ref) in enumerate(((w_gate, grad_gate), (w_up, grad_up))):
            piece = blocks_ref[s, m * block : (m + 1) * block].astype(F32).T
            g_ref[:, at] = piece
            total = total + jnp.sum(piece * w_ref[:, at].astype(F32), axis=1, keepdims=True)
        grad_down[at, :] = blocks_ref[s, 2 * block :].astype(F32)
    along_ref[...] = jnp.broadcast_to(total, along_ref.shape)


def columns_of(x_ref, parts, k, span):
    if parts == 1:
        return slice(0, span)
    return pl.ds(pl.multiple_of((k + x_ref[0] - 2 * k * x_ref[0]) * span, LANES), span)


def mixer_forward_kernel(parts, copies, x_ref, *refs):
    gain, tokens, bound, keep = refs[:4]
    weights = refs[4 : 4 + parts * parts]
    normed, raw, decay, local, through, edge, drive = refs[4 + parts * parts :]
    group, feats = raw.shape[0], bound.shape[1]
    width = gain.shape[1]
    rows = group // CHUNKS

    @pl.loop(0, group // 32)
    def _(i):
        at = pl.ds(i * 32, 32)
        value = tokens[at, :width].astype(F32)
        normed[at, :] = (value * inverse_rms(value) * gain[...]).astype(BF)

    copies.flush(0)
    copies.wait(*range(2, 4 + parts * parts))

    @pl.loop(0, 4)
    def _(i):
        at = pl.ds(i * (group // 4), group // 4)
        deep, span = width // parts, 3 * feats // parts
        for k in range(parts):
            total = None
            for d in range(parts):
                part = dot(normed[at, d * deep : (d + 1) * deep], weights[d * parts + k][...])
                total = part if total is None else total + part
            raw[at, columns_of(x_ref, parts, k, span)] = total

    copies.flush(1)
    count = feats // LANES

    @pl.loop(0, CHUNKS)
    def _(i):
        at = pl.ds(i * rows, rows)
        for j in range(count):
            lanes = slice(j * LANES, (j + 1) * LANES)
            inner = raw[at, lanes]
            forget_raw = raw[at, feats + j * LANES : feats + (j + 1) * LANES]
            low = bound[:, lanes]
            forget = low + (1.0 - low) * jax.nn.sigmoid(forget_raw)
            drive[j, at, :] = inner * jax.nn.sigmoid(inner) * (1.0 - forget)
            decay[j, at, :] = forget * keep[at, :]

    copies.flush(2)

    def step(t, carry):
        out = []
        at = pl.ds(t, CHUNKS, stride=rows)
        for j in range(count):
            state, passed = carry[2 * j], carry[2 * j + 1]
            here = decay[j, at, :]
            state = here * state + drive[j, at, :]
            passed = here * passed
            local[j, at, :] = state
            through[j, at, :] = passed
            out += [state, passed]
        return tuple(out)

    zero, one = jnp.zeros((CHUNKS, LANES), F32), jnp.ones((CHUNKS, LANES), F32)
    last = lax.fori_loop(0, rows, step, (zero, one) * count, unroll=8)
    for j in range(count):
        edge[:CHUNKS, j * LANES : (j + 1) * LANES] = last[2 * j + 1]
        edge[CHUNKS:, j * LANES : (j + 1) * LANES] = last[2 * j]


def entries(order, backwards, count, passed, last, entry):
    def step(n, running):
        row = pl.ds(order[count - 1 - n if backwards else n], 1)
        entry[row, :] = running
        return passed[row, :] * running + last[row, :]

    lax.fori_loop(0, count, step, jnp.zeros((1, last.shape[1]), F32))


def collect(parties, at, to):
    base = 0
    for p in parties:
        for g in range(p.shape[0] // (at[1] * CHUNKS)):
            begin = (g * at[1] + at[0]) * CHUNKS
            to[base : base + CHUNKS, :] = p[begin : begin + CHUNKS, :]
            base += CHUNKS


def mixer_out_kernel(parties, count, copies, order, *refs):
    edges = refs[:parties]
    local, through, raw, mix_gain, out_w = refs[parties : parties + 5]
    states, entry_own, partial, passed, last, entry, mixed = refs[parties + 5 :]
    group, feats = raw.shape[0], mix_gain.shape[1]
    width = out_w.shape[1]
    rows = group // CHUNKS
    collect(edges, (0, 2), passed)
    collect(edges, (1, 2), last)
    entries(order, False, count, passed, last, entry)
    base = order[count]
    entry_own[...] = entry[pl.ds(pl.multiple_of(base, CHUNKS), CHUNKS), :]
    copies.wait(*range(parties, parties + 4))
    for s in range(CHUNKS):
        at = slice(s * rows, (s + 1) * rows)
        total = jnp.zeros((rows, LANES), F32)
        for j in range(feats // LANES):
            lanes = slice(j * LANES, (j + 1) * LANES)
            state = local[j, at, :] + through[j, at, :] * entry_own[s : s + 1, lanes]
            gate = raw[at, 2 * feats + j * LANES : 2 * feats + (j + 1) * LANES]
            mixed[at, lanes] = (state * (mix_gain[:, lanes] * (gate * jax.nn.sigmoid(gate)))).astype(BF)
            states[j, at, :] = state
            total = total + state * state
        squares = jnp.sum(total, axis=1, keepdims=True)
        partial[at, width:] = stat_block([squares], 2 * order[count + 1]).astype(BF)
    copies.flush(0)
    copies.wait(parties + 4)
    for k in range(4):
        at = slice(k * group // 4, (k + 1) * group // 4)
        partial[at, :width] = dot(mixed[at, :], out_w[...]).astype(BF)


STEP = 16


def resid_kernel(summed, tokens, gain, resid, hidden, scale):
    width = tokens.shape[1]

    @pl.loop(0, tokens.shape[0] // STEP)
    def _(i):
        at = pl.ds(i * STEP, STEP)
        squares = jnp.sum(summed[at, width:].astype(F32), axis=1, keepdims=True)
        q = lax.rsqrt(squares / width + epsilon)
        value = tokens[at, :].astype(F32) + q * summed[at, :width].astype(F32)
        resid[at, :] = value
        hidden[at, :] = (value * inverse_rms(value) * gain[...]).astype(BF)
        scale[at, :] = jnp.broadcast_to(q, (STEP, LANES))


def glu_kernel(copies, hidden, grad, *refs):
    weights, outs, total, partial = refs[:4], refs[4:10], refs[11], refs[10]
    group, block = outs[0].shape
    for k in range(2):
        gate_up, down = weights[k], weights[2 + k]
        act, d_gate, d_up = outs[3 * k : 3 * k + 3]
        w_gate, w_up = gate_up.at[:block, :], gate_up.at[block:, :]
        copies.wait(0, 2 + k)
        for i in range(4):
            at = slice(i * group // 4, (i + 1) * group // 4)
            gate = times_transposed(hidden[at, :], w_gate[...])
            up = times_transposed(hidden[at, :], w_up[...])
            copies.wait(1, 4 + k)
            d_act = times_transposed(grad[at, :], down[...])
            sig = jax.nn.sigmoid(gate)
            silu = gate * sig
            act[at, :] = (silu * up).astype(BF)
            d_gate[at, :] = (d_act * up * sigmoid_slope(gate, sig)).astype(BF)
            d_up[at, :] = (d_act * silu).astype(BF)
            value = dot(d_gate[at, :], w_gate[...]) + dot(d_up[at, :], w_up[...])
            if k == 0:
                total[at, :] = value
            else:
                partial[at, :] = (total[at, :] + value).astype(BF)
        copies.flush(3 * k, 3 * k + 1, 3 * k + 2)


def glu_out_kernel(act0, act1, w0, w1, partial):
    group = act0.shape[0]
    for k in range(4):
        at = slice(k * group // 4, (k + 1) * group // 4)
        partial[at, :] = (dot(act0[at, :], w0[...]) + dot(act1[at, :], w1[...])).astype(BF)


def glu_weights_kernel(parts, terms, *refs):
    count = len(terms)
    lefts, rights, outs = refs[: 2 * count], refs[2 * count : 2 * count + max(terms) + 1], None
    outs = refs[2 * count + max(terms) + 1 :]
    block = lefts[0].shape[1]
    part = rights[0].shape[1] // parts
    cut = count * block // 2
    for k in range(2):
        for m, right in enumerate(terms):
            begin, end = m * block, (m + 1) * block
            for d in range(parts):
                value = contract_rows(lefts[k * count + m][...], rights[right][:, d * part : (d + 1) * part])
                value = value.astype(BF)
                if parts == 1:
                    outs[k][begin:end, :] = value
                    continue
                upper, lower = outs[k], outs[2 + d]
                if begin < cut:
                    upper[d, begin : min(end, cut)] = value[: min(end, cut) - begin]
                if end > cut:
                    lower[k, max(begin, cut) - cut : end - cut] = value[max(begin, cut) - begin :]


def first_sums_kernel(upper, upper_got, lower, lower_got, upper_keep, upper_send, lower_keep, lower_send):
    for mine, got, keep, send in (
        (upper, upper_got, upper_keep, upper_send),
        (lower, lower_got, lower_keep, lower_send),
    ):
        keep[...] = mine[0].astype(F32) + got[0].astype(F32)
        send[...] = (mine[1].astype(F32) + got[1].astype(F32)).astype(BF)


def last_sums_kernel(*refs):
    *pieces, blocks = refs
    begin = 0
    for mine, got in zip(pieces[::2], pieces[1::2]):
        for s in range(CHUNKS):
            cols = slice(s * LANES, (s + 1) * LANES)
            blocks[s, begin : begin + mine.shape[0]] = (mine[:, cols] + got[:, cols].astype(F32)).astype(BF)
        begin += mine.shape[0]


def d_resid_kernel(summed, resid, tokens, grad, gain, scale, d_resid, piece):
    width = tokens.shape[1]

    @pl.loop(0, tokens.shape[0] // STEP)
    def _(i):
        at = pl.ds(i * STEP, STEP)
        d_hidden = summed[at, :].astype(F32) * gain[...]
        value = resid[at, :]
        inv = inverse_rms(value)
        hat = value * inv
        d_value = grad[at, :].astype(F32) + inv * (d_hidden - hat * mean_last(d_hidden * hat))
        d_resid[at, :] = d_value
        low = d_value.astype(BF)
        piece[at, :width] = low
        mean = mean_last(low.astype(F32) * (value - tokens[at, :].astype(F32)))
        piece[at, width:] = stat_block([scale[at, :1], mean]).astype(BF)


def mixer_back_kernel(copies, d_mixed, out_w, raw, states, mix_gain, decay, *refs):
    mixed, d_gate_raw, local, after, first, d_mixin, d_states = refs
    width = out_w.shape[1]
    group, feats = raw.shape[0], mix_gain.shape[1]
    rows = group // CHUNKS
    count = feats // LANES
    for k in range(2):
        at = slice(k * group // 2, (k + 1) * group // 2)
        d_mixin[at, :] = times_transposed(d_mixed[at, :width], out_w[...])
    copies.wait(2, 3, 4, 5)
    for s in range(CHUNKS):
        at = slice(s * rows, (s + 1) * rows)
        stats = d_mixed[at, width:]
        q, mean = stat(stats, 0), stat(stats, 1)
        for j in range(count):
            lanes = slice(j * LANES, (j + 1) * LANES)
            hat = states[j, at, :] * q
            gate = raw[at, 2 * feats + j * LANES : 2 * feats + (j + 1) * LANES]
            sig = jax.nn.sigmoid(gate)
            silu = gate * sig
            gain = mix_gain[:, lanes]
            d = d_mixin[at, lanes] * gain
            mixed[at, lanes] = (hat * gain * silu).astype(BF)
            d_gate_raw[at, lanes] = (d * hat * sigmoid_slope(gate, sig)).astype(BF)
            d_states[j, at, :] = q * (d * silu - hat * mean)
    copies.flush(0, 1)

    def step(t, carry):
        out = []
        at = pl.ds(rows - 1 - t, CHUNKS, stride=rows)
        for j in range(count):
            coming, passed = carry[2 * j], carry[2 * j + 1]
            here = decay[j, at, :]
            adjoint = d_states[j, at, :] + coming
            local[j, at, :] = adjoint
            after[j, at, :] = passed
            out += [here * adjoint, here * passed]
        return tuple(out)

    zero, one = jnp.zeros((CHUNKS, LANES), F32), jnp.ones((CHUNKS, LANES), F32)
    last = lax.fori_loop(0, rows, step, (zero, one) * count, unroll=8)
    for j in range(count):
        first[:, j * LANES : (j + 1) * LANES] = last[2 * j]


def mixer_weights_kernel(parts, normed, *refs):
    d_raw, outs = refs[:parts], refs[parts:]
    deep = normed.shape[1] // parts
    for d in range(parts):
        for k in range(parts):
            outs[d * parts + k][...] = contract_rows(normed[:, d * deep : (d + 1) * deep], d_raw[k][...]).astype(BF)


def d_mixer_kernel(parties, parts, count, copies, x_ref, order, *refs):
    edges, firsts = refs[:parties], refs[parties : 2 * parties]
    refs = refs[2 * parties :]
    local, after, states, entry_own, raw, keep_mask, bound, d_gate_raw = refs[:8]
    weights = refs[8 : 8 + parts * parts]
    refs = refs[8 + parts * parts :]
    d_parts, (d_bound, partial, passed, last, entry, d_raw) = refs[:parts], refs[parts:]
    group, feats = raw.shape[0], bound.shape[1]
    rows = group // CHUNKS
    collect(edges, (0, 2), passed)
    collect(firsts, (0, 1), last)
    entries(order, True, count, passed, last, entry)
    base = pl.multiple_of(order[count], CHUNKS)
    copies.wait(*range(2 * parties, 2 * parties + 8))
    top = lax.broadcasted_iota(jnp.int32, (rows, LANES), 0) == 0
    for j in range(feats // LANES):
        lanes = slice(j * LANES, (j + 1) * LANES)
        coming = entry[pl.ds(base, CHUNKS), lanes]
        low = bound[:, lanes]
        total = jnp.zeros((1, LANES), F32)
        for s in range(CHUNKS):
            at = slice(s * rows, (s + 1) * rows)
            adjoint = local[j, at, :] + after[j, at, :] * coming[s : s + 1, :]
            previous = jnp.where(top, entry_own[s : s + 1, lanes], pltpu.roll(states[j, at, :], 1, 0))
            inner = raw[at, lanes]
            sig_inner = jax.nn.sigmoid(inner)
            sig = jax.nn.sigmoid(raw[at, feats + j * LANES : feats + (j + 1) * LANES])
            open_part = (1.0 - low) * (1.0 - sig)
            d_forget = adjoint * (previous * keep_mask[at, :] - inner * sig_inner)
            d_inner = adjoint * open_part * sigmoid_slope(inner, sig_inner)
            d_raw[at, lanes] = d_inner.astype(BF)
            d_raw[at, feats + j * LANES : feats + (j + 1) * LANES] = (d_forget * open_part * sig).astype(BF)
            total = total + jnp.sum(d_forget * (1.0 - sig), axis=0, keepdims=True)
        d_bound[:, lanes] = total
    d_raw[:, 2 * feats :] = d_gate_raw[...]
    for k, d_part in enumerate(d_parts):
        d_part[...] = d_raw[:, columns_of(x_ref, parts, k, 3 * feats // parts)]
    copies.flush(*range(parts + 1))
    copies.wait(*range(2 * parties + 8, 2 * parties + 8 + parts * parts))
    deep = partial.shape[1] // parts
    for d in range(parts):
        for i in range(4):
            at = slice(i * group // 4, (i + 1) * group // 4)
            total = None
            for k, d_part in enumerate(d_parts):
                part = times_transposed(d_part[at, :], weights[d * parts + k][...])
                total = part if total is None else total + part
            partial[at, d * deep : (d + 1) * deep] = total.astype(BF)


def token_grad_kernel(summed, tokens, d_resid, gain, out):
    @pl.loop(0, tokens.shape[0] // STEP)
    def _(i):
        at = pl.ds(i * STEP, STEP)
        value = tokens[at, :].astype(F32)
        inv = inverse_rms(value)
        hat = value * inv
        d = summed[at, :].astype(F32) * gain[...]
        out[at, :] = d_resid[at, :] + inv * (d - hat * mean_last(d * hat))


def result_kernel(summed, resid, out):
    out[...] = (resid[...] + summed[...].astype(F32)).astype(BF)


def after(value, *others):
    return lax.optimization_barrier((value, *others))[0]


def gather_rows(own):
    return lax.all_gather(own, ("z", "c"), axis=0, tiled=True)


def scatter_rows(partial):
    return lax.psum_scatter(partial, ("z", "c"), scatter_dimension=0, tiled=True)


def per_device(
    tokens, lengths, w_in, w_forget, w_gate, w_out, attn_gain, mix_gain, bound_table,
    ff_gate, ff_up, ff_down, mlp_gain, out_grad,
):
    Y = lax.axis_size("y")
    pair = Y == 2
    parts = 2 if pair else 1
    z, y, c, x = (lax.axis_index(a) for a in "zycx")
    rows, width = tokens.shape
    sub = w_in.shape[0]
    feats = Y * sub
    block = ff_gate.shape[1] // CHUNKS
    tall = 3 * block
    group = rows * CHUNKS
    near_y = y[None].astype(jnp.int32)

    def y_first(*values):
        if pair:
            return call(
                functools.partial(reorder_kernel, False),
                [(v.shape, v.dtype) for v in values], near_y, *values, smem=1,
            )
        return [
            v.reshape(v.shape[0], Z, Y, C * sub).transpose(0, 2, 1, 3).reshape(v.shape) for v in values
        ]

    def z_first(*values):
        if pair:
            return call(
                functools.partial(reorder_kernel, True),
                [(v.shape, v.dtype) for v in values], near_y, *values, smem=1,
            )
        return [
            v.reshape(v.shape[0], Y, Z, C * sub).transpose(0, 2, 1, 3).reshape(v.shape) for v in values
        ]

    def over_y(value):
        if pair:
            return [value, swap(value, "y")]
        return [lax.all_gather(value, "y", axis=0, tiled=True)]

    def in_order(value):
        if pair:
            other = swap(value, "y")
            return jnp.concatenate(
                [jnp.where(y == 0, value, other), jnp.where(y == 0, other, value)], axis=0
            )
        return lax.all_gather(value, "y", axis=0, tiled=True)

    def spread(value):
        return lax.all_to_all(value, ("z", "c"), 0, 0, tiled=True)

    def both(own, sent, axis):
        return own.astype(BF).astype(F32) + swap(sent.astype(BF), axis).astype(F32)

    near_x = x[None].astype(jnp.int32)

    def own_and_neighbours(value):
        corner = lax.ppermute(value, ("y", "x"), [(i, 3 - i) for i in range(4)])
        return [value, swap(value, "x"), swap(value, "y"), corner]

    table_f = bound_table.astype(F32)
    soft = jax.nn.softmax(table_f, axis=0)
    own_bound = jnp.sum(soft[1 : LAYER + 1], axis=0)

    tokens_y, grad_y = y_first(tokens, out_grad)
    if pair:
        (blocks,) = call(
            mixer_blocks_kernel, [((CHUNKS, sub, 3 * feats // 2), BF)], near_x, w_in, w_forget, w_gate, smem=1
        )
        moved = spread(blocks)
        small = jnp.stack([attn_gain.astype(F32), mlp_gain.astype(F32), own_bound, mix_gain.astype(F32)])
        small = [small, swap(small, "y")]
        (piece,) = call(
            token_piece_kernel, [((rows, width + LANES), BF)],
            near_y, tokens, jnp.concatenate([v[:2] for v in small]), smem=1,
        )
        grad_all = gather_rows(grad_y)
        tokens_all = gather_rows(after(piece, moved))
        gains = tokens_all.reshape(CHUNKS, rows, -1)[:, :4, width:].astype(F32)
        attn_g, mlp_g = (
            jnp.concatenate([gains[:, k].reshape(1, -1), gains[:, 2 + k].reshape(1, -1)], axis=1) for k in range(2)
        )
        small = jnp.stack([v[2:] for v in small])
        small = jnp.where(y == 0, small, small[::-1])
        mixer = own_and_neighbours(moved.reshape(CHUNKS * sub, 3 * feats // 2))
    else:
        gains = lax.all_gather(jnp.stack([attn_gain, mlp_gain]), ("z", "y", "c"), axis=1, tiled=True)
        attn_g, mlp_g = y_first(gains[:1].astype(F32), gains[1:].astype(F32))
        tokens_all, grad_all = gather_rows(tokens_y), gather_rows(grad_y)
        small = in_order(jnp.stack([own_bound, mix_gain.astype(F32)])[None])
        mixer = [
            w.reshape(sub, Z, Y, C, sub).transpose(1, 3, 0, 2, 4).reshape(CHUNKS, sub, feats)
            for w in (w_in, w_forget, w_gate)
        ]
        moved = spread(jnp.concatenate(mixer, axis=2))
        mixer = over_y(moved.reshape(CHUNKS * sub, 3 * feats))
    (out_rows,) = y_first(in_order(w_out))
    bound = small[:, 0].reshape(1, feats)
    mix_g = small[:, 1].reshape(1, feats)

    if pair:
        (glu,) = call(glu_blocks_kernel, [((CHUNKS, tall, sub), BF)], ff_gate, ff_up, ff_down)
    else:
        glu = jnp.concatenate([w.T.reshape(CHUNKS, block, sub) for w in (ff_gate, ff_up)], axis=1)
        glu = jnp.concatenate([glu, ff_down.reshape(CHUNKS, block, sub)], axis=1)
    glu = spread(after(glu, moved))

    slot = jnp.arange(lengths.shape[0])
    starts = jnp.sum(jnp.where(slot[None, :] < slot[:, None], lengths[None, :], 0), axis=1)
    slot = jnp.arange(CHUNKS)
    chunk = (slot // C * Y + y) * (C * X) + slot % C * X + x
    position = (chunk[:, None] * rows + jnp.arange(rows)[None, :]).reshape(group)
    keep = 1.0 - jnp.any(position[:, None] == starts[None, :], axis=1).astype(F32)[:, None]
    count = Z * Y * C * X
    number = jnp.arange(count)
    xn, cn = number % X, number // X % C
    yn, zn = number // (X * C) % Y, number // (X * C * Y)
    party = (yn ^ y) * X + (xn ^ x) if pair else yn * X + xn
    order = party * CHUNKS + zn * C + cn
    base = 0 * y if pair else (y * X + x) * CHUNKS
    order = jnp.concatenate([order, jnp.stack([base, z * C + c])]).astype(jnp.int32)

    def parties(value):
        if pair:
            return own_and_neighbours(value)
        return [lax.all_gather(value, ("y", "x"), axis=0, tiled=True)]

    crowd = 4 if pair else 1
    featured = ((feats // LANES, group, LANES), F32)
    normed, raw, decay, local, through, edge = call(
        functools.partial(mixer_forward_kernel, parts),
        [((group, width), BF), ((group, 3 * feats), F32)] + [featured] * 3 + [((2 * CHUNKS, feats), F32)],
        near_x, attn_g, tokens_all, bound, keep, *mixer,
        smem=1, scratch=[pltpu.VMEM(*featured)], late=2,
    )
    edges = parties(edge)
    def assemble(pieces):
        return jnp.concatenate([p.transpose(1, 0, 2).reshape(p.shape[1], -1) for p in pieces], axis=1)

    def around(blocks):
        cut = blocks.shape[1] // 2
        side, up_y = swap(blocks, "x"), swap(blocks, "y")
        corner = [swap(up_y[:, :cut], "x"), swap(side[:, cut:], "y")]
        near, far = assemble([blocks, up_y]), assemble([side, jnp.concatenate(corner, axis=1)])
        return [near, far], (side, up_y), corner

    early, late, last = (), (), ()
    gate_up, down = glu[:, : 2 * block], glu[:, 2 * block :]
    if pair:
        gate_up_w, early, _ = around(after(gate_up, edges[0]))
        down_w, late, last = around(after(down, *early))
    else:
        gate_up_w, down_w = (assemble(over_y(v)) for v in (gate_up, down))
        gate_up_w, down_w = ([v, swap(v, "x")] for v in (gate_up_w, down_w))
    carries = [pltpu.VMEM((Y * X * CHUNKS, feats), F32)] * 3
    states, entry, partial = call(
        functools.partial(mixer_out_kernel, crowd, count),
        [featured, ((CHUNKS, feats), F32), ((group, width + LANES), BF)],
        order, *edges, local, through, raw, mix_g, out_rows,
        smem=1, scratch=carries + [pltpu.VMEM((group, feats), BF)], late=crowd,
    )
    summed = scatter_rows(after(partial, glu))
    resid, hidden, scale = call(
        resid_kernel,
        [((rows, width), F32), ((rows, width), BF), ((rows, LANES), F32)],
        after(summed, *early), tokens_y, mlp_g,
    )
    hidden_all = after(gather_rows(hidden), *late)
    thin = ((group, block), BF)
    act0, d_gate0, d_up0, act1, d_gate1, d_up1, partial = call(
        glu_kernel, [thin] * 6 + [((group, width), BF)],
        hidden_all, grad_all, *gate_up_w, *down_w, late=0, scratch=[pltpu.VMEM((group, width), F32)],
    )
    acts = [act0, act1]

    def weight_pieces(terms, lefts, *rights):
        height = len(terms) * block
        shapes = [((height, width), BF)] * 2
        if pair:
            shapes = [((2, height // 2, width // 2), BF)] * 4
        return call(
            functools.partial(glu_weights_kernel, parts, terms), shapes, *lefts, *rights,
        )

    def first_swaps(pieces):
        upper, upper_sent, lower, lower_sent = pieces
        return upper, swap(upper_sent, "x"), lower, swap(lower_sent, "y")

    def first_sums(pieces):
        height = pieces[0].shape[1]
        shapes = [((height, width // 2), F32), ((height, width // 2), BF)] * 2
        return call(first_sums_kernel, shapes, *pieces)

    def last_swaps(pieces):
        upper, upper_sent, lower, lower_sent = pieces
        return upper, swap(upper_sent, "y"), lower, swap(lower_sent, "x")

    def last_sums(*pieces):
        return call(last_sums_kernel, [((CHUNKS, tall, sub), BF)], *pieces)[0]

    def to_blocks(value):
        return value.reshape(value.shape[0], -1, sub).transpose(1, 0, 2)

    def total_blocks(pieces):
        blocks = to_blocks(both(*pieces, "x").astype(BF))
        return lax.psum_scatter(blocks, "y", scatter_dimension=0, tiled=True)

    summed = scatter_rows(partial)
    gate_up = weight_pieces((0, 0), [d_gate0, d_up0, d_gate1, d_up1], hidden_all)
    (partial_out,) = call(glu_out_kernel, [((group, width), BF)], *acts, *down_w)
    down = weight_pieces((0,), acts, grad_all)
    summed = after(summed, partial_out, *down)
    if pair:
        gate_up = first_swaps(gate_up)
        summed, *gate_up = lax.optimization_barrier((summed, *gate_up))
        gate_up = first_sums(gate_up)
    d_resid, piece = call(
        d_resid_kernel, [((rows, width), F32), ((rows, width + LANES), BF)],
        summed, resid, tokens_y, grad_y, mlp_g, scale,
    )
    d_mixed = gather_rows(piece)
    if pair:
        down = first_swaps(down)
        gate_up = last_swaps(gate_up)
        d_mixed, *gate_up = lax.optimization_barrier((d_mixed, *gate_up))
        d_mixed, *down = lax.optimization_barrier((d_mixed, *down))
        down = first_sums(down)

    mixed_in, d_gate_raw, adjoint, passed, first = call(
        mixer_back_kernel,
        [((group, feats), BF)] * 2 + [featured] * 2 + [((CHUNKS, feats), F32)],
        d_mixed, out_rows, raw, states, mix_g, decay,
        scratch=[pltpu.VMEM((group, feats), F32), pltpu.VMEM(*featured)], late=2,
    )
    firsts = parties(first)
    if pair:
        down = last_swaps(after(down, *firsts))
        glu_grad = last_sums(*gate_up, *down)
    else:
        glu_grad = jnp.concatenate([total_blocks(gate_up), total_blocks(down)], axis=1)
    glu_grad = spread(glu_grad)
    *d_raw, part_bound, partial = call(
        functools.partial(d_mixer_kernel, crowd, parts, count),
        [((group, 3 * feats // parts), BF)] * parts
        + [((1, feats), F32), ((group, width), BF)],
        near_x, order, *edges, *firsts, adjoint, passed, states, entry, raw, keep, bound, d_gate_raw, *mixer,
        smem=2, scratch=carries + [pltpu.VMEM((group, 3 * feats), BF)], late=2 * crowd,
    )

    result_sum = scatter_rows(after(partial_out, d_mixed))
    (token_grad_y,) = call(
        token_grad_kernel, [((rows, width), F32)],
        after(scatter_rows(partial), result_sum), tokens_y, d_resid, attn_g,
    )
    (result_y,) = call(result_kernel, [((rows, width), BF)], result_sum, resid)
    result, token_grad = z_first(result_y, token_grad_y)

    pieces = call(
        functools.partial(mixer_weights_kernel, parts),
        [((width // parts, 3 * feats // parts), BF)] * parts**2,
        normed, *d_raw,
    )
    part_bound = part_bound.reshape(feats)
    if pair:
        pieces = [
            pieces[0],
            swap(pieces[1], "x"),
            swap(pieces[2], "y"),
            lax.ppermute(pieces[3], ("y", "x"), [(i, 3 - i) for i in range(4)]),
        ]
        mixer_grad = sum(p.astype(F32) for p in pieces).astype(BF)
        mixed_in, part_bound = after((mixed_in, part_bound), mixer_grad)
        top, bottom = jnp.split(part_bound, 2)
        d_bound = jnp.where(y == 0, top, bottom) + swap(jnp.where(y == 0, bottom, top), "y")
    else:
        d_bound = lax.psum_scatter(part_bound, "y", scatter_dimension=0, tiled=True)
        mixer_grad = lax.psum_scatter(pieces[0], "y", scatter_dimension=0, tiled=True)
        mixer_grad = both(mixer_grad, mixer_grad, "x").astype(BF)
    d_bound = d_bound + swap(d_bound, "x")
    row_ids = jnp.arange(bound_table.shape[0])[:, None]
    member = jnp.logical_and(row_ids >= 1, row_ids <= LAYER).astype(F32)
    grad_table = soft * (member - own_bound[None, :]) * d_bound[None, :]
    mixer_grad = spread(after(mixer_grad, glu_grad).reshape(CHUNKS, sub, 3 * feats // parts))

    grad_out = contract_rows(mixed_in, d_mixed[:, :width])
    (grad_out,) = z_first(grad_out.astype(BF))
    if pair:
        top, bottom = jnp.split(grad_out, 2, axis=0)
        grad_out = both(jnp.where(y == 0, top, bottom), jnp.where(y == 0, bottom, top), "y")
    else:
        grad_out = lax.psum_scatter(grad_out, "y", scatter_dimension=0, tiled=True)
    grad_out = both(grad_out, grad_out, "x")
    if pair:
        mixer_grad = after(mixer_grad, grad_out, d_bound)
        mixer_grad = [mixer_grad, swap(mixer_grad, "x")]

    def along(weight, grad):
        return jnp.sum(weight.astype(F32) * grad, axis=1)

    square, glued = ((sub, width), F32), ((sub, CHUNKS * block), F32)
    if pair:
        grad_gate_ff, grad_up_ff, grad_down, grad_mlp = call(
            glu_grads_kernel, [glued] * 2 + [((CHUNKS * block, sub), F32), ((sub, LANES), F32)],
            glu_grad, ff_gate, ff_up,
        )
        grad_mlp = grad_mlp[:, 0]
        grad_mlp = grad_mlp + swap(grad_mlp, "x")
        grad_in, grad_forget, grad_gate, grad_attn = call(
            mixer_grads_kernel, [square] * 3 + [((sub, LANES), F32)],
            near_x, mixer_grad[0], after(mixer_grad[1], grad_mlp), w_in, w_forget, w_gate, smem=1,
        )
        grad_attn = grad_attn[:, 0]
    else:
        mixer_grad = mixer_grad.reshape(Z, C, sub, 3, Y, sub).transpose(3, 2, 0, 4, 1, 5)
        grad_in, grad_forget, grad_gate = mixer_grad.reshape(3, sub, width).astype(F32)
        grad_attn = along(w_in, grad_in) + along(w_forget, grad_forget) + along(w_gate, grad_gate)
        grad_gate_ff, grad_up_ff = (
            glu_grad[:, k * block : (k + 1) * block].astype(F32).reshape(CHUNKS * block, sub).T for k in range(2)
        )
        grad_down = glu_grad[:, 2 * block :].reshape(CHUNKS * block, sub).astype(F32)
        grad_mlp = along(ff_gate, grad_gate_ff) + along(ff_up, grad_up_ff)
        grad_mlp = grad_mlp + swap(grad_mlp, "x")
    grad_attn = grad_attn / attn_gain.astype(F32)
    grad_mix = along(w_out, grad_out) / mix_gain.astype(F32)
    grad_mlp = grad_mlp / mlp_gain.astype(F32)
    return (
        result, token_grad, grad_in, grad_forget, grad_gate, grad_out, grad_attn, grad_mix,
        grad_table, grad_gate_ff, grad_up_ff, grad_down, grad_mlp,
    )


def solution(mesh):
    dp, mp = mesh.devices.shape
    grid = Mesh(mesh.devices.reshape(Z, dp // CHUNKS, C, mp), ("z", "y", "c", "x"))
    dp_axes = ("z", "y", "c")
    every = ("z", "y", "c", "x")
    mat, row, gain = P(dp_axes, None), P(every, None), P(dp_axes)
    table, glu, glu_down = P(None, dp_axes), P(dp_axes, "x"), P("x", dp_axes)
    return jax.shard_map(
        per_device,
        mesh=grid,
        in_specs=(
            row, P(), mat, mat, mat, mat, gain, gain, table, glu, glu, glu_down, gain, row,
        ),
        out_specs=(
            row, row, mat, mat, mat, mat, gain, gain, table, glu, glu, glu_down, gain,
        ),
        check_vma=False,
    )
```

```python
import functools

import jax
import jax.numpy as jnp
from jax import lax
from jax.experimental import pallas as pl
from jax.experimental.pallas import tpu as pltpu
from jax.sharding import Mesh, PartitionSpec as P

LAYER = 12
Z, C, X = 4, 2, 2
CHUNKS = Z * C
LANES = 128
epsilon = 1e-06
VMEM_LIMIT = 56 << 20
BF, F32 = jnp.bfloat16, jnp.float32


def swap(value, axis):
    return lax.ppermute(value, axis, [(0, 1), (1, 0)])


def dot(left, right):
    return jnp.dot(left, right, preferred_element_type=F32)


def contract_rows(left, right):
    return lax.dot_general(left, right, (((0,), (0,)), ((), ())), preferred_element_type=F32)


def times_transposed(left, right):
    return lax.dot_general(left, right, (((1,), (1,)), ((), ())), preferred_element_type=F32)


def mean_last(value):
    return jnp.mean(value, axis=-1, keepdims=True)


def inverse_rms(value):
    return lax.rsqrt(mean_last(value * value) + epsilon)


def sigmoid_slope(raw, sig):
    return sig * (1.0 + raw * (1.0 - sig))


class Copies:
    def __init__(self, inputs, outputs):
        self.inputs, self.outputs, self.waited, self.flushed = inputs, outputs, set(), set()
        for copy in inputs:
            copy.start()

    def wait(self, *numbers):
        for k in numbers:
            if k not in self.waited:
                self.waited.add(k)
                self.inputs[k].wait()

    def flush(self, *numbers):
        for k in numbers:
            if k not in self.flushed:
                self.flushed.add(k)
                self.outputs[k].start()


def call(kernel, outs, *ins, smem=0, scratch=(), late=None):
    n_in, n_out = len(ins) - smem, len(outs)

    def body(*refs):
        scalars, refs = refs[:smem], refs[smem:]
        far_in, far_out, refs = refs[:n_in], refs[n_in : n_in + n_out], refs[n_in + n_out :]
        near_in, near_out, refs = refs[:n_in], refs[n_in : n_in + n_out], refs[n_in + n_out :]
        *own, in_sems, out_sems = refs
        copies = Copies(
            [pltpu.make_async_copy(f, n, in_sems.at[k]) for k, (f, n) in enumerate(zip(far_in, near_in))],
            [pltpu.make_async_copy(n, f, out_sems.at[k]) for k, (f, n) in enumerate(zip(far_out, near_out))],
        )
        copies.wait(*range(n_in if late is None else late))
        kernel(*([] if late is None else [copies]), *scalars, *near_in, *near_out, *own)
        copies.wait(*range(n_in))
        copies.flush(*range(n_out))
        for copy in copies.outputs:
            copy.wait()

    shapes = [jax.ShapeDtypeStruct(s, t) for s, t in outs]
    near = [pltpu.VMEM(v.shape, v.dtype) for v in list(ins[smem:]) + shapes]
    return pl.pallas_call(
        body,
        out_shape=shapes,
        in_specs=[pl.BlockSpec(memory_space=pltpu.SMEM)] * smem + [pl.BlockSpec(memory_space=pl.ANY)] * n_in,
        out_specs=[pl.BlockSpec(memory_space=pl.ANY)] * n_out,
        scratch_shapes=near
        + list(scratch)
        + [pltpu.SemaphoreType.DMA((n_in,)), pltpu.SemaphoreType.DMA((n_out,))],
        compiler_params=pltpu.CompilerParams(vmem_limit_bytes=VMEM_LIMIT),
        cost_estimate=pl.CostEstimate(flops=0, bytes_accessed=1024, transcendentals=0),
    )(*ins)


def stat_block(columns, first=0):
    rows = columns[0].shape[0]
    lane = lax.broadcasted_iota(jnp.int32, (rows, LANES), 1) - first
    block = jnp.zeros((rows, LANES), F32)
    for k, column in enumerate(columns):
        high = column.astype(BF).astype(F32)
        block = jnp.where(lane == 2 * k, high, block)
        block = jnp.where(lane == 2 * k + 1, column - high, block)
    return block


def stat(block, k):
    lane = lax.broadcasted_iota(jnp.int32, block.shape, 1)
    picked = jnp.where((lane == 2 * k) | (lane == 2 * k + 1), block.astype(F32), 0.0)
    return jnp.sum(picked, axis=1, keepdims=True)


def reorder_kernel(back, y_ref, *refs):
    y = y_ref[0]
    half = len(refs) // 2
    for in_ref, out_ref in zip(refs[:half], refs[half:]):
        width = in_ref.shape[1] // CHUNKS
        for k in range(2):
            there = k + y - 2 * k * y
            for z in range(Z):
                near = slice((k * Z + z) * width, (k * Z + z + 1) * width)
                far = pl.ds(pl.multiple_of((z * 2 + there) * width, width), width)
                if back:
                    out_ref[:, far] = in_ref[:, near]
                else:
                    out_ref[:, near] = in_ref[:, far]


def token_piece_kernel(y_ref, tokens, gains, piece):
    width = tokens.shape[1]
    reorder_kernel(False, y_ref, tokens, piece.at[:, :width])
    row = lax.broadcasted_iota(jnp.int32, (tokens.shape[0], LANES), 0)
    block = jnp.zeros((tokens.shape[0], LANES), F32)
    for k in range(gains.shape[0]):
        block = jnp.where(row == k, gains[k : k + 1, :], block)
    piece[:, width:] = block.astype(BF)


def mixer_blocks_kernel(x_ref, *refs):
    *weights, out_ref = refs
    half = len(weights)
    x = x_ref[0]
    for z in range(Z):
        for c in range(C):
            for k in range(half):
                pieces = []
                for j in (k, half + k):
                    at = ((z * 2 + j % 2) * C + c) * LANES
                    pieces.append(weights[j // 2][:, at : at + LANES])
                out_ref[z * C + c, :, k * LANES : (k + 1) * LANES] = jnp.where(x == 0, *pieces)


def mixer_sums_kernel(at_ref, *refs):
    pieces, theirs, mine = refs[:4], refs[4], refs[5:]
    z, c = at_ref[0], at_ref[1]
    sub = theirs.shape[1]
    for k in range(Z):
        bits = [(z // 2 + k // 2) % 2, (z + k) % 2]
        for other in range(2):
            core = c + other - 2 * c * other
            row = pl.ds(pl.multiple_of(((bits[0] * 2 + bits[1]) * 2 + core) * sub, sub), sub)
            total = pieces[0][row, :].astype(F32)
            for p in pieces[1:]:
                total = total + p[row, :].astype(F32)
            if other:
                theirs[k] = total.astype(BF)
            else:
                mine[k][0] = total.astype(BF)
                mine[k][1] = jnp.zeros(theirs.shape[1:], BF)


def mixer_grads_kernel(
    at_ref, mine, theirs, w_in, w_forget, w_gate, grad_in, grad_forget, grad_gate, along_ref
):
    x, z, c = at_ref[0], at_ref[1], at_ref[2]
    total = jnp.zeros((w_in.shape[0], 1), F32)
    for m, (w_ref, g_ref) in enumerate(((w_in, grad_in), (w_forget, grad_forget), (w_gate, grad_gate))):
        for k in range(Z):
            there = (z // 2 + k // 2) % 2 * 2 + (z + k) % 2
            for y in range(2):
                for other in range(2):
                    core = c + other - 2 * c * other
                    j = m * 2 + y
                    to = pl.ds(pl.multiple_of(((there * 2 + y) * C + core) * LANES, LANES), LANES)
                    at = j % 3 * LANES
                    piece = jnp.where(
                        x == j // 3,
                        mine[k * 2 + other, :, at : at + LANES],
                        theirs[k * 2 + other, :, at : at + LANES],
                    ).astype(F32)
                    g_ref[:, to] = piece
                    weight = w_ref[:, to].astype(F32)
                    total = total + jnp.sum(piece * weight, axis=1, keepdims=True)
    along_ref[...] = jnp.broadcast_to(total, along_ref.shape)


def glu_blocks_kernel(gate_ref, up_ref, down_ref, out_ref):
    block = down_ref.shape[0] // CHUNKS
    for s in range(CHUNKS):
        at = slice(s * block, (s + 1) * block)
        out_ref[s, :block] = gate_ref[:, at].astype(F32).T.astype(BF)
        out_ref[s, block : 2 * block] = up_ref[:, at].astype(F32).T.astype(BF)
        out_ref[s, 2 * block :] = down_ref[at, :]


def glu_grads_kernel(blocks_ref, w_gate, w_up, grad_gate, grad_up, grad_down, along_ref):
    block = blocks_ref.shape[1] // 3
    total = jnp.zeros((w_gate.shape[0], 1), F32)
    for s in range(CHUNKS):
        at = slice(s * block, (s + 1) * block)
        for m, (w_ref, g_ref) in enumerate(((w_gate, grad_gate), (w_up, grad_up))):
            piece = blocks_ref[s, m * block : (m + 1) * block].astype(F32).T
            g_ref[:, at] = piece
            total = total + jnp.sum(piece * w_ref[:, at].astype(F32), axis=1, keepdims=True)
        grad_down[at, :] = blocks_ref[s, 2 * block :].astype(F32)
    along_ref[...] = jnp.broadcast_to(total, along_ref.shape)


def columns_of(x_ref, parts, k, span):
    if parts == 1:
        return slice(0, span)
    return pl.ds(pl.multiple_of((k + x_ref[0] - 2 * k * x_ref[0]) * span, LANES), span)


def mixer_forward_kernel(parts, copies, x_ref, *refs):
    gain, tokens, bound, keep = refs[:4]
    weights = refs[4 : 4 + parts * parts]
    normed, raw, decay, local, through, edge, drive = refs[4 + parts * parts :]
    group, feats = raw.shape[0], bound.shape[1]
    width = gain.shape[1]
    rows = group // CHUNKS

    @pl.loop(0, group // 32)
    def _(i):
        at = pl.ds(i * 32, 32)
        value = tokens[at, :width].astype(F32)
        normed[at, :] = (value * inverse_rms(value) * gain[...]).astype(BF)

    copies.flush(0)
    copies.wait(*range(2, 4 + parts * parts))

    @pl.loop(0, 2)
    def _(i):
        at = pl.ds(i * (group // 2), group // 2)
        deep, span = width // parts, 3 * feats // parts
        for k in range(parts):
            total = None
            for d in range(parts):
                part = dot(normed[at, d * deep : (d + 1) * deep], weights[d * parts + k][...])
                total = part if total is None else total + part
            raw[at, columns_of(x_ref, parts, k, span)] = total

    copies.flush(1)
    count = feats // LANES

    @pl.loop(0, CHUNKS)
    def _(i):
        at = pl.ds(i * rows, rows)
        for j in range(count):
            lanes = slice(j * LANES, (j + 1) * LANES)
            inner = raw[at, lanes]
            forget_raw = raw[at, feats + j * LANES : feats + (j + 1) * LANES]
            low = bound[:, lanes]
            forget = low + (1.0 - low) * jax.nn.sigmoid(forget_raw)
            drive[j, at, :] = inner * jax.nn.sigmoid(inner) * (1.0 - forget)
            decay[j, at, :] = forget * keep[at, :]

    copies.flush(2)

    def step(t, carry):
        out = []
        at = pl.ds(t, CHUNKS, stride=rows)
        for j in range(count):
            state, passed = carry[2 * j], carry[2 * j + 1]
            here = decay[j, at, :]
            state = here * state + drive[j, at, :]
            passed = here * passed
            local[j, at, :] = state
            through[j, at, :] = passed
            out += [state, passed]
        return tuple(out)

    zero, one = jnp.zeros((CHUNKS, LANES), F32), jnp.ones((CHUNKS, LANES), F32)
    last = lax.fori_loop(0, rows, step, (zero, one) * count, unroll=8)
    for j in range(count):
        edge[:CHUNKS, j * LANES : (j + 1) * LANES] = last[2 * j + 1]
        edge[CHUNKS:, j * LANES : (j + 1) * LANES] = last[2 * j]


def entries(order, backwards, count, passed, last, entry):
    def step(n, running):
        row = pl.ds(order[count - 1 - n if backwards else n], 1)
        entry[row, :] = running
        return passed[row, :] * running + last[row, :]

    lax.fori_loop(0, count, step, jnp.zeros((1, last.shape[1]), F32))


def collect(parties, at, to):
    base = 0
    for p in parties:
        for g in range(p.shape[0] // (at[1] * CHUNKS)):
            begin = (g * at[1] + at[0]) * CHUNKS
            to[base : base + CHUNKS, :] = p[begin : begin + CHUNKS, :]
            base += CHUNKS


def mixer_out_kernel(parties, count, copies, order, *refs):
    edges = refs[:parties]
    local, through, raw, mix_gain, out_w = refs[parties : parties + 5]
    states, entry_own, partial, passed, last, entry, mixed = refs[parties + 5 :]
    group, feats = raw.shape[0], mix_gain.shape[1]
    width = out_w.shape[1]
    rows = group // CHUNKS
    collect(edges, (0, 2), passed)
    collect(edges, (1, 2), last)
    entries(order, False, count, passed, last, entry)
    base = order[count]
    entry_own[...] = entry[pl.ds(pl.multiple_of(base, CHUNKS), CHUNKS), :]
    copies.wait(*range(parties, parties + 4))
    for s in range(CHUNKS):
        at = slice(s * rows, (s + 1) * rows)
        total = jnp.zeros((rows, LANES), F32)
        for j in range(feats // LANES):
            lanes = slice(j * LANES, (j + 1) * LANES)
            state = local[j, at, :] + through[j, at, :] * entry_own[s : s + 1, lanes]
            gate = raw[at, 2 * feats + j * LANES : 2 * feats + (j + 1) * LANES]
            mixed[at, lanes] = (state * (mix_gain[:, lanes] * (gate * jax.nn.sigmoid(gate)))).astype(BF)
            states[j, at, :] = state
            total = total + state * state
        squares = jnp.sum(total, axis=1, keepdims=True)
        partial[at, width:] = stat_block([squares], 2 * order[count + 1]).astype(BF)
    copies.flush(0)
    copies.wait(parties + 4)
    for k in range(2):
        at = slice(k * group // 2, (k + 1) * group // 2)
        partial[at, :width] = dot(mixed[at, :], out_w[...]).astype(BF)


STEP = 16


def resid_kernel(summed, tokens, gain, resid, hidden, scale):
    width = tokens.shape[1]

    @pl.loop(0, tokens.shape[0] // STEP)
    def _(i):
        at = pl.ds(i * STEP, STEP)
        squares = jnp.sum(summed[at, width:].astype(F32), axis=1, keepdims=True)
        q = lax.rsqrt(squares / width + epsilon)
        value = tokens[at, :].astype(F32) + q * summed[at, :width].astype(F32)
        resid[at, :] = value
        hidden[at, :] = (value * inverse_rms(value) * gain[...]).astype(BF)
        scale[at, :] = jnp.broadcast_to(q, (STEP, LANES))


def glu_kernel(copies, hidden, grad, *refs):
    weights, outs, partial, total = refs[:4], refs[4:10], refs[10], refs[11]
    group, block = outs[0].shape
    width = hidden.shape[1]
    for k in range(2):
        gate_up, down = weights[k], weights[2 + k]
        act, d_gate, d_up = outs[3 * k : 3 * k + 3]
        w_gate, w_up = gate_up.at[:block, :], gate_up.at[block:, :]
        copies.wait(0, 2 + k)
        for i in range(2):
            at = slice(i * group // 2, (i + 1) * group // 2)
            gate = times_transposed(hidden[at, :], w_gate[...])
            up = times_transposed(hidden[at, :], w_up[...])
            copies.wait(1, 4 + k)
            d_act = times_transposed(grad[at, :], down[...])
            sig = jax.nn.sigmoid(gate)
            silu = gate * sig
            act[at, :] = (silu * up).astype(BF)
            d_gate[at, :] = (d_act * up * sigmoid_slope(gate, sig)).astype(BF)
            d_up[at, :] = (d_act * silu).astype(BF)
            back = dot(d_gate[at, :], w_gate[...]) + dot(d_up[at, :], w_up[...])
            for cols, value in ((slice(0, width), back), (slice(width, None), dot(act[at, :], down[...]))):
                if k == 0:
                    total[at, cols] = value
                else:
                    partial[at, cols] = (total[at, cols] + value).astype(BF)
        copies.flush(3 * k, 3 * k + 1, 3 * k + 2)


def glu_weights_kernel(parts, terms, *refs):
    count = len(terms)
    lefts, rights, outs = refs[: 2 * count], refs[2 * count : 2 * count + max(terms) + 1], None
    outs = refs[2 * count + max(terms) + 1 :]
    block = lefts[0].shape[1]
    part = rights[0].shape[1] // parts
    cut = count * block // 2
    for k in range(2):
        for m, right in enumerate(terms):
            begin, end = m * block, (m + 1) * block
            for d in range(parts):
                value = contract_rows(lefts[k * count + m][...], rights[right][:, d * part : (d + 1) * part])
                value = value.astype(BF)
                if parts == 1:
                    outs[k][begin:end, :] = value
                    continue
                upper, lower = outs[k], outs[2 + d]
                if begin < cut:
                    upper[d, begin : min(end, cut)] = value[: min(end, cut) - begin]
                if end > cut:
                    lower[k, max(begin, cut) - cut : end - cut] = value[max(begin, cut) - begin :]


def first_sums_kernel(upper, upper_got, lower, lower_got, upper_keep, upper_send, lower_keep, lower_send):
    for mine, got, keep, send in (
        (upper, upper_got, upper_keep, upper_send),
        (lower, lower_got, lower_keep, lower_send),
    ):
        keep[...] = mine[0].astype(F32) + got[0].astype(F32)
        send[...] = (mine[1].astype(F32) + got[1].astype(F32)).astype(BF)


def last_sums_kernel(*refs):
    *pieces, blocks = refs
    begin = 0
    for mine, got in zip(pieces[::2], pieces[1::2]):
        for s in range(CHUNKS):
            cols = slice(s * LANES, (s + 1) * LANES)
            blocks[s, begin : begin + mine.shape[0]] = (mine[:, cols] + got[:, cols].astype(F32)).astype(BF)
        begin += mine.shape[0]


def d_resid_kernel(summed, resid, tokens, grad, gain, scale, d_resid, piece, result):
    width = tokens.shape[1]

    @pl.loop(0, tokens.shape[0] // STEP)
    def _(i):
        at = pl.ds(i * STEP, STEP)
        d_hidden = summed[at, :width].astype(F32) * gain[...]
        value = resid[at, :]
        inv = inverse_rms(value)
        hat = value * inv
        d_value = grad[at, :].astype(F32) + inv * (d_hidden - hat * mean_last(d_hidden * hat))
        d_resid[at, :] = d_value
        result[at, :] = (value + summed[at, width:].astype(F32)).astype(BF)
        low = d_value.astype(BF)
        piece[at, :width] = low
        mean = mean_last(low.astype(F32) * (value - tokens[at, :].astype(F32)))
        piece[at, width:] = stat_block([scale[at, :1], mean]).astype(BF)


def mixer_back_kernel(copies, d_mixed, out_w, raw, states, mix_gain, decay, *refs):
    mixed, d_gate_raw, local, after, first, d_mixin, d_states = refs
    width = out_w.shape[1]
    group, feats = raw.shape[0], mix_gain.shape[1]
    rows = group // CHUNKS
    count = feats // LANES
    for k in range(2):
        at = slice(k * group // 2, (k + 1) * group // 2)
        d_mixin[at, :] = times_transposed(d_mixed[at, :width], out_w[...])
    copies.wait(2, 3, 4, 5)
    for s in range(CHUNKS):
        at = slice(s * rows, (s + 1) * rows)
        stats = d_mixed[at, width:]
        q, mean = stat(stats, 0), stat(stats, 1)
        for j in range(count):
            lanes = slice(j * LANES, (j + 1) * LANES)
            hat = states[j, at, :] * q
            gate = raw[at, 2 * feats + j * LANES : 2 * feats + (j + 1) * LANES]
            sig = jax.nn.sigmoid(gate)
            silu = gate * sig
            gain = mix_gain[:, lanes]
            d = d_mixin[at, lanes] * gain
            mixed[at, lanes] = (hat * gain * silu).astype(BF)
            d_gate_raw[at, lanes] = (d * hat * sigmoid_slope(gate, sig)).astype(BF)
            d_states[j, at, :] = q * (d * silu - hat * mean)
    copies.flush(0, 1)

    def step(t, carry):
        out = []
        at = pl.ds(rows - 1 - t, CHUNKS, stride=rows)
        for j in range(count):
            coming, passed = carry[2 * j], carry[2 * j + 1]
            here = decay[j, at, :]
            adjoint = d_states[j, at, :] + coming
            local[j, at, :] = adjoint
            after[j, at, :] = passed
            out += [here * adjoint, here * passed]
        return tuple(out)

    zero, one = jnp.zeros((CHUNKS, LANES), F32), jnp.ones((CHUNKS, LANES), F32)
    last = lax.fori_loop(0, rows, step, (zero, one) * count, unroll=8)
    for j in range(count):
        first[:, j * LANES : (j + 1) * LANES] = last[2 * j]


def mixer_weights_kernel(parts, normed, *refs):
    d_raw, outs = refs[:parts], refs[parts:]
    deep = normed.shape[1] // parts
    for d in range(parts):
        for k in range(parts):
            outs[d * parts + k][...] = contract_rows(normed[:, d * deep : (d + 1) * deep], d_raw[k][...]).astype(BF)


def out_weights_kernel(y_ref, x_ref, mixed, d_mixed, *refs):
    *outs, full = refs
    y, x = y_ref[0], x_ref[0]
    width = full.shape[1]
    sub, part = mixed.shape[1] // 2, width // CHUNKS
    for k in range(2):
        row = pl.multiple_of((k + y - 2 * k * y) * sub, sub)
        full[...] = contract_rows(mixed[:, pl.ds(row, sub)], d_mixed[:, :width])
        for m in range(2):
            half = m + x - 2 * m * x
            for z in range(Z // 2):
                for there in range(2):
                    near = (there + y - 2 * there * y) * Z + half * (Z // 2) + z
                    at = pl.ds(pl.multiple_of(near * part, part), part)
                    to = (z * 2 + there) * part
                    outs[k * 2 + m][:, to : to + part] = full[:, at].astype(BF)


def d_mixer_kernel(parties, parts, count, copies, x_ref, order, *refs):
    edges, firsts = refs[:parties], refs[parties : 2 * parties]
    refs = refs[2 * parties :]
    local, after, states, entry_own, raw, keep_mask, bound, d_gate_raw = refs[:8]
    weights = refs[8 : 8 + parts * parts]
    refs = refs[8 + parts * parts :]
    d_parts, (d_bound, partial, passed, last, entry, d_raw) = refs[:parts], refs[parts:]
    group, feats = raw.shape[0], bound.shape[1]
    rows = group // CHUNKS
    collect(edges, (0, 2), passed)
    collect(firsts, (0, 1), last)
    entries(order, True, count, passed, last, entry)
    base = pl.multiple_of(order[count], CHUNKS)
    copies.wait(*range(2 * parties, 2 * parties + 8))
    top = lax.broadcasted_iota(jnp.int32, (rows, LANES), 0) == 0
    for j in range(feats // LANES):
        lanes = slice(j * LANES, (j + 1) * LANES)
        coming = entry[pl.ds(base, CHUNKS), lanes]
        low = bound[:, lanes]
        total = jnp.zeros((1, LANES), F32)
        for s in range(CHUNKS):
            at = slice(s * rows, (s + 1) * rows)
            adjoint = local[j, at, :] + after[j, at, :] * coming[s : s + 1, :]
            previous = jnp.where(top, entry_own[s : s + 1, lanes], pltpu.roll(states[j, at, :], 1, 0))
            inner = raw[at, lanes]
            sig_inner = jax.nn.sigmoid(inner)
            sig = jax.nn.sigmoid(raw[at, feats + j * LANES : feats + (j + 1) * LANES])
            open_part = (1.0 - low) * (1.0 - sig)
            d_forget = adjoint * (previous * keep_mask[at, :] - inner * sig_inner)
            d_inner = adjoint * open_part * sigmoid_slope(inner, sig_inner)
            d_raw[at, lanes] = d_inner.astype(BF)
            d_raw[at, feats + j * LANES : feats + (j + 1) * LANES] = (d_forget * open_part * sig).astype(BF)
            total = total + jnp.sum(d_forget * (1.0 - sig), axis=0, keepdims=True)
        d_bound[:, lanes] = total
    d_raw[:, 2 * feats :] = d_gate_raw[...]
    for k, d_part in enumerate(d_parts):
        d_part[...] = d_raw[:, columns_of(x_ref, parts, k, 3 * feats // parts)]
    copies.flush(*range(parts + 1))
    copies.wait(*range(2 * parties + 8, 2 * parties + 8 + parts * parts))
    deep = partial.shape[1] // parts
    for d in range(parts):
        for i in range(2):
            at = slice(i * group // 2, (i + 1) * group // 2)
            total = None
            for k, d_part in enumerate(d_parts):
                part = times_transposed(d_part[at, :], weights[d * parts + k][...])
                total = part if total is None else total + part
            partial[at, d * deep : (d + 1) * deep] = total.astype(BF)


def token_grad_kernel(summed, tokens, d_resid, gain, out):
    @pl.loop(0, tokens.shape[0] // STEP)
    def _(i):
        at = pl.ds(i * STEP, STEP)
        value = tokens[at, :].astype(F32)
        inv = inverse_rms(value)
        hat = value * inv
        d = summed[at, :].astype(F32) * gain[...]
        out[at, :] = d_resid[at, :] + inv * (d - hat * mean_last(d * hat))


def after(value, *others):
    return lax.optimization_barrier((value, *others))[0]


def gather_rows(own):
    return lax.all_gather(own, ("z", "c"), axis=0, tiled=True)


def scatter_rows(partial):
    return lax.psum_scatter(partial, ("z", "c"), scatter_dimension=0, tiled=True)


def per_device(
    tokens, lengths, w_in, w_forget, w_gate, w_out, attn_gain, mix_gain, bound_table,
    ff_gate, ff_up, ff_down, mlp_gain, out_grad,
):
    Y = lax.axis_size("y")
    pair = Y == 2
    parts = 2 if pair else 1
    z, y, c, x = (lax.axis_index(a) for a in "zycx")
    rows, width = tokens.shape
    sub = w_in.shape[0]
    feats = Y * sub
    block = ff_gate.shape[1] // CHUNKS
    tall = 3 * block
    group = rows * CHUNKS
    near_y = y[None].astype(jnp.int32)

    def y_first(*values):
        if pair:
            return call(
                functools.partial(reorder_kernel, False),
                [(v.shape, v.dtype) for v in values], near_y, *values, smem=1,
            )
        return [
            v.reshape(v.shape[0], Z, Y, C * sub).transpose(0, 2, 1, 3).reshape(v.shape) for v in values
        ]

    def z_first(*values):
        if pair:
            return call(
                functools.partial(reorder_kernel, True),
                [(v.shape, v.dtype) for v in values], near_y, *values, smem=1,
            )
        return [
            v.reshape(v.shape[0], Y, Z, C * sub).transpose(0, 2, 1, 3).reshape(v.shape) for v in values
        ]

    def over_y(value):
        if pair:
            return [value, swap(value, "y")]
        return [lax.all_gather(value, "y", axis=0, tiled=True)]

    def in_order(value):
        if pair:
            other = swap(value, "y")
            return jnp.concatenate(
                [jnp.where(y == 0, value, other), jnp.where(y == 0, other, value)], axis=0
            )
        return lax.all_gather(value, "y", axis=0, tiled=True)

    def spread(value):
        return lax.all_to_all(value, ("z", "c"), 0, 0, tiled=True)

    def both(own, sent, axis):
        return own.astype(BF).astype(F32) + swap(sent.astype(BF), axis).astype(F32)

    near_x = x[None].astype(jnp.int32)
    z_c = jnp.stack([z, c]).astype(jnp.int32)

    def own_and_neighbours(value):
        corner = lax.ppermute(value, ("y", "x"), [(i, 3 - i) for i in range(4)])
        return [value, swap(value, "x"), swap(value, "y"), corner]

    table_f = bound_table.astype(F32)
    soft = jax.nn.softmax(table_f, axis=0)
    own_bound = jnp.sum(soft[1 : LAYER + 1], axis=0)

    if pair:
        (glu,) = call(glu_blocks_kernel, [((CHUNKS, tall, sub), BF)], ff_gate, ff_up, ff_down)
    else:
        glu = jnp.concatenate([w.T.reshape(CHUNKS, block, sub) for w in (ff_gate, ff_up)], axis=1)
        glu = jnp.concatenate([glu, ff_down.reshape(CHUNKS, block, sub)], axis=1)
    (out_rows,) = y_first(in_order(w_out))

    tokens_y, grad_y = y_first(tokens, out_grad)
    if pair:
        (blocks,) = call(
            mixer_blocks_kernel, [((CHUNKS, sub, 3 * feats // 2), BF)], near_x, w_in, w_forget, w_gate, smem=1
        )
        moved = after(spread(blocks), glu, out_rows)
        small = jnp.stack([attn_gain.astype(F32), mlp_gain.astype(F32), own_bound, mix_gain.astype(F32)])
        small = [small, swap(small, "y")]
        (piece,) = call(
            token_piece_kernel, [((rows, width + LANES), BF)],
            near_y, tokens, jnp.concatenate([v[:2] for v in small]), smem=1,
        )
        tokens_all = gather_rows(after(piece, moved))
        gains = tokens_all.reshape(CHUNKS, rows, -1)[:, :4, width:].astype(F32)
        attn_g, mlp_g = (
            jnp.concatenate([gains[:, k].reshape(1, -1), gains[:, 2 + k].reshape(1, -1)], axis=1) for k in range(2)
        )
        small = jnp.stack([v[2:] for v in small])
        small = jnp.where(y == 0, small, small[::-1])
        mixer = own_and_neighbours(moved.reshape(CHUNKS * sub, 3 * feats // 2))
    else:
        gains = lax.all_gather(jnp.stack([attn_gain, mlp_gain]), ("z", "y", "c"), axis=1, tiled=True)
        attn_g, mlp_g = y_first(gains[:1].astype(F32), gains[1:].astype(F32))
        tokens_all = gather_rows(tokens_y)
        small = in_order(jnp.stack([own_bound, mix_gain.astype(F32)])[None])
        mixer = [
            w.reshape(sub, Z, Y, C, sub).transpose(1, 3, 0, 2, 4).reshape(CHUNKS, sub, feats)
            for w in (w_in, w_forget, w_gate)
        ]
        moved = spread(jnp.concatenate(mixer, axis=2))
        mixer = over_y(moved.reshape(CHUNKS * sub, 3 * feats))
    glu = spread(after(glu, moved))
    bound = small[:, 0].reshape(1, feats)
    mix_g = small[:, 1].reshape(1, feats)

    slot = jnp.arange(lengths.shape[0])
    starts = jnp.sum(jnp.where(slot[None, :] < slot[:, None], lengths[None, :], 0), axis=1)
    slot = jnp.arange(CHUNKS)
    chunk = (slot // C * Y + y) * (C * X) + slot % C * X + x
    position = (chunk[:, None] * rows + jnp.arange(rows)[None, :]).reshape(group)
    keep = 1.0 - jnp.any(position[:, None] == starts[None, :], axis=1).astype(F32)[:, None]
    count = Z * Y * C * X
    number = jnp.arange(count)
    xn, cn = number % X, number // X % C
    yn, zn = number // (X * C) % Y, number // (X * C * Y)
    party = (yn ^ y) * X + (xn ^ x) if pair else yn * X + xn
    order = party * CHUNKS + zn * C + cn
    base = 0 * y if pair else (y * X + x) * CHUNKS
    order = jnp.concatenate([order, jnp.stack([base, z * C + c])]).astype(jnp.int32)

    def parties(value):
        if pair:
            return own_and_neighbours(value)
        return [lax.all_gather(value, ("y", "x"), axis=0, tiled=True)]

    crowd = 4 if pair else 1
    featured = ((feats // LANES, group, LANES), F32)
    normed, raw, decay, local, through, edge = call(
        functools.partial(mixer_forward_kernel, parts),
        [((group, width), BF), ((group, 3 * feats), F32)] + [featured] * 3 + [((2 * CHUNKS, feats), F32)],
        near_x, attn_g, tokens_all, bound, keep, *mixer,
        smem=1, scratch=[pltpu.VMEM(*featured)], late=2,
    )
    edges = parties(edge)
    def assemble(pieces):
        return jnp.concatenate([p.transpose(1, 0, 2).reshape(p.shape[1], -1) for p in pieces], axis=1)

    def around(blocks):
        cut = blocks.shape[1] // 2
        side, up_y = swap(blocks, "x"), swap(blocks, "y")
        corner = [swap(up_y[:, :cut], "x"), swap(side[:, cut:], "y")]
        near, far = assemble([blocks, up_y]), assemble([side, jnp.concatenate(corner, axis=1)])
        return [near, far], (side, up_y), corner

    early, late, last = (), (), ()
    gate_up, down = glu[:, : 2 * block], glu[:, 2 * block :]
    if pair:
        gate_up_w, early, _ = around(after(gate_up, edges[0]))
        down_w, late, last = around(after(down, *early))
    else:
        gate_up_w, down_w = (assemble(over_y(v)) for v in (gate_up, down))
        gate_up_w, down_w = ([v, swap(v, "x")] for v in (gate_up_w, down_w))
    carries = [pltpu.VMEM((Y * X * CHUNKS, feats), F32)] * 3
    states, entry, partial = call(
        functools.partial(mixer_out_kernel, crowd, count),
        [featured, ((CHUNKS, feats), F32), ((group, width + LANES), BF)],
        order, *edges, local, through, raw, mix_g, out_rows,
        smem=1, scratch=carries + [pltpu.VMEM((group, feats), BF)], late=crowd,
    )
    summed = scatter_rows(after(partial, glu))
    own_grad = lax.all_to_all(jnp.broadcast_to(after(grad_y, glu)[None], (Z, rows, width)), "z", 0, 0, tiled=False)
    other_grad = swap(own_grad, "c")
    grad_all = jnp.where(
        c == 0, jnp.stack([own_grad, other_grad], axis=1), jnp.stack([other_grad, own_grad], axis=1)
    ).reshape(group, width)
    resid, hidden, scale = call(
        resid_kernel,
        [((rows, width), F32), ((rows, width), BF), ((rows, LANES), F32)],
        after(summed, own_grad, *early, *late), tokens_y, mlp_g,
    )
    hidden_all = after(gather_rows(hidden), grad_all)
    thin = ((group, block), BF)
    act0, d_gate0, d_up0, act1, d_gate1, d_up1, partial = call(
        glu_kernel, [thin] * 6 + [((group, 2 * width), BF)],
        hidden_all, grad_all, *gate_up_w, *down_w, late=0, scratch=[pltpu.VMEM((group, 2 * width), F32)],
    )
    acts = [act0, act1]

    def weight_pieces(terms, lefts, *rights):
        height = len(terms) * block
        shapes = [((height, width), BF)] * 2
        if pair:
            shapes = [((2, height // 2, width // 2), BF)] * 4
        return call(
            functools.partial(glu_weights_kernel, parts, terms), shapes, *lefts, *rights,
        )

    def first_swaps(pieces):
        upper, upper_sent, lower, lower_sent = pieces
        return upper, swap(upper_sent, "x"), lower, swap(lower_sent, "y")

    def first_sums(pieces):
        height = pieces[0].shape[1]
        shapes = [((height, width // 2), F32), ((height, width // 2), BF)] * 2
        return call(first_sums_kernel, shapes, *pieces)

    def last_swaps(pieces):
        upper, upper_sent, lower, lower_sent = pieces
        return upper, swap(upper_sent, "y"), lower, swap(lower_sent, "x")

    def last_sums(*pieces):
        height = sum(p.shape[0] for p in pieces[::2])
        return call(last_sums_kernel, [((CHUNKS, height, sub), BF)], *pieces)[0]

    def to_blocks(value):
        return value.reshape(value.shape[0], -1, sub).transpose(1, 0, 2)

    def total_blocks(pieces):
        blocks = to_blocks(both(*pieces, "x").astype(BF))
        return lax.psum_scatter(blocks, "y", scatter_dimension=0, tiled=True)

    summed = scatter_rows(partial)
    gate_up = weight_pieces((0, 0), [d_gate0, d_up0, d_gate1, d_up1], hidden_all)
    down = weight_pieces((0,), acts, grad_all)
    if pair:
        gate_up = first_sums(first_swaps(gate_up))
        down = first_swaps(down)
        summed, *gate_up = lax.optimization_barrier((summed, *gate_up))
        summed, *down = lax.optimization_barrier((summed, *down))
    d_resid, piece, result_y = call(
        d_resid_kernel, [((rows, width), F32), ((rows, width + LANES), BF), ((rows, width), BF)],
        summed, resid, tokens_y, grad_y, mlp_g, scale,
    )
    d_mixed = gather_rows(piece)
    if pair:
        gate_up = last_swaps(gate_up)
        down = last_swaps(first_sums(down))
        d_mixed, *gate_up = lax.optimization_barrier((d_mixed, *gate_up))
        d_mixed, *down = lax.optimization_barrier((d_mixed, *down))

    mixed_in, d_gate_raw, adjoint, passed, first = call(
        mixer_back_kernel,
        [((group, feats), BF)] * 2 + [featured] * 2 + [((CHUNKS, feats), F32)],
        d_mixed, out_rows, raw, states, mix_g, decay,
        scratch=[pltpu.VMEM((group, feats), F32), pltpu.VMEM(*featured)], late=2,
    )
    firsts = parties(first)
    if pair:
        glu_grad = last_sums(*after((*gate_up, *down), first))
    else:
        glu_grad = jnp.concatenate([total_blocks(gate_up), total_blocks(down)], axis=1)
    raw = after(raw, glu_grad)
    glu_grad = spread(glu_grad)
    *d_raw, part_bound, partial = call(
        functools.partial(d_mixer_kernel, crowd, parts, count),
        [((group, 3 * feats // parts), BF)] * parts
        + [((1, feats), F32), ((group, width), BF)],
        near_x, order, *edges, *firsts, adjoint, passed, states, entry, raw, keep, bound, d_gate_raw, *mixer,
        smem=2, scratch=carries + [pltpu.VMEM((group, 3 * feats), BF)], late=2 * crowd,
    )

    (token_grad_y,) = call(
        token_grad_kernel, [((rows, width), F32)],
        scatter_rows(partial), tokens_y, d_resid, attn_g,
    )
    result, token_grad = z_first(result_y, token_grad_y)

    pieces = call(
        functools.partial(mixer_weights_kernel, parts),
        [((width // parts, 3 * feats // parts), BF)] * parts**2,
        normed, *d_raw,
    )
    part_bound = part_bound.reshape(feats)
    if pair:
        pieces = [
            pieces[0],
            swap(pieces[1], "x"),
            swap(pieces[2], "y"),
            lax.ppermute(pieces[3], ("y", "x"), [(i, 3 - i) for i in range(4)]),
        ]
        top, bottom = jnp.split(part_bound, 2)
        d_bound = jnp.where(y == 0, top, bottom) + swap(jnp.where(y == 0, bottom, top), "y")
        out_pieces = call(
            out_weights_kernel, [((sub, width // 2), BF)] * 4,
            near_y, near_x, after(mixed_in, *d_raw), d_mixed, smem=2, scratch=[pltpu.VMEM((sub, width), F32)],
        )
        pieces = after(pieces, *out_pieces, d_bound)
        shape = (2, sub, 3 * feats // 2)
        theirs, *mine = call(
            mixer_sums_kernel, [((Z, *shape[1:]), BF)] + [(shape, BF)] * Z, z_c, *pieces, smem=1
        )
        out_pieces = after(out_pieces, theirs)
        got = swap(theirs, "c")
        mine = [v.at[1].set(got[k]) for k, v in enumerate(mine)]
        mixer_grad = [mine[0]] + [lax.ppermute(mine[k], "z", [(i, i ^ k) for i in range(Z)]) for k in range(1, Z)]
        mixer_grad = jnp.concatenate(mixer_grad, axis=0)
    else:
        d_bound = lax.psum_scatter(part_bound, "y", scatter_dimension=0, tiled=True)
        mixer_grad = lax.psum_scatter(pieces[0], "y", scatter_dimension=0, tiled=True)
        mixer_grad = both(mixer_grad, mixer_grad, "x").astype(BF)
        mixer_grad = spread(mixer_grad.reshape(CHUNKS, sub, 3 * feats))
    d_bound = d_bound + swap(d_bound, "x")
    row_ids = jnp.arange(bound_table.shape[0])[:, None]
    member = jnp.logical_and(row_ids >= 1, row_ids <= LAYER).astype(F32)
    grad_table = soft * (member - own_bound[None, :]) * d_bound[None, :]

    if pair:
        grad_out = sum(
            p.astype(F32)
            for p in (
                out_pieces[0],
                swap(out_pieces[1], "x"),
                swap(out_pieces[2], "y"),
                lax.ppermute(out_pieces[3], ("y", "x"), [(i, 3 - i) for i in range(4)]),
            )
        ).astype(BF)
        grad_gate_ff, grad_up_ff, grad_down, along_ff = call(
            glu_grads_kernel,
            [((sub, CHUNKS * block), F32)] * 2 + [((CHUNKS * block, sub), F32), ((sub, LANES), F32)],
            glu_grad, ff_gate, ff_up,
        )
        grad_mlp = along_ff[:, 0]
        grad_mlp = grad_mlp + swap(grad_mlp, "x")
        mixer_grad = after(mixer_grad, grad_out, d_bound, grad_mlp)
        mixer_grad = [mixer_grad, swap(mixer_grad, "x")]
        other = swap(grad_out, "x")
        grad_out = jnp.concatenate(
            [jnp.where(x == 0, grad_out, other), jnp.where(x == 0, other, grad_out)], axis=1
        ).astype(F32)
    else:
        (grad_out,) = z_first(contract_rows(mixed_in, d_mixed[:, :width]).astype(BF))
        grad_out = lax.psum_scatter(grad_out, "y", scatter_dimension=0, tiled=True)
        grad_out = both(grad_out, grad_out, "x")

    def along(weight, grad):
        return jnp.sum(weight.astype(F32) * grad, axis=1)

    square = ((sub, width), F32)
    if pair:
        grad_in, grad_forget, grad_gate, grad_attn = call(
            mixer_grads_kernel, [square] * 3 + [((sub, LANES), F32)],
            jnp.concatenate([near_x, z_c]), *mixer_grad, w_in, w_forget, w_gate, smem=1,
        )
        grad_attn = grad_attn[:, 0]
    else:
        mixer_grad = mixer_grad.reshape(Z, C, sub, 3, Y, sub).transpose(3, 2, 0, 4, 1, 5)
        grad_in, grad_forget, grad_gate = mixer_grad.reshape(3, sub, width).astype(F32)
        grad_attn = along(w_in, grad_in) + along(w_forget, grad_forget) + along(w_gate, grad_gate)
        grad_gate_ff, grad_up_ff = (
            glu_grad[:, k * block : (k + 1) * block].astype(F32).reshape(CHUNKS * block, sub).T for k in range(2)
        )
        grad_down = glu_grad[:, 2 * block :].reshape(CHUNKS * block, sub).astype(F32)
        grad_mlp = along(ff_gate, grad_gate_ff) + along(ff_up, grad_up_ff)
        grad_mlp = grad_mlp + swap(grad_mlp, "x")
    grad_attn = grad_attn / attn_gain.astype(F32)
    grad_mix = along(w_out, grad_out) / mix_gain.astype(F32)
    grad_mlp = grad_mlp / mlp_gain.astype(F32)
    return (
        result, token_grad, grad_in, grad_forget, grad_gate, grad_out, grad_attn, grad_mix,
        grad_table, grad_gate_ff, grad_up_ff, grad_down, grad_mlp,
    )


def solution(mesh):
    dp, mp = mesh.devices.shape
    grid = Mesh(mesh.devices.reshape(Z, dp // CHUNKS, C, mp), ("z", "y", "c", "x"))
    dp_axes = ("z", "y", "c")
    every = ("z", "y", "c", "x")
    mat, row, gain = P(dp_axes, None), P(every, None), P(dp_axes)
    table, glu, glu_down = P(None, dp_axes), P(dp_axes, "x"), P("x", dp_axes)
    return jax.shard_map(
        per_device,
        mesh=grid,
        in_specs=(
            row, P(), mat, mat, mat, mat, gain, gain, table, glu, glu, glu_down, gain, row,
        ),
        out_specs=(
            row, row, mat, mat, mat, mat, gain, gain, table, glu, glu, glu_down, gain,
        ),
        check_vma=False,
    )
```

```python
import functools

import jax
import jax.numpy as jnp
from jax import lax
from jax.experimental import pallas as pl
from jax.experimental.pallas import tpu as pltpu
from jax.sharding import Mesh, PartitionSpec as P

LAYER = 12
Z, C, X = 4, 2, 2
CHUNKS = Z * C
LANES = 128
epsilon = 1e-06
VMEM_LIMIT = 56 << 20
BF, F32 = jnp.bfloat16, jnp.float32


def swap(value, axis):
    return lax.ppermute(value, axis, [(0, 1), (1, 0)])


def dot(left, right):
    return jnp.dot(left, right, preferred_element_type=F32)


def contract_rows(left, right):
    return lax.dot_general(left, right, (((0,), (0,)), ((), ())), preferred_element_type=F32)


def times_transposed(left, right):
    return lax.dot_general(left, right, (((1,), (1,)), ((), ())), preferred_element_type=F32)


def mean_last(value):
    return jnp.mean(value, axis=-1, keepdims=True)


def inverse_rms(value):
    return lax.rsqrt(mean_last(value * value) + epsilon)


def sigmoid_slope(raw, sig):
    return sig * (1.0 + raw * (1.0 - sig))


class Copies:
    def __init__(self, inputs, outputs):
        self.inputs, self.outputs, self.waited, self.flushed = inputs, outputs, set(), set()
        for copy in inputs:
            copy.start()

    def wait(self, *numbers):
        for k in numbers:
            if k not in self.waited:
                self.waited.add(k)
                self.inputs[k].wait()

    def flush(self, *numbers):
        for k in numbers:
            if k not in self.flushed:
                self.flushed.add(k)
                self.outputs[k].start()


def call(kernel, outs, *ins, smem=0, scratch=(), late=None):
    n_in, n_out = len(ins) - smem, len(outs)

    def body(*refs):
        scalars, refs = refs[:smem], refs[smem:]
        far_in, far_out, refs = refs[:n_in], refs[n_in : n_in + n_out], refs[n_in + n_out :]
        near_in, near_out, refs = refs[:n_in], refs[n_in : n_in + n_out], refs[n_in + n_out :]
        *own, in_sems, out_sems = refs
        copies = Copies(
            [pltpu.make_async_copy(f, n, in_sems.at[k]) for k, (f, n) in enumerate(zip(far_in, near_in))],
            [pltpu.make_async_copy(n, f, out_sems.at[k]) for k, (f, n) in enumerate(zip(far_out, near_out))],
        )
        copies.wait(*range(n_in if late is None else late))
        kernel(*([] if late is None else [copies]), *scalars, *near_in, *near_out, *own)
        copies.wait(*range(n_in))
        copies.flush(*range(n_out))
        for copy in copies.outputs:
            copy.wait()

    shapes = [jax.ShapeDtypeStruct(s, t) for s, t in outs]
    near = [pltpu.VMEM(v.shape, v.dtype) for v in list(ins[smem:]) + shapes]
    return pl.pallas_call(
        body,
        out_shape=shapes,
        in_specs=[pl.BlockSpec(memory_space=pltpu.SMEM)] * smem + [pl.BlockSpec(memory_space=pl.ANY)] * n_in,
        out_specs=[pl.BlockSpec(memory_space=pl.ANY)] * n_out,
        scratch_shapes=near
        + list(scratch)
        + [pltpu.SemaphoreType.DMA((n_in,)), pltpu.SemaphoreType.DMA((n_out,))],
        compiler_params=pltpu.CompilerParams(vmem_limit_bytes=VMEM_LIMIT),
        cost_estimate=pl.CostEstimate(flops=0, bytes_accessed=1024, transcendentals=0),
    )(*ins)


def stat_block(columns, first=0):
    rows = columns[0].shape[0]
    lane = lax.broadcasted_iota(jnp.int32, (rows, LANES), 1) - first
    block = jnp.zeros((rows, LANES), F32)
    for k, column in enumerate(columns):
        high = column.astype(BF).astype(F32)
        block = jnp.where(lane == 2 * k, high, block)
        block = jnp.where(lane == 2 * k + 1, column - high, block)
    return block


def stat(block, k):
    lane = lax.broadcasted_iota(jnp.int32, block.shape, 1)
    picked = jnp.where((lane == 2 * k) | (lane == 2 * k + 1), block.astype(F32), 0.0)
    return jnp.sum(picked, axis=1, keepdims=True)


def reorder_kernel(back, y_ref, *refs):
    y = y_ref[0]
    half = len(refs) // 2
    for in_ref, out_ref in zip(refs[:half], refs[half:]):
        width = in_ref.shape[1] // CHUNKS
        for k in range(2):
            there = k + y - 2 * k * y
            for z in range(Z):
                near = slice((k * Z + z) * width, (k * Z + z + 1) * width)
                far = pl.ds(pl.multiple_of((z * 2 + there) * width, width), width)
                if back:
                    out_ref[:, far] = in_ref[:, near]
                else:
                    out_ref[:, near] = in_ref[:, far]


def token_piece_kernel(y_ref, tokens, gains, piece):
    width = tokens.shape[1]
    reorder_kernel(False, y_ref, tokens, piece.at[:, :width])
    row = lax.broadcasted_iota(jnp.int32, (tokens.shape[0], LANES), 0)
    block = jnp.zeros((tokens.shape[0], LANES), F32)
    for k in range(gains.shape[0]):
        block = jnp.where(row == k, gains[k : k + 1, :], block)
    piece[:, width:] = block.astype(BF)


def mixer_blocks_kernel(x_ref, *refs):
    *weights, out_ref = refs
    half = len(weights)
    x = x_ref[0]
    for z in range(Z):
        for c in range(C):
            for k in range(half):
                pieces = []
                for j in (k, half + k):
                    at = ((z * 2 + j % 2) * C + c) * LANES
                    pieces.append(weights[j // 2][:, at : at + LANES])
                out_ref[z * C + c, :, k * LANES : (k + 1) * LANES] = jnp.where(x == 0, *pieces)


def mixer_sums_kernel(at_ref, *refs):
    pieces, theirs, mine = refs[:4], refs[4], refs[5:]
    z, c = at_ref[0], at_ref[1]
    sub = theirs.shape[1]
    for k in range(Z):
        bits = [(z // 2 + k // 2) % 2, (z + k) % 2]
        for other in range(2):
            core = c + other - 2 * c * other
            row = pl.ds(pl.multiple_of(((bits[0] * 2 + bits[1]) * 2 + core) * sub, sub), sub)
            total = pieces[0][row, :].astype(F32)
            for p in pieces[1:]:
                total = total + p[row, :].astype(F32)
            if other:
                theirs[k] = total.astype(BF)
            else:
                mine[k][0] = total.astype(BF)
                mine[k][1] = jnp.zeros(theirs.shape[1:], BF)


def mixer_grads_kernel(at_ref, *refs):
    mine, theirs, refs = refs[:Z], refs[Z : 2 * Z], refs[2 * Z :]
    w_in, w_forget, w_gate, grad_in, grad_forget, grad_gate, along_ref = refs
    x, z, c = at_ref[0], at_ref[1], at_ref[2]
    total = jnp.zeros((w_in.shape[0], 1), F32)
    for m, (w_ref, g_ref) in enumerate(((w_in, grad_in), (w_forget, grad_forget), (w_gate, grad_gate))):
        for k in range(Z):
            there = (z // 2 + k // 2) % 2 * 2 + (z + k) % 2
            for y in range(2):
                for other in range(2):
                    core = c + other - 2 * c * other
                    j = m * 2 + y
                    to = pl.ds(pl.multiple_of(((there * 2 + y) * C + core) * LANES, LANES), LANES)
                    at = j % 3 * LANES
                    piece = jnp.where(
                        x == j // 3,
                        mine[k][other, :, at : at + LANES],
                        theirs[k][other, :, at : at + LANES],
                    ).astype(F32)
                    g_ref[:, to] = piece
                    weight = w_ref[:, to].astype(F32)
                    total = total + jnp.sum(piece * weight, axis=1, keepdims=True)
    along_ref[...] = jnp.broadcast_to(total, along_ref.shape)


def glu_blocks_kernel(gate_ref, up_ref, down_ref, out_ref):
    block = down_ref.shape[0] // CHUNKS
    for s in range(CHUNKS):
        at = slice(s * block, (s + 1) * block)
        out_ref[s, :block] = gate_ref[:, at].astype(F32).T.astype(BF)
        out_ref[s, block : 2 * block] = up_ref[:, at].astype(F32).T.astype(BF)
        out_ref[s, 2 * block :] = down_ref[at, :]


def glu_grads_kernel(blocks_ref, w_gate, w_up, grad_gate, grad_up, grad_down, along_ref):
    block = blocks_ref.shape[1] // 3
    total = jnp.zeros((w_gate.shape[0], 1), F32)
    for s in range(CHUNKS):
        at = slice(s * block, (s + 1) * block)
        for m, (w_ref, g_ref) in enumerate(((w_gate, grad_gate), (w_up, grad_up))):
            piece = blocks_ref[s, m * block : (m + 1) * block].astype(F32).T
            g_ref[:, at] = piece
            total = total + jnp.sum(piece * w_ref[:, at].astype(F32), axis=1, keepdims=True)
        grad_down[at, :] = blocks_ref[s, 2 * block :].astype(F32)
    along_ref[...] = jnp.broadcast_to(total, along_ref.shape)


def columns_of(x_ref, parts, k, span):
    if parts == 1:
        return slice(0, span)
    return pl.ds(pl.multiple_of((k + x_ref[0] - 2 * k * x_ref[0]) * span, LANES), span)


def mixer_forward_kernel(parts, copies, x_ref, *refs):
    gain, tokens, bound, keep = refs[:4]
    weights = refs[4 : 4 + parts * parts]
    normed, raw, decay, local, through, edge, drive = refs[4 + parts * parts :]
    group, feats = raw.shape[0], bound.shape[1]
    width = gain.shape[1]
    rows = group // CHUNKS

    @pl.loop(0, group // 32)
    def _(i):
        at = pl.ds(i * 32, 32)
        value = tokens[at, :width].astype(F32)
        normed[at, :] = (value * inverse_rms(value) * gain[...]).astype(BF)

    copies.flush(0)
    copies.wait(*range(2, 4 + parts * parts))

    @pl.loop(0, 2)
    def _(i):
        at = pl.ds(i * (group // 2), group // 2)
        deep, span = width // parts, 3 * feats // parts
        for k in range(parts):
            total = None
            for d in range(parts):
                part = dot(normed[at, d * deep : (d + 1) * deep], weights[d * parts + k][...])
                total = part if total is None else total + part
            raw[at, columns_of(x_ref, parts, k, span)] = total

    copies.flush(1)
    count = feats // LANES

    @pl.loop(0, CHUNKS)
    def _(i):
        at = pl.ds(i * rows, rows)
        for j in range(count):
            lanes = slice(j * LANES, (j + 1) * LANES)
            inner = raw[at, lanes]
            forget_raw = raw[at, feats + j * LANES : feats + (j + 1) * LANES]
            low = bound[:, lanes]
            forget = low + (1.0 - low) * jax.nn.sigmoid(forget_raw)
            drive[j, at, :] = inner * jax.nn.sigmoid(inner) * (1.0 - forget)
            decay[j, at, :] = forget * keep[at, :]

    copies.flush(2)

    def step(t, carry):
        out = []
        at = pl.ds(t, CHUNKS, stride=rows)
        for j in range(count):
            state, passed = carry[2 * j], carry[2 * j + 1]
            here = decay[j, at, :]
            state = here * state + drive[j, at, :]
            passed = here * passed
            local[j, at, :] = state
            through[j, at, :] = passed
            out += [state, passed]
        return tuple(out)

    zero, one = jnp.zeros((CHUNKS, LANES), F32), jnp.ones((CHUNKS, LANES), F32)
    last = lax.fori_loop(0, rows, step, (zero, one) * count, unroll=8)
    for j in range(count):
        edge[:CHUNKS, j * LANES : (j + 1) * LANES] = last[2 * j + 1]
        edge[CHUNKS:, j * LANES : (j + 1) * LANES] = last[2 * j]


def entries(order, backwards, count, passed, last, entry):
    def step(n, running):
        row = pl.ds(order[count - 1 - n if backwards else n], 1)
        entry[row, :] = running
        return passed[row, :] * running + last[row, :]

    lax.fori_loop(0, count, step, jnp.zeros((1, last.shape[1]), F32))


def collect(parties, at, to):
    base = 0
    for p in parties:
        for g in range(p.shape[0] // (at[1] * CHUNKS)):
            begin = (g * at[1] + at[0]) * CHUNKS
            to[base : base + CHUNKS, :] = p[begin : begin + CHUNKS, :]
            base += CHUNKS


def mixer_out_kernel(parties, count, copies, order, *refs):
    edges = refs[:parties]
    local, through, raw, mix_gain, out_w = refs[parties : parties + 5]
    states, entry_own, partial, passed, last, entry, mixed = refs[parties + 5 :]
    group, feats = raw.shape[0], mix_gain.shape[1]
    width = out_w.shape[1]
    rows = group // CHUNKS
    collect(edges, (0, 2), passed)
    collect(edges, (1, 2), last)
    entries(order, False, count, passed, last, entry)
    base = order[count]
    entry_own[...] = entry[pl.ds(pl.multiple_of(base, CHUNKS), CHUNKS), :]
    copies.wait(*range(parties, parties + 4))
    for s in range(CHUNKS):
        at = slice(s * rows, (s + 1) * rows)
        total = jnp.zeros((rows, LANES), F32)
        for j in range(feats // LANES):
            lanes = slice(j * LANES, (j + 1) * LANES)
            state = local[j, at, :] + through[j, at, :] * entry_own[s : s + 1, lanes]
            gate = raw[at, 2 * feats + j * LANES : 2 * feats + (j + 1) * LANES]
            mixed[at, lanes] = (state * (mix_gain[:, lanes] * (gate * jax.nn.sigmoid(gate)))).astype(BF)
            states[j, at, :] = state
            total = total + state * state
        squares = jnp.sum(total, axis=1, keepdims=True)
        partial[at, width:] = stat_block([squares], 2 * order[count + 1]).astype(BF)
    copies.flush(0)
    copies.wait(parties + 4)
    for k in range(2):
        at = slice(k * group // 2, (k + 1) * group // 2)
        partial[at, :width] = dot(mixed[at, :], out_w[...]).astype(BF)


STEP = 16


def resid_kernel(summed, tokens, gain, resid, hidden, scale):
    width = tokens.shape[1]

    @pl.loop(0, tokens.shape[0] // STEP)
    def _(i):
        at = pl.ds(i * STEP, STEP)
        squares = jnp.sum(summed[at, width:].astype(F32), axis=1, keepdims=True)
        q = lax.rsqrt(squares / width + epsilon)
        value = tokens[at, :].astype(F32) + q * summed[at, :width].astype(F32)
        resid[at, :] = value
        hidden[at, :] = (value * inverse_rms(value) * gain[...]).astype(BF)
        scale[at, :] = jnp.broadcast_to(q, (STEP, LANES))


def glu_kernel(copies, hidden, grad, *refs):
    weights, outs, partial, total = refs[:4], refs[4:10], refs[10], refs[11]
    group, block = outs[0].shape
    width = hidden.shape[1]
    for k in range(2):
        gate_up, down = weights[k], weights[2 + k]
        act, d_gate, d_up = outs[3 * k : 3 * k + 3]
        w_gate, w_up = gate_up.at[:block, :], gate_up.at[block:, :]
        copies.wait(0, 2 + k)
        for i in range(2):
            at = slice(i * group // 2, (i + 1) * group // 2)
            gate = times_transposed(hidden[at, :], w_gate[...])
            up = times_transposed(hidden[at, :], w_up[...])
            copies.wait(1, 4 + k)
            d_act = times_transposed(grad[at, :], down[...])
            sig = jax.nn.sigmoid(gate)
            silu = gate * sig
            act[at, :] = (silu * up).astype(BF)
            d_gate[at, :] = (d_act * up * sigmoid_slope(gate, sig)).astype(BF)
            d_up[at, :] = (d_act * silu).astype(BF)
            back = dot(d_gate[at, :], w_gate[...]) + dot(d_up[at, :], w_up[...])
            for cols, value in ((slice(0, width), back), (slice(width, None), dot(act[at, :], down[...]))):
                if k == 0:
                    total[at, cols] = value
                else:
                    partial[at, cols] = (total[at, cols] + value).astype(BF)
        copies.flush(3 * k, 3 * k + 1, 3 * k + 2)


def glu_weights_kernel(parts, terms, *refs):
    count = len(terms)
    lefts, rights, outs = refs[: 2 * count], refs[2 * count : 2 * count + max(terms) + 1], None
    outs = refs[2 * count + max(terms) + 1 :]
    block = lefts[0].shape[1]
    part = rights[0].shape[1] // parts
    cut = count * block // 2
    for k in range(2):
        for m, right in enumerate(terms):
            begin, end = m * block, (m + 1) * block
            for d in range(parts):
                value = contract_rows(lefts[k * count + m][...], rights[right][:, d * part : (d + 1) * part])
                value = value.astype(BF)
                if parts == 1:
                    outs[k][begin:end, :] = value
                    continue
                upper, lower = outs[k], outs[2 + d]
                if begin < cut:
                    upper[d, begin : min(end, cut)] = value[: min(end, cut) - begin]
                if end > cut:
                    lower[k, max(begin, cut) - cut : end - cut] = value[max(begin, cut) - begin :]


def first_sums_kernel(upper, upper_got, lower, lower_got, upper_keep, upper_send, lower_keep, lower_send):
    for mine, got, keep, send in (
        (upper, upper_got, upper_keep, upper_send),
        (lower, lower_got, lower_keep, lower_send),
    ):
        keep[...] = mine[0].astype(F32) + got[0].astype(F32)
        send[...] = (mine[1].astype(F32) + got[1].astype(F32)).astype(BF)


def last_sums_kernel(*refs):
    *pieces, blocks = refs
    begin = 0
    for mine, got in zip(pieces[::2], pieces[1::2]):
        for s in range(CHUNKS):
            cols = slice(s * LANES, (s + 1) * LANES)
            blocks[s, begin : begin + mine.shape[0]] = (mine[:, cols] + got[:, cols].astype(F32)).astype(BF)
        begin += mine.shape[0]


def d_resid_kernel(summed, resid, tokens, grad, gain, scale, d_resid, piece, result):
    width = tokens.shape[1]

    @pl.loop(0, tokens.shape[0] // STEP)
    def _(i):
        at = pl.ds(i * STEP, STEP)
        d_hidden = summed[at, :width].astype(F32) * gain[...]
        value = resid[at, :]
        inv = inverse_rms(value)
        hat = value * inv
        d_value = grad[at, :].astype(F32) + inv * (d_hidden - hat * mean_last(d_hidden * hat))
        d_resid[at, :] = d_value
        result[at, :] = (value + summed[at, width:].astype(F32)).astype(BF)
        low = d_value.astype(BF)
        piece[at, :width] = low
        mean = mean_last(low.astype(F32) * (value - tokens[at, :].astype(F32)))
        piece[at, width:] = stat_block([scale[at, :1], mean]).astype(BF)


def mixer_back_kernel(copies, d_mixed, out_w, raw, states, mix_gain, decay, *refs):
    mixed, d_gate_raw, local, after, first, d_mixin, d_states = refs
    width = out_w.shape[1]
    group, feats = raw.shape[0], mix_gain.shape[1]
    rows = group // CHUNKS
    count = feats // LANES
    for k in range(2):
        at = slice(k * group // 2, (k + 1) * group // 2)
        d_mixin[at, :] = times_transposed(d_mixed[at, :width], out_w[...])
    copies.wait(2, 3, 4, 5)
    for s in range(CHUNKS):
        at = slice(s * rows, (s + 1) * rows)
        stats = d_mixed[at, width:]
        q, mean = stat(stats, 0), stat(stats, 1)
        for j in range(count):
            lanes = slice(j * LANES, (j + 1) * LANES)
            hat = states[j, at, :] * q
            gate = raw[at, 2 * feats + j * LANES : 2 * feats + (j + 1) * LANES]
            sig = jax.nn.sigmoid(gate)
            silu = gate * sig
            gain = mix_gain[:, lanes]
            d = d_mixin[at, lanes] * gain
            mixed[at, lanes] = (hat * gain * silu).astype(BF)
            d_gate_raw[at, lanes] = (d * hat * sigmoid_slope(gate, sig)).astype(BF)
            d_states[j, at, :] = q * (d * silu - hat * mean)
    copies.flush(0, 1)

    def step(t, carry):
        out = []
        at = pl.ds(rows - 1 - t, CHUNKS, stride=rows)
        for j in range(count):
            coming, passed = carry[2 * j], carry[2 * j + 1]
            here = decay[j, at, :]
            adjoint = d_states[j, at, :] + coming
            local[j, at, :] = adjoint
            after[j, at, :] = passed
            out += [here * adjoint, here * passed]
        return tuple(out)

    zero, one = jnp.zeros((CHUNKS, LANES), F32), jnp.ones((CHUNKS, LANES), F32)
    last = lax.fori_loop(0, rows, step, (zero, one) * count, unroll=8)
    for j in range(count):
        first[:, j * LANES : (j + 1) * LANES] = last[2 * j]


def mixer_weights_kernel(parts, normed, *refs):
    d_raw, outs = refs[:parts], refs[parts:]
    deep = normed.shape[1] // parts
    for d in range(parts):
        for k in range(parts):
            outs[d * parts + k][...] = contract_rows(normed[:, d * deep : (d + 1) * deep], d_raw[k][...]).astype(BF)


def out_weights_kernel(y_ref, x_ref, mixed, d_mixed, *refs):
    *outs, full = refs
    y, x = y_ref[0], x_ref[0]
    width = full.shape[1]
    sub, part = mixed.shape[1] // 2, width // CHUNKS
    for k in range(2):
        row = pl.multiple_of((k + y - 2 * k * y) * sub, sub)
        full[...] = contract_rows(mixed[:, pl.ds(row, sub)], d_mixed[:, :width])
        for m in range(2):
            half = m + x - 2 * m * x
            for z in range(Z // 2):
                for there in range(2):
                    near = (there + y - 2 * there * y) * Z + half * (Z // 2) + z
                    at = pl.ds(pl.multiple_of(near * part, part), part)
                    to = (z * 2 + there) * part
                    outs[k * 2 + m][:, to : to + part] = full[:, at].astype(BF)


def d_mixer_kernel(parties, parts, count, copies, x_ref, order, *refs):
    edges, firsts = refs[:parties], refs[parties : 2 * parties]
    refs = refs[2 * parties :]
    local, after, states, entry_own, raw, keep_mask, bound, d_gate_raw = refs[:8]
    refs = refs[8:]
    d_parts, (d_bound, passed, last, entry, d_raw) = refs[:parts], refs[parts:]
    group, feats = raw.shape[0], bound.shape[1]
    rows = group // CHUNKS
    collect(edges, (0, 2), passed)
    collect(firsts, (0, 1), last)
    entries(order, True, count, passed, last, entry)
    base = pl.multiple_of(order[count], CHUNKS)
    copies.wait(*range(2 * parties, 2 * parties + 8))
    top = lax.broadcasted_iota(jnp.int32, (rows, LANES), 0) == 0
    for j in range(feats // LANES):
        lanes = slice(j * LANES, (j + 1) * LANES)
        coming = entry[pl.ds(base, CHUNKS), lanes]
        low = bound[:, lanes]
        total = jnp.zeros((1, LANES), F32)
        for s in range(CHUNKS):
            at = slice(s * rows, (s + 1) * rows)
            adjoint = local[j, at, :] + after[j, at, :] * coming[s : s + 1, :]
            previous = jnp.where(top, entry_own[s : s + 1, lanes], pltpu.roll(states[j, at, :], 1, 0))
            inner = raw[at, lanes]
            sig_inner = jax.nn.sigmoid(inner)
            sig = jax.nn.sigmoid(raw[at, feats + j * LANES : feats + (j + 1) * LANES])
            open_part = (1.0 - low) * (1.0 - sig)
            d_forget = adjoint * (previous * keep_mask[at, :] - inner * sig_inner)
            d_inner = adjoint * open_part * sigmoid_slope(inner, sig_inner)
            d_raw[at, lanes] = d_inner.astype(BF)
            d_raw[at, feats + j * LANES : feats + (j + 1) * LANES] = (d_forget * open_part * sig).astype(BF)
            total = total + jnp.sum(d_forget * (1.0 - sig), axis=0, keepdims=True)
        d_bound[:, lanes] = total
    d_raw[:, 2 * feats :] = d_gate_raw[...]
    for k, d_part in enumerate(d_parts):
        d_part[...] = d_raw[:, columns_of(x_ref, parts, k, 3 * feats // parts)]


def d_normed_kernel(parts, copies, *refs):
    d_parts, weights, partial = refs[:parts], refs[parts:-1], refs[-1]
    group, deep = partial.shape[0], partial.shape[1] // parts
    for d in range(parts):
        copies.wait(*range(parts + d * parts, parts + (d + 1) * parts))
        for i in range(2):
            at = slice(i * group // 2, (i + 1) * group // 2)
            total = None
            for k, d_part in enumerate(d_parts):
                part = times_transposed(d_part[at, :], weights[d * parts + k][...])
                total = part if total is None else total + part
            partial[at, d * deep : (d + 1) * deep] = total.astype(BF)


def token_grad_kernel(summed, tokens, d_resid, gain, out):
    @pl.loop(0, tokens.shape[0] // STEP)
    def _(i):
        at = pl.ds(i * STEP, STEP)
        value = tokens[at, :].astype(F32)
        inv = inverse_rms(value)
        hat = value * inv
        d = summed[at, :].astype(F32) * gain[...]
        out[at, :] = d_resid[at, :] + inv * (d - hat * mean_last(d * hat))


def after(value, *others):
    return lax.optimization_barrier((value, *others))[0]


def gather_rows(own):
    return lax.all_gather(own, ("z", "c"), axis=0, tiled=True)


def scatter_rows(partial):
    return lax.psum_scatter(partial, ("z", "c"), scatter_dimension=0, tiled=True)


def per_device(
    tokens, lengths, w_in, w_forget, w_gate, w_out, attn_gain, mix_gain, bound_table,
    ff_gate, ff_up, ff_down, mlp_gain, out_grad,
):
    Y = lax.axis_size("y")
    pair = Y == 2
    parts = 2 if pair else 1
    z, y, c, x = (lax.axis_index(a) for a in "zycx")
    rows, width = tokens.shape
    sub = w_in.shape[0]
    feats = Y * sub
    block = ff_gate.shape[1] // CHUNKS
    tall = 3 * block
    group = rows * CHUNKS
    near_y = y[None].astype(jnp.int32)

    def y_first(*values):
        if pair:
            return call(
                functools.partial(reorder_kernel, False),
                [(v.shape, v.dtype) for v in values], near_y, *values, smem=1,
            )
        return [
            v.reshape(v.shape[0], Z, Y, C * sub).transpose(0, 2, 1, 3).reshape(v.shape) for v in values
        ]

    def z_first(*values):
        if pair:
            return call(
                functools.partial(reorder_kernel, True),
                [(v.shape, v.dtype) for v in values], near_y, *values, smem=1,
            )
        return [
            v.reshape(v.shape[0], Y, Z, C * sub).transpose(0, 2, 1, 3).reshape(v.shape) for v in values
        ]

    def over_y(value):
        if pair:
            return [value, swap(value, "y")]
        return [lax.all_gather(value, "y", axis=0, tiled=True)]

    def in_order(value):
        if pair:
            other = swap(value, "y")
            return jnp.concatenate(
                [jnp.where(y == 0, value, other), jnp.where(y == 0, other, value)], axis=0
            )
        return lax.all_gather(value, "y", axis=0, tiled=True)

    def spread(value):
        return lax.all_to_all(value, ("z", "c"), 0, 0, tiled=True)

    def both(own, sent, axis):
        return own.astype(BF).astype(F32) + swap(sent.astype(BF), axis).astype(F32)

    near_x = x[None].astype(jnp.int32)
    z_c = jnp.stack([z, c]).astype(jnp.int32)

    def own_and_neighbours(value):
        corner = lax.ppermute(value, ("y", "x"), [(i, 3 - i) for i in range(4)])
        return [value, swap(value, "x"), swap(value, "y"), corner]

    table_f = bound_table.astype(F32)
    soft = jax.nn.softmax(table_f, axis=0)
    own_bound = jnp.sum(soft[1 : LAYER + 1], axis=0)

    if pair:
        (glu,) = call(glu_blocks_kernel, [((CHUNKS, tall, sub), BF)], ff_gate, ff_up, ff_down)
    else:
        glu = jnp.concatenate([w.T.reshape(CHUNKS, block, sub) for w in (ff_gate, ff_up)], axis=1)
        glu = jnp.concatenate([glu, ff_down.reshape(CHUNKS, block, sub)], axis=1)
    (out_rows,) = y_first(in_order(w_out))

    tokens_y, grad_y = y_first(tokens, out_grad)
    if pair:
        (blocks,) = call(
            mixer_blocks_kernel, [((CHUNKS, sub, 3 * feats // 2), BF)], near_x, w_in, w_forget, w_gate, smem=1
        )
        moved = after(spread(blocks), glu, out_rows)
        small = jnp.stack([attn_gain.astype(F32), mlp_gain.astype(F32), own_bound, mix_gain.astype(F32)])
        small = [small, swap(small, "y")]
        (piece,) = call(
            token_piece_kernel, [((rows, width + LANES), BF)],
            near_y, tokens, jnp.concatenate([v[:2] for v in small]), smem=1,
        )
        tokens_all = gather_rows(after(piece, moved))
        gains = tokens_all.reshape(CHUNKS, rows, -1)[:, :4, width:].astype(F32)
        attn_g, mlp_g = (
            jnp.concatenate([gains[:, k].reshape(1, -1), gains[:, 2 + k].reshape(1, -1)], axis=1) for k in range(2)
        )
        small = jnp.stack([v[2:] for v in small])
        small = jnp.where(y == 0, small, small[::-1])
        mixer = own_and_neighbours(moved.reshape(CHUNKS * sub, 3 * feats // 2))
    else:
        gains = lax.all_gather(jnp.stack([attn_gain, mlp_gain]), ("z", "y", "c"), axis=1, tiled=True)
        attn_g, mlp_g = y_first(gains[:1].astype(F32), gains[1:].astype(F32))
        tokens_all = gather_rows(tokens_y)
        small = in_order(jnp.stack([own_bound, mix_gain.astype(F32)])[None])
        mixer = [
            w.reshape(sub, Z, Y, C, sub).transpose(1, 3, 0, 2, 4).reshape(CHUNKS, sub, feats)
            for w in (w_in, w_forget, w_gate)
        ]
        moved = spread(jnp.concatenate(mixer, axis=2))
        mixer = over_y(moved.reshape(CHUNKS * sub, 3 * feats))
    glu = spread(after(glu, moved))
    bound = small[:, 0].reshape(1, feats)
    mix_g = small[:, 1].reshape(1, feats)

    slot = jnp.arange(lengths.shape[0])
    starts = jnp.sum(jnp.where(slot[None, :] < slot[:, None], lengths[None, :], 0), axis=1)
    slot = jnp.arange(CHUNKS)
    chunk = (slot // C * Y + y) * (C * X) + slot % C * X + x
    position = (chunk[:, None] * rows + jnp.arange(rows)[None, :]).reshape(group)
    keep = 1.0 - jnp.any(position[:, None] == starts[None, :], axis=1).astype(F32)[:, None]
    count = Z * Y * C * X
    number = jnp.arange(count)
    xn, cn = number % X, number // X % C
    yn, zn = number // (X * C) % Y, number // (X * C * Y)
    party = (yn ^ y) * X + (xn ^ x) if pair else yn * X + xn
    order = party * CHUNKS + zn * C + cn
    base = 0 * y if pair else (y * X + x) * CHUNKS
    order = jnp.concatenate([order, jnp.stack([base, z * C + c])]).astype(jnp.int32)

    def parties(value):
        if pair:
            return own_and_neighbours(value)
        return [lax.all_gather(value, ("y", "x"), axis=0, tiled=True)]

    crowd = 4 if pair else 1
    featured = ((feats // LANES, group, LANES), F32)
    normed, raw, decay, local, through, edge = call(
        functools.partial(mixer_forward_kernel, parts),
        [((group, width), BF), ((group, 3 * feats), F32)] + [featured] * 3 + [((2 * CHUNKS, feats), F32)],
        near_x, attn_g, tokens_all, bound, keep, *mixer,
        smem=1, scratch=[pltpu.VMEM(*featured)], late=2,
    )
    edges = parties(edge)
    def assemble(pieces):
        return jnp.concatenate([p.transpose(1, 0, 2).reshape(p.shape[1], -1) for p in pieces], axis=1)

    def around(blocks):
        cut = blocks.shape[1] // 2
        side, up_y = swap(blocks, "x"), swap(blocks, "y")
        corner = [swap(up_y[:, :cut], "x"), swap(side[:, cut:], "y")]
        near, far = assemble([blocks, up_y]), assemble([side, jnp.concatenate(corner, axis=1)])
        return [near, far], (side, up_y), corner

    early, late, last = (), (), ()
    gate_up, down = glu[:, : 2 * block], glu[:, 2 * block :]
    if pair:
        gate_up_w, early, _ = around(after(gate_up, edges[0]))
        down_w, late, last = around(after(down, *early))
    else:
        gate_up_w, down_w = (assemble(over_y(v)) for v in (gate_up, down))
        gate_up_w, down_w = ([v, swap(v, "x")] for v in (gate_up_w, down_w))
    carries = [pltpu.VMEM((Y * X * CHUNKS, feats), F32)] * 3
    states, entry, partial = call(
        functools.partial(mixer_out_kernel, crowd, count),
        [featured, ((CHUNKS, feats), F32), ((group, width + LANES), BF)],
        order, *edges, local, through, raw, mix_g, out_rows,
        smem=1, scratch=carries + [pltpu.VMEM((group, feats), BF)], late=crowd,
    )
    summed = scatter_rows(after(partial, glu))
    own_grad = lax.all_to_all(jnp.broadcast_to(after(grad_y, glu)[None], (Z, rows, width)), "z", 0, 0, tiled=False)
    other_grad = swap(own_grad, "c")
    grad_all = jnp.where(
        c == 0, jnp.stack([own_grad, other_grad], axis=1), jnp.stack([other_grad, own_grad], axis=1)
    ).reshape(group, width)
    resid, hidden, scale = call(
        resid_kernel,
        [((rows, width), F32), ((rows, width), BF), ((rows, LANES), F32)],
        after(summed, own_grad, *early, *late), tokens_y, mlp_g,
    )
    hidden_all = after(gather_rows(hidden), grad_all)
    thin = ((group, block), BF)
    act0, d_gate0, d_up0, act1, d_gate1, d_up1, partial = call(
        glu_kernel, [thin] * 6 + [((group, 2 * width), BF)],
        hidden_all, grad_all, *gate_up_w, *down_w, late=0, scratch=[pltpu.VMEM((group, 2 * width), F32)],
    )
    acts = [act0, act1]

    def weight_pieces(terms, lefts, *rights):
        height = len(terms) * block
        shapes = [((height, width), BF)] * 2
        if pair:
            shapes = [((2, height // 2, width // 2), BF)] * 4
        return call(
            functools.partial(glu_weights_kernel, parts, terms), shapes, *lefts, *rights,
        )

    def first_swaps(pieces):
        upper, upper_sent, lower, lower_sent = pieces
        return upper, swap(upper_sent, "x"), lower, swap(lower_sent, "y")

    def first_sums(pieces):
        height = pieces[0].shape[1]
        shapes = [((height, width // 2), F32), ((height, width // 2), BF)] * 2
        return call(first_sums_kernel, shapes, *pieces)

    def last_swaps(pieces):
        upper, upper_sent, lower, lower_sent = pieces
        return upper, swap(upper_sent, "y"), lower, swap(lower_sent, "x")

    def last_sums(*pieces):
        height = sum(p.shape[0] for p in pieces[::2])
        return call(last_sums_kernel, [((CHUNKS, height, sub), BF)], *pieces)[0]

    def to_blocks(value):
        return value.reshape(value.shape[0], -1, sub).transpose(1, 0, 2)

    def total_blocks(pieces):
        blocks = to_blocks(both(*pieces, "x").astype(BF))
        return lax.psum_scatter(blocks, "y", scatter_dimension=0, tiled=True)

    summed = scatter_rows(partial)
    gate_up = weight_pieces((0, 0), [d_gate0, d_up0, d_gate1, d_up1], hidden_all)
    down = weight_pieces((0,), acts, grad_all)
    if pair:
        gate_up = first_sums(first_swaps(gate_up))
        down = first_swaps(down)
        summed, *gate_up = lax.optimization_barrier((summed, *gate_up))
    d_resid, piece, result_y = call(
        d_resid_kernel, [((rows, width), F32), ((rows, width + LANES), BF), ((rows, width), BF)],
        summed, resid, tokens_y, grad_y, mlp_g, scale,
    )
    if pair:
        piece, *down = lax.optimization_barrier((piece, *down))
    d_mixed = gather_rows(piece)
    if pair:
        gate_up = last_swaps(gate_up)
        down = last_swaps(first_sums(down))
        d_mixed, *gate_up = lax.optimization_barrier((d_mixed, *gate_up))
        d_mixed, *down = lax.optimization_barrier((d_mixed, *down))

    mixed_in, d_gate_raw, adjoint, passed, first = call(
        mixer_back_kernel,
        [((group, feats), BF)] * 2 + [featured] * 2 + [((CHUNKS, feats), F32)],
        d_mixed, out_rows, raw, states, mix_g, decay,
        scratch=[pltpu.VMEM((group, feats), F32), pltpu.VMEM(*featured)], late=2,
    )
    firsts = parties(first)
    grad_out = mixed_in
    if pair:
        out_pieces = call(
            out_weights_kernel, [((sub, width // 2), BF)] * 4,
            near_y, near_x, mixed_in, d_mixed, smem=2, scratch=[pltpu.VMEM((sub, width), F32)],
        )
        out_pieces = after(out_pieces, *firsts)
        grad_out = sum(
            p.astype(F32)
            for p in (
                out_pieces[0],
                swap(out_pieces[1], "x"),
                swap(out_pieces[2], "y"),
                lax.ppermute(out_pieces[3], ("y", "x"), [(i, 3 - i) for i in range(4)]),
            )
        ).astype(BF)
    if pair:
        glu_grad = last_sums(*after((*gate_up, *down), first))
    else:
        glu_grad = jnp.concatenate([total_blocks(gate_up), total_blocks(down)], axis=1)
    raw = after(raw, glu_grad)
    glu_grad = spread(glu_grad)
    *d_raw, part_bound = call(
        functools.partial(d_mixer_kernel, crowd, parts, count),
        [((group, 3 * feats // parts), BF)] * parts
        + [((1, feats), F32)],
        near_x, order, *edges, *firsts, adjoint, passed, states, entry, raw, keep, bound, d_gate_raw,
        smem=2, scratch=carries + [pltpu.VMEM((group, 3 * feats), BF)], late=2 * crowd,
    )

    pieces = call(
        functools.partial(mixer_weights_kernel, parts),
        [((width // parts, 3 * feats // parts), BF)] * parts**2,
        normed, *d_raw,
    )
    (partial,) = call(
        functools.partial(d_normed_kernel, parts), [((group, width), BF)],
        *after(d_raw, grad_out, *pieces), *mixer, late=parts,
    )
    (token_grad_y,) = call(
        token_grad_kernel, [((rows, width), F32)],
        scatter_rows(partial), tokens_y, d_resid, attn_g,
    )
    result, token_grad = z_first(result_y, token_grad_y)

    part_bound = part_bound.reshape(feats)
    if pair:
        pieces = [
            pieces[0],
            swap(pieces[1], "x"),
            swap(pieces[2], "y"),
            lax.ppermute(pieces[3], ("y", "x"), [(i, 3 - i) for i in range(4)]),
        ]
        top, bottom = jnp.split(part_bound, 2)
        d_bound = jnp.where(y == 0, top, bottom) + swap(jnp.where(y == 0, bottom, top), "y")
        pieces = after(pieces, d_bound)
        shape = (2, sub, 3 * feats // 2)
        theirs, *mine = call(
            mixer_sums_kernel, [((Z, *shape[1:]), BF)] + [(shape, BF)] * Z, z_c, *pieces, smem=1
        )
        got = swap(theirs, "c")
        d_bound = after(d_bound, got)
        mine = [v.at[1].set(got[k]) for k, v in enumerate(mine)]
        mixer_grad = [mine[0]] + [lax.ppermute(mine[k], "z", [(i, i ^ k) for i in range(Z)]) for k in range(1, Z)]
    else:
        d_bound = lax.psum_scatter(part_bound, "y", scatter_dimension=0, tiled=True)
        mixer_grad = lax.psum_scatter(pieces[0], "y", scatter_dimension=0, tiled=True)
        mixer_grad = both(mixer_grad, mixer_grad, "x").astype(BF)
        mixer_grad = spread(mixer_grad.reshape(CHUNKS, sub, 3 * feats))
    if pair:
        grad_gate_ff, grad_up_ff, grad_down, along_ff = call(
            glu_grads_kernel,
            [((sub, CHUNKS * block), F32)] * 2 + [((CHUNKS * block, sub), F32), ((sub, LANES), F32)],
            glu_grad, ff_gate, ff_up,
        )
        grad_mlp = along_ff[:, 0]
        grad_mlp = grad_mlp + swap(grad_mlp, "x")
        d_bound = d_bound + swap(d_bound, "x")
        mixer_grad[-1] = after(mixer_grad[-1], grad_out, d_bound, grad_mlp)
        mixer_grad = mixer_grad + [swap(v, "x") for v in mixer_grad]
        other = swap(grad_out, "x")
        grad_out = jnp.concatenate(
            [jnp.where(x == 0, grad_out, other), jnp.where(x == 0, other, grad_out)], axis=1
        ).astype(F32)
    else:
        (grad_out,) = z_first(contract_rows(mixed_in, d_mixed[:, :width]).astype(BF))
        grad_out = lax.psum_scatter(grad_out, "y", scatter_dimension=0, tiled=True)
        grad_out = both(grad_out, grad_out, "x")
        d_bound = d_bound + swap(d_bound, "x")
    row_ids = jnp.arange(bound_table.shape[0])[:, None]
    member = jnp.logical_and(row_ids >= 1, row_ids <= LAYER).astype(F32)
    grad_table = soft * (member - own_bound[None, :]) * d_bound[None, :]

    def along(weight, grad):
        return jnp.sum(weight.astype(F32) * grad, axis=1)

    square = ((sub, width), F32)
    if pair:
        grad_in, grad_forget, grad_gate, grad_attn = call(
            mixer_grads_kernel, [square] * 3 + [((sub, LANES), F32)],
            jnp.concatenate([near_x, z_c]), *mixer_grad, w_in, w_forget, w_gate, smem=1,
        )
        grad_attn = grad_attn[:, 0]
    else:
        mixer_grad = mixer_grad.reshape(Z, C, sub, 3, Y, sub).transpose(3, 2, 0, 4, 1, 5)
        grad_in, grad_forget, grad_gate = mixer_grad.reshape(3, sub, width).astype(F32)
        grad_attn = along(w_in, grad_in) + along(w_forget, grad_forget) + along(w_gate, grad_gate)
        grad_gate_ff, grad_up_ff = (
            glu_grad[:, k * block : (k + 1) * block].astype(F32).reshape(CHUNKS * block, sub).T for k in range(2)
        )
        grad_down = glu_grad[:, 2 * block :].reshape(CHUNKS * block, sub).astype(F32)
        grad_mlp = along(ff_gate, grad_gate_ff) + along(ff_up, grad_up_ff)
        grad_mlp = grad_mlp + swap(grad_mlp, "x")
    grad_attn = grad_attn / attn_gain.astype(F32)
    grad_mix = along(w_out, grad_out) / mix_gain.astype(F32)
    grad_mlp = grad_mlp / mlp_gain.astype(F32)
    return (
        result, token_grad, grad_in, grad_forget, grad_gate, grad_out, grad_attn, grad_mix,
        grad_table, grad_gate_ff, grad_up_ff, grad_down, grad_mlp,
    )


def solution(mesh):
    dp, mp = mesh.devices.shape
    grid = Mesh(mesh.devices.reshape(Z, dp // CHUNKS, C, mp), ("z", "y", "c", "x"))
    dp_axes = ("z", "y", "c")
    every = ("z", "y", "c", "x")
    mat, row, gain = P(dp_axes, None), P(every, None), P(dp_axes)
    table, glu, glu_down = P(None, dp_axes), P(dp_axes, "x"), P("x", dp_axes)
    return jax.shard_map(
        per_device,
        mesh=grid,
        in_specs=(
            row, P(), mat, mat, mat, mat, gain, gain, table, glu, glu, glu_down, gain, row,
        ),
        out_specs=(
            row, row, mat, mat, mat, mat, gain, gain, table, glu, glu, glu_down, gain,
        ),
        check_vma=False,
    )
```

```python
import functools

import jax
import jax.numpy as jnp
from jax import lax
from jax.experimental import pallas as pl
from jax.experimental.pallas import tpu as pltpu
from jax.sharding import Mesh, PartitionSpec as P

LAYER = 12
Z, C, X = 4, 2, 2
CHUNKS = Z * C
LANES = 128
epsilon = 1e-06
VMEM_LIMIT = 56 << 20
BF, F32 = jnp.bfloat16, jnp.float32


def swap(value, axis):
    return lax.ppermute(value, axis, [(0, 1), (1, 0)])


def dot(left, right):
    return jnp.dot(left, right, preferred_element_type=F32)


def contract_rows(left, right):
    return lax.dot_general(left, right, (((0,), (0,)), ((), ())), preferred_element_type=F32)


def times_transposed(left, right):
    return lax.dot_general(left, right, (((1,), (1,)), ((), ())), preferred_element_type=F32)


def mean_last(value):
    return jnp.mean(value, axis=-1, keepdims=True)


def inverse_rms(value):
    return lax.rsqrt(mean_last(value * value) + epsilon)


def sigmoid_slope(raw, sig):
    return sig * (1.0 + raw * (1.0 - sig))


class Copies:
    def __init__(self, inputs, outputs):
        self.inputs, self.outputs, self.waited, self.flushed = inputs, outputs, set(), set()
        for copy in inputs:
            copy.start()

    def wait(self, *numbers):
        for k in numbers:
            if k not in self.waited:
                self.waited.add(k)
                self.inputs[k].wait()

    def flush(self, *numbers):
        for k in numbers:
            if k not in self.flushed:
                self.flushed.add(k)
                self.outputs[k].start()


def call(kernel, outs, *ins, smem=0, scratch=(), late=None):
    n_in, n_out = len(ins) - smem, len(outs)

    def body(*refs):
        scalars, refs = refs[:smem], refs[smem:]
        far_in, far_out, refs = refs[:n_in], refs[n_in : n_in + n_out], refs[n_in + n_out :]
        near_in, near_out, refs = refs[:n_in], refs[n_in : n_in + n_out], refs[n_in + n_out :]
        *own, in_sems, out_sems = refs
        copies = Copies(
            [pltpu.make_async_copy(f, n, in_sems.at[k]) for k, (f, n) in enumerate(zip(far_in, near_in))],
            [pltpu.make_async_copy(n, f, out_sems.at[k]) for k, (f, n) in enumerate(zip(far_out, near_out))],
        )
        copies.wait(*range(n_in if late is None else late))
        kernel(*([] if late is None else [copies]), *scalars, *near_in, *near_out, *own)
        copies.wait(*range(n_in))
        copies.flush(*range(n_out))
        for copy in copies.outputs:
            copy.wait()

    shapes = [jax.ShapeDtypeStruct(s, t) for s, t in outs]
    near = [pltpu.VMEM(v.shape, v.dtype) for v in list(ins[smem:]) + shapes]
    return pl.pallas_call(
        body,
        out_shape=shapes,
        in_specs=[pl.BlockSpec(memory_space=pltpu.SMEM)] * smem + [pl.BlockSpec(memory_space=pl.ANY)] * n_in,
        out_specs=[pl.BlockSpec(memory_space=pl.ANY)] * n_out,
        scratch_shapes=near
        + list(scratch)
        + [pltpu.SemaphoreType.DMA((n_in,)), pltpu.SemaphoreType.DMA((n_out,))],
        compiler_params=pltpu.CompilerParams(vmem_limit_bytes=VMEM_LIMIT),
        cost_estimate=pl.CostEstimate(flops=0, bytes_accessed=1024, transcendentals=0),
    )(*ins)


def stat_block(columns, first=0):
    rows = columns[0].shape[0]
    lane = lax.broadcasted_iota(jnp.int32, (rows, LANES), 1) - first
    block = jnp.zeros((rows, LANES), F32)
    for k, column in enumerate(columns):
        high = column.astype(BF).astype(F32)
        block = jnp.where(lane == 2 * k, high, block)
        block = jnp.where(lane == 2 * k + 1, column - high, block)
    return block


def stat(block, k):
    lane = lax.broadcasted_iota(jnp.int32, block.shape, 1)
    picked = jnp.where((lane == 2 * k) | (lane == 2 * k + 1), block.astype(F32), 0.0)
    return jnp.sum(picked, axis=1, keepdims=True)


def reorder_kernel(back, y_ref, *refs):
    y = y_ref[0]
    half = len(refs) // 2
    for in_ref, out_ref in zip(refs[:half], refs[half:]):
        width = in_ref.shape[1] // CHUNKS
        for k in range(2):
            there = k + y - 2 * k * y
            for z in range(Z):
                near = slice((k * Z + z) * width, (k * Z + z + 1) * width)
                far = pl.ds(pl.multiple_of((z * 2 + there) * width, width), width)
                if back:
                    out_ref[:, far] = in_ref[:, near]
                else:
                    out_ref[:, near] = in_ref[:, far]


def token_piece_kernel(y_ref, tokens, gains, piece):
    width = tokens.shape[1]
    reorder_kernel(False, y_ref, tokens, piece.at[:, :width])
    row = lax.broadcasted_iota(jnp.int32, (tokens.shape[0], LANES), 0)
    block = jnp.zeros((tokens.shape[0], LANES), F32)
    for k in range(gains.shape[0]):
        block = jnp.where(row == k, gains[k : k + 1, :], block)
    piece[:, width:] = block.astype(BF)


def mixer_blocks_kernel(x_ref, *refs):
    *weights, out_ref = refs
    half = len(weights)
    x = x_ref[0]
    for z in range(Z):
        for c in range(C):
            for k in range(half):
                pieces = []
                for j in (k, half + k):
                    at = ((z * 2 + j % 2) * C + c) * LANES
                    pieces.append(weights[j // 2][:, at : at + LANES])
                out_ref[z * C + c, :, k * LANES : (k + 1) * LANES] = jnp.where(x == 0, *pieces)


def mixer_sums_kernel(at_ref, *refs):
    pieces, theirs, mine = refs[:4], refs[4], refs[5:]
    z, c = at_ref[0], at_ref[1]
    sub = theirs.shape[1]
    for k in range(Z):
        bits = [(z // 2 + k // 2) % 2, (z + k) % 2]
        for other in range(2):
            core = c + other - 2 * c * other
            row = pl.ds(pl.multiple_of(((bits[0] * 2 + bits[1]) * 2 + core) * sub, sub), sub)
            total = pieces[0][row, :].astype(F32)
            for p in pieces[1:]:
                total = total + p[row, :].astype(F32)
            if other:
                theirs[k] = total.astype(BF)
            else:
                mine[k][0] = total.astype(BF)
                mine[k][1] = jnp.zeros(theirs.shape[1:], BF)


def mixer_grads_kernel(at_ref, *refs):
    mine, theirs, refs = refs[:Z], refs[Z : 2 * Z], refs[2 * Z :]
    w_in, w_forget, w_gate, grad_in, grad_forget, grad_gate, along_ref = refs
    x, z, c = at_ref[0], at_ref[1], at_ref[2]
    total = jnp.zeros((w_in.shape[0], 1), F32)
    for m, (w_ref, g_ref) in enumerate(((w_in, grad_in), (w_forget, grad_forget), (w_gate, grad_gate))):
        for k in range(Z):
            there = (z // 2 + k // 2) % 2 * 2 + (z + k) % 2
            for y in range(2):
                for other in range(2):
                    core = c + other - 2 * c * other
                    j = m * 2 + y
                    to = pl.ds(pl.multiple_of(((there * 2 + y) * C + core) * LANES, LANES), LANES)
                    at = j % 3 * LANES
                    piece = jnp.where(
                        x == j // 3,
                        mine[k][other, :, at : at + LANES],
                        theirs[k][other, :, at : at + LANES],
                    ).astype(F32)
                    g_ref[:, to] = piece
                    weight = w_ref[:, to].astype(F32)
                    total = total + jnp.sum(piece * weight, axis=1, keepdims=True)
    along_ref[...] = jnp.broadcast_to(total, along_ref.shape)


def glu_blocks_kernel(gate_ref, up_ref, down_ref, out_ref):
    block = down_ref.shape[0] // CHUNKS
    for s in range(CHUNKS):
        at = slice(s * block, (s + 1) * block)
        out_ref[s, :block] = gate_ref[:, at].astype(F32).T.astype(BF)
        out_ref[s, block : 2 * block] = up_ref[:, at].astype(F32).T.astype(BF)
        out_ref[s, 2 * block :] = down_ref[at, :]


def glu_grads_kernel(blocks_ref, w_gate, w_up, grad_gate, grad_up, grad_down, along_ref):
    block = blocks_ref.shape[1] // 3
    total = jnp.zeros((w_gate.shape[0], 1), F32)
    for s in range(CHUNKS):
        at = slice(s * block, (s + 1) * block)
        for m, (w_ref, g_ref) in enumerate(((w_gate, grad_gate), (w_up, grad_up))):
            piece = blocks_ref[s, m * block : (m + 1) * block].astype(F32).T
            g_ref[:, at] = piece
            total = total + jnp.sum(piece * w_ref[:, at].astype(F32), axis=1, keepdims=True)
        grad_down[at, :] = blocks_ref[s, 2 * block :].astype(F32)
    along_ref[...] = jnp.broadcast_to(total, along_ref.shape)


def columns_of(x_ref, parts, k, span):
    if parts == 1:
        return slice(0, span)
    return pl.ds(pl.multiple_of((k + x_ref[0] - 2 * k * x_ref[0]) * span, LANES), span)


def mixer_forward_kernel(parts, copies, x_ref, *refs):
    gain, tokens, bound, keep = refs[:4]
    weights = refs[4 : 4 + parts * parts]
    normed, raw, decay, local, through, edge, drive = refs[4 + parts * parts :]
    group, feats = raw.shape[0], bound.shape[1]
    width = gain.shape[1]
    rows = group // CHUNKS

    @pl.loop(0, group // 32)
    def _(i):
        at = pl.ds(i * 32, 32)
        value = tokens[at, :width].astype(F32)
        normed[at, :] = (value * inverse_rms(value) * gain[...]).astype(BF)

    copies.flush(0)
    copies.wait(*range(2, 4 + parts * parts))

    @pl.loop(0, 2)
    def _(i):
        at = pl.ds(i * (group // 2), group // 2)
        deep, span = width // parts, 3 * feats // parts
        for k in range(parts):
            total = None
            for d in range(parts):
                part = dot(normed[at, d * deep : (d + 1) * deep], weights[d * parts + k][...])
                total = part if total is None else total + part
            raw[at, columns_of(x_ref, parts, k, span)] = total

    copies.flush(1)
    count = feats // LANES

    @pl.loop(0, CHUNKS)
    def _(i):
        at = pl.ds(i * rows, rows)
        for j in range(count):
            lanes = slice(j * LANES, (j + 1) * LANES)
            inner = raw[at, lanes]
            forget_raw = raw[at, feats + j * LANES : feats + (j + 1) * LANES]
            low = bound[:, lanes]
            forget = low + (1.0 - low) * jax.nn.sigmoid(forget_raw)
            drive[j, at, :] = inner * jax.nn.sigmoid(inner) * (1.0 - forget)
            decay[j, at, :] = forget * keep[at, :]

    copies.flush(2)

    def step(t, carry):
        out = []
        at = pl.ds(t, CHUNKS, stride=rows)
        for j in range(count):
            state, passed = carry[2 * j], carry[2 * j + 1]
            here = decay[j, at, :]
            state = here * state + drive[j, at, :]
            passed = here * passed
            local[j, at, :] = state
            through[j, at, :] = passed
            out += [state, passed]
        return tuple(out)

    zero, one = jnp.zeros((CHUNKS, LANES), F32), jnp.ones((CHUNKS, LANES), F32)
    last = lax.fori_loop(0, rows, step, (zero, one) * count, unroll=8)
    for j in range(count):
        edge[:CHUNKS, j * LANES : (j + 1) * LANES] = last[2 * j + 1]
        edge[CHUNKS:, j * LANES : (j + 1) * LANES] = last[2 * j]


def entries(order, backwards, count, passed, last, entry):
    def step(n, running):
        row = pl.ds(order[count - 1 - n if backwards else n], 1)
        entry[row, :] = running
        return passed[row, :] * running + last[row, :]

    lax.fori_loop(0, count, step, jnp.zeros((1, last.shape[1]), F32))


def collect(parties, at, to):
    base = 0
    for p in parties:
        for g in range(p.shape[0] // (at[1] * CHUNKS)):
            begin = (g * at[1] + at[0]) * CHUNKS
            to[base : base + CHUNKS, :] = p[begin : begin + CHUNKS, :]
            base += CHUNKS


def mixer_out_kernel(parties, count, copies, order, *refs):
    edges = refs[:parties]
    local, through, raw, mix_gain, out_w = refs[parties : parties + 5]
    states, entry_own, partial, passed, last, entry, mixed = refs[parties + 5 :]
    group, feats = raw.shape[0], mix_gain.shape[1]
    width = out_w.shape[1]
    rows = group // CHUNKS
    collect(edges, (0, 2), passed)
    collect(edges, (1, 2), last)
    entries(order, False, count, passed, last, entry)
    base = order[count]
    entry_own[...] = entry[pl.ds(pl.multiple_of(base, CHUNKS), CHUNKS), :]
    copies.wait(*range(parties, parties + 4))
    for s in range(CHUNKS):
        at = slice(s * rows, (s + 1) * rows)
        total = jnp.zeros((rows, LANES), F32)
        for j in range(feats // LANES):
            lanes = slice(j * LANES, (j + 1) * LANES)
            state = local[j, at, :] + through[j, at, :] * entry_own[s : s + 1, lanes]
            gate = raw[at, 2 * feats + j * LANES : 2 * feats + (j + 1) * LANES]
            mixed[at, lanes] = (state * (mix_gain[:, lanes] * (gate * jax.nn.sigmoid(gate)))).astype(BF)
            states[j, at, :] = state
            total = total + state * state
        squares = jnp.sum(total, axis=1, keepdims=True)
        partial[at, width:] = stat_block([squares], 2 * order[count + 1]).astype(BF)
    copies.flush(0)
    copies.wait(parties + 4)
    for k in range(2):
        at = slice(k * group // 2, (k + 1) * group // 2)
        partial[at, :width] = dot(mixed[at, :], out_w[...]).astype(BF)


STEP = 16


def resid_kernel(summed, tokens, gain, resid, hidden, scale):
    width = tokens.shape[1]

    @pl.loop(0, tokens.shape[0] // STEP)
    def _(i):
        at = pl.ds(i * STEP, STEP)
        squares = jnp.sum(summed[at, width:].astype(F32), axis=1, keepdims=True)
        q = lax.rsqrt(squares / width + epsilon)
        value = tokens[at, :].astype(F32) + q * summed[at, :width].astype(F32)
        resid[at, :] = value
        hidden[at, :] = (value * inverse_rms(value) * gain[...]).astype(BF)
        scale[at, :] = jnp.broadcast_to(q, (STEP, LANES))


def glu_kernel(copies, hidden, grad, *refs):
    weights, outs, partial, total = refs[:4], refs[4:10], refs[10], refs[11]
    group, block = outs[0].shape
    width = hidden.shape[1]
    for k in range(2):
        gate_up, down = weights[k], weights[2 + k]
        act, d_gate, d_up = outs[3 * k : 3 * k + 3]
        w_gate, w_up = gate_up.at[:block, :], gate_up.at[block:, :]
        copies.wait(0, 2 + k)
        for i in range(2):
            at = slice(i * group // 2, (i + 1) * group // 2)
            gate = times_transposed(hidden[at, :], w_gate[...])
            up = times_transposed(hidden[at, :], w_up[...])
            copies.wait(1, 4 + k)
            d_act = times_transposed(grad[at, :], down[...])
            sig = jax.nn.sigmoid(gate)
            silu = gate * sig
            act[at, :] = (silu * up).astype(BF)
            d_gate[at, :] = (d_act * up * sigmoid_slope(gate, sig)).astype(BF)
            d_up[at, :] = (d_act * silu).astype(BF)
            back = dot(d_gate[at, :], w_gate[...]) + dot(d_up[at, :], w_up[...])
            for cols, value in ((slice(0, width), back), (slice(width, None), dot(act[at, :], down[...]))):
                if k == 0:
                    total[at, cols] = value
                else:
                    partial[at, cols] = (total[at, cols] + value).astype(BF)
        copies.flush(3 * k, 3 * k + 1, 3 * k + 2)


def glu_weights_kernel(parts, terms, *refs):
    count = len(terms)
    lefts, rights, outs = refs[: 2 * count], refs[2 * count : 2 * count + max(terms) + 1], None
    outs = refs[2 * count + max(terms) + 1 :]
    block = lefts[0].shape[1]
    part = rights[0].shape[1] // parts
    cut = count * block // 2
    for k in range(2):
        for m, right in enumerate(terms):
            begin, end = m * block, (m + 1) * block
            for d in range(parts):
                value = contract_rows(lefts[k * count + m][...], rights[right][:, d * part : (d + 1) * part])
                value = value.astype(BF)
                if parts == 1:
                    outs[k][begin:end, :] = value
                    continue
                upper, lower = outs[k], outs[2 + d]
                if begin < cut:
                    upper[d, begin : min(end, cut)] = value[: min(end, cut) - begin]
                if end > cut:
                    lower[k, max(begin, cut) - cut : end - cut] = value[max(begin, cut) - begin :]


def first_sums_kernel(upper, upper_got, lower, lower_got, upper_keep, upper_send, lower_keep, lower_send):
    for mine, got, keep, send in (
        (upper, upper_got, upper_keep, upper_send),
        (lower, lower_got, lower_keep, lower_send),
    ):
        keep[...] = mine[0].astype(F32) + got[0].astype(F32)
        send[...] = (mine[1].astype(F32) + got[1].astype(F32)).astype(BF)


def last_sums_kernel(*refs):
    *pieces, blocks = refs
    begin = 0
    for mine, got in zip(pieces[::2], pieces[1::2]):
        for s in range(CHUNKS):
            cols = slice(s * LANES, (s + 1) * LANES)
            blocks[s, begin : begin + mine.shape[0]] = (mine[:, cols] + got[:, cols].astype(F32)).astype(BF)
        begin += mine.shape[0]


def d_resid_kernel(summed, resid, tokens, grad, gain, scale, d_resid, piece, result):
    width = tokens.shape[1]

    @pl.loop(0, tokens.shape[0] // STEP)
    def _(i):
        at = pl.ds(i * STEP, STEP)
        d_hidden = summed[at, :width].astype(F32) * gain[...]
        value = resid[at, :]
        inv = inverse_rms(value)
        hat = value * inv
        d_value = grad[at, :].astype(F32) + inv * (d_hidden - hat * mean_last(d_hidden * hat))
        d_resid[at, :] = d_value
        result[at, :] = (value + summed[at, width:].astype(F32)).astype(BF)
        low = d_value.astype(BF)
        piece[at, :width] = low
        mean = mean_last(low.astype(F32) * (value - tokens[at, :].astype(F32)))
        piece[at, width:] = stat_block([scale[at, :1], mean]).astype(BF)


def mixer_back_kernel(copies, d_mixed, out_w, raw, states, mix_gain, decay, *refs):
    mixed, d_gate_raw, local, after, first, d_mixin, d_states = refs
    width = out_w.shape[1]
    group, feats = raw.shape[0], mix_gain.shape[1]
    rows = group // CHUNKS
    count = feats // LANES
    for k in range(2):
        at = slice(k * group // 2, (k + 1) * group // 2)
        d_mixin[at, :] = times_transposed(d_mixed[at, :width], out_w[...])
    copies.wait(2, 3, 4, 5)
    for s in range(CHUNKS):
        at = slice(s * rows, (s + 1) * rows)
        stats = d_mixed[at, width:]
        q, mean = stat(stats, 0), stat(stats, 1)
        for j in range(count):
            lanes = slice(j * LANES, (j + 1) * LANES)
            hat = states[j, at, :] * q
            gate = raw[at, 2 * feats + j * LANES : 2 * feats + (j + 1) * LANES]
            sig = jax.nn.sigmoid(gate)
            silu = gate * sig
            gain = mix_gain[:, lanes]
            d = d_mixin[at, lanes] * gain
            mixed[at, lanes] = (hat * gain * silu).astype(BF)
            d_gate_raw[at, lanes] = (d * hat * sigmoid_slope(gate, sig)).astype(BF)
            d_states[j, at, :] = q * (d * silu - hat * mean)
    copies.flush(0, 1)

    def step(t, carry):
        out = []
        at = pl.ds(rows - 1 - t, CHUNKS, stride=rows)
        for j in range(count):
            coming, passed = carry[2 * j], carry[2 * j + 1]
            here = decay[j, at, :]
            adjoint = d_states[j, at, :] + coming
            local[j, at, :] = adjoint
            after[j, at, :] = passed
            out += [here * adjoint, here * passed]
        return tuple(out)

    zero, one = jnp.zeros((CHUNKS, LANES), F32), jnp.ones((CHUNKS, LANES), F32)
    last = lax.fori_loop(0, rows, step, (zero, one) * count, unroll=8)
    for j in range(count):
        first[:, j * LANES : (j + 1) * LANES] = last[2 * j]


def mixer_weights_kernel(parts, normed, *refs):
    d_raw, outs = refs[:parts], refs[parts:]
    deep = normed.shape[1] // parts
    for d in range(parts):
        for k in range(parts):
            outs[d * parts + k][...] = contract_rows(normed[:, d * deep : (d + 1) * deep], d_raw[k][...]).astype(BF)


def out_weights_kernel(y_ref, x_ref, mixed, d_mixed, *refs):
    *outs, full = refs
    y, x = y_ref[0], x_ref[0]
    width = full.shape[1]
    sub, part = mixed.shape[1] // 2, width // CHUNKS
    for k in range(2):
        row = pl.multiple_of((k + y - 2 * k * y) * sub, sub)
        full[...] = contract_rows(mixed[:, pl.ds(row, sub)], d_mixed[:, :width])
        for m in range(2):
            half = m + x - 2 * m * x
            for z in range(Z // 2):
                for there in range(2):
                    near = (there + y - 2 * there * y) * Z + half * (Z // 2) + z
                    at = pl.ds(pl.multiple_of(near * part, part), part)
                    to = (z * 2 + there) * part
                    outs[k * 2 + m][:, to : to + part] = full[:, at].astype(BF)


def d_mixer_kernel(parties, parts, count, copies, x_ref, order, *refs):
    edges, firsts = refs[:parties], refs[parties : 2 * parties]
    refs = refs[2 * parties :]
    local, after, states, entry_own, raw, keep_mask, bound, d_gate_raw = refs[:8]
    refs = refs[8:]
    d_parts, (d_bound, passed, last, entry, d_raw) = refs[:parts], refs[parts:]
    group, feats = raw.shape[0], bound.shape[1]
    rows = group // CHUNKS
    collect(edges, (0, 2), passed)
    collect(firsts, (0, 1), last)
    entries(order, True, count, passed, last, entry)
    base = pl.multiple_of(order[count], CHUNKS)
    copies.wait(*range(2 * parties, 2 * parties + 8))
    top = lax.broadcasted_iota(jnp.int32, (rows, LANES), 0) == 0
    for j in range(feats // LANES):
        lanes = slice(j * LANES, (j + 1) * LANES)
        coming = entry[pl.ds(base, CHUNKS), lanes]
        low = bound[:, lanes]
        total = jnp.zeros((1, LANES), F32)
        for s in range(CHUNKS):
            at = slice(s * rows, (s + 1) * rows)
            adjoint = local[j, at, :] + after[j, at, :] * coming[s : s + 1, :]
            previous = jnp.where(top, entry_own[s : s + 1, lanes], pltpu.roll(states[j, at, :], 1, 0))
            inner = raw[at, lanes]
            sig_inner = jax.nn.sigmoid(inner)
            sig = jax.nn.sigmoid(raw[at, feats + j * LANES : feats + (j + 1) * LANES])
            open_part = (1.0 - low) * (1.0 - sig)
            d_forget = adjoint * (previous * keep_mask[at, :] - inner * sig_inner)
            d_inner = adjoint * open_part * sigmoid_slope(inner, sig_inner)
            d_raw[at, lanes] = d_inner.astype(BF)
            d_raw[at, feats + j * LANES : feats + (j + 1) * LANES] = (d_forget * open_part * sig).astype(BF)
            total = total + jnp.sum(d_forget * (1.0 - sig), axis=0, keepdims=True)
        d_bound[:, lanes] = total
    d_raw[:, 2 * feats :] = d_gate_raw[...]
    for k, d_part in enumerate(d_parts):
        d_part[...] = d_raw[:, columns_of(x_ref, parts, k, 3 * feats // parts)]


def d_normed_kernel(parts, copies, *refs):
    d_parts, weights, partial = refs[:parts], refs[parts:-1], refs[-1]
    group, deep = partial.shape[0], partial.shape[1] // parts
    for d in range(parts):
        copies.wait(*range(parts + d * parts, parts + (d + 1) * parts))
        for i in range(2):
            at = slice(i * group // 2, (i + 1) * group // 2)
            total = None
            for k, d_part in enumerate(d_parts):
                part = times_transposed(d_part[at, :], weights[d * parts + k][...])
                total = part if total is None else total + part
            partial[at, d * deep : (d + 1) * deep] = total.astype(BF)


def token_grad_kernel(summed, tokens, d_resid, gain, out):
    @pl.loop(0, tokens.shape[0] // STEP)
    def _(i):
        at = pl.ds(i * STEP, STEP)
        value = tokens[at, :].astype(F32)
        inv = inverse_rms(value)
        hat = value * inv
        d = summed[at, :].astype(F32) * gain[...]
        out[at, :] = d_resid[at, :] + inv * (d - hat * mean_last(d * hat))


def after(value, *others):
    return lax.optimization_barrier((value, *others))[0]


def gather_rows(own):
    return lax.all_gather(own, ("z", "c"), axis=0, tiled=True)


def scatter_rows(partial):
    return lax.psum_scatter(partial, ("z", "c"), scatter_dimension=0, tiled=True)


def per_device(
    tokens, lengths, w_in, w_forget, w_gate, w_out, attn_gain, mix_gain, bound_table,
    ff_gate, ff_up, ff_down, mlp_gain, out_grad,
):
    Y = lax.axis_size("y")
    pair = Y == 2
    parts = 2 if pair else 1
    z, y, c, x = (lax.axis_index(a) for a in "zycx")
    rows, width = tokens.shape
    sub = w_in.shape[0]
    feats = Y * sub
    block = ff_gate.shape[1] // CHUNKS
    tall = 3 * block
    group = rows * CHUNKS
    near_y = y[None].astype(jnp.int32)

    def y_first(*values):
        if pair:
            return call(
                functools.partial(reorder_kernel, False),
                [(v.shape, v.dtype) for v in values], near_y, *values, smem=1,
            )
        return [
            v.reshape(v.shape[0], Z, Y, C * sub).transpose(0, 2, 1, 3).reshape(v.shape) for v in values
        ]

    def z_first(*values):
        if pair:
            return call(
                functools.partial(reorder_kernel, True),
                [(v.shape, v.dtype) for v in values], near_y, *values, smem=1,
            )
        return [
            v.reshape(v.shape[0], Y, Z, C * sub).transpose(0, 2, 1, 3).reshape(v.shape) for v in values
        ]

    def over_y(value):
        if pair:
            return [value, swap(value, "y")]
        return [lax.all_gather(value, "y", axis=0, tiled=True)]

    def in_order(value):
        if pair:
            other = swap(value, "y")
            return jnp.concatenate(
                [jnp.where(y == 0, value, other), jnp.where(y == 0, other, value)], axis=0
            )
        return lax.all_gather(value, "y", axis=0, tiled=True)

    def spread(value):
        return lax.all_to_all(value, ("z", "c"), 0, 0, tiled=True)

    def both(own, sent, axis):
        return own.astype(BF).astype(F32) + swap(sent.astype(BF), axis).astype(F32)

    near_x = x[None].astype(jnp.int32)
    z_c = jnp.stack([z, c]).astype(jnp.int32)

    def own_and_neighbours(value):
        corner = lax.ppermute(value, ("y", "x"), [(i, 3 - i) for i in range(4)])
        return [value, swap(value, "x"), swap(value, "y"), corner]

    table_f = bound_table.astype(F32)
    soft = jax.nn.softmax(table_f, axis=0)
    own_bound = jnp.sum(soft[1 : LAYER + 1], axis=0)

    if pair:
        (glu,) = call(glu_blocks_kernel, [((CHUNKS, tall, sub), BF)], ff_gate, ff_up, ff_down)
    else:
        glu = jnp.concatenate([w.T.reshape(CHUNKS, block, sub) for w in (ff_gate, ff_up)], axis=1)
        glu = jnp.concatenate([glu, ff_down.reshape(CHUNKS, block, sub)], axis=1)
    (out_rows,) = y_first(in_order(w_out))

    tokens_y, grad_y = y_first(tokens, out_grad)
    if pair:
        (blocks,) = call(
            mixer_blocks_kernel, [((CHUNKS, sub, 3 * feats // 2), BF)], near_x, w_in, w_forget, w_gate, smem=1
        )
        moved = after(spread(blocks), glu, out_rows)
        small = jnp.stack([attn_gain.astype(F32), mlp_gain.astype(F32), own_bound, mix_gain.astype(F32)])
        small = [small, swap(small, "y")]
        (piece,) = call(
            token_piece_kernel, [((rows, width + LANES), BF)],
            near_y, tokens, jnp.concatenate([v[:2] for v in small]), smem=1,
        )
        tokens_all = gather_rows(after(piece, moved))
        gains = tokens_all.reshape(CHUNKS, rows, -1)[:, :4, width:].astype(F32)
        attn_g, mlp_g = (
            jnp.concatenate([gains[:, k].reshape(1, -1), gains[:, 2 + k].reshape(1, -1)], axis=1) for k in range(2)
        )
        small = jnp.stack([v[2:] for v in small])
        small = jnp.where(y == 0, small, small[::-1])
        mixer = own_and_neighbours(moved.reshape(CHUNKS * sub, 3 * feats // 2))
    else:
        gains = lax.all_gather(jnp.stack([attn_gain, mlp_gain]), ("z", "y", "c"), axis=1, tiled=True)
        attn_g, mlp_g = y_first(gains[:1].astype(F32), gains[1:].astype(F32))
        tokens_all = gather_rows(tokens_y)
        small = in_order(jnp.stack([own_bound, mix_gain.astype(F32)])[None])
        mixer = [
            w.reshape(sub, Z, Y, C, sub).transpose(1, 3, 0, 2, 4).reshape(CHUNKS, sub, feats)
            for w in (w_in, w_forget, w_gate)
        ]
        moved = spread(jnp.concatenate(mixer, axis=2))
        mixer = over_y(moved.reshape(CHUNKS * sub, 3 * feats))
    glu = spread(after(glu, moved))
    bound = small[:, 0].reshape(1, feats)
    mix_g = small[:, 1].reshape(1, feats)

    slot = jnp.arange(lengths.shape[0])
    starts = jnp.sum(jnp.where(slot[None, :] < slot[:, None], lengths[None, :], 0), axis=1)
    slot = jnp.arange(CHUNKS)
    chunk = (slot // C * Y + y) * (C * X) + slot % C * X + x
    position = (chunk[:, None] * rows + jnp.arange(rows)[None, :]).reshape(group)
    keep = 1.0 - jnp.any(position[:, None] == starts[None, :], axis=1).astype(F32)[:, None]
    count = Z * Y * C * X
    number = jnp.arange(count)
    xn, cn = number % X, number // X % C
    yn, zn = number // (X * C) % Y, number // (X * C * Y)
    party = (yn ^ y) * X + (xn ^ x) if pair else yn * X + xn
    order = party * CHUNKS + zn * C + cn
    base = 0 * y if pair else (y * X + x) * CHUNKS
    order = jnp.concatenate([order, jnp.stack([base, z * C + c])]).astype(jnp.int32)

    def parties(value):
        if pair:
            return own_and_neighbours(value)
        return [lax.all_gather(value, ("y", "x"), axis=0, tiled=True)]

    crowd = 4 if pair else 1
    featured = ((feats // LANES, group, LANES), F32)
    normed, raw, decay, local, through, edge = call(
        functools.partial(mixer_forward_kernel, parts),
        [((group, width), BF), ((group, 3 * feats), F32)] + [featured] * 3 + [((2 * CHUNKS, feats), F32)],
        near_x, attn_g, tokens_all, bound, keep, *mixer,
        smem=1, scratch=[pltpu.VMEM(*featured)], late=2,
    )
    edges = parties(edge)
    def assemble(pieces):
        return jnp.concatenate([p.transpose(1, 0, 2).reshape(p.shape[1], -1) for p in pieces], axis=1)

    def around(blocks):
        cut = blocks.shape[1] // 2
        side, up_y = swap(blocks, "x"), swap(blocks, "y")
        corner = [swap(up_y[:, :cut], "x"), swap(side[:, cut:], "y")]
        near, far = assemble([blocks, up_y]), assemble([side, jnp.concatenate(corner, axis=1)])
        return [near, far], (side, up_y), corner

    early, late, last = (), (), ()
    gate_up, down = glu[:, : 2 * block], glu[:, 2 * block :]
    if pair:
        gate_up_w, early, _ = around(after(gate_up, edges[0]))
        down_w, late, last = around(after(down, *early))
    else:
        gate_up_w, down_w = (assemble(over_y(v)) for v in (gate_up, down))
        gate_up_w, down_w = ([v, swap(v, "x")] for v in (gate_up_w, down_w))
    carries = [pltpu.VMEM((Y * X * CHUNKS, feats), F32)] * 3
    states, entry, partial = call(
        functools.partial(mixer_out_kernel, crowd, count),
        [featured, ((CHUNKS, feats), F32), ((group, width + LANES), BF)],
        order, *edges, local, through, raw, mix_g, out_rows,
        smem=1, scratch=carries + [pltpu.VMEM((group, feats), BF)], late=crowd,
    )
    summed = scatter_rows(after(partial, glu))
    own_grad = lax.all_to_all(jnp.broadcast_to(after(grad_y, glu)[None], (Z, rows, width)), "z", 0, 0, tiled=False)
    other_grad = swap(own_grad, "c")
    grad_all = jnp.where(
        c == 0, jnp.stack([own_grad, other_grad], axis=1), jnp.stack([other_grad, own_grad], axis=1)
    ).reshape(group, width)
    resid, hidden, scale = call(
        resid_kernel,
        [((rows, width), F32), ((rows, width), BF), ((rows, LANES), F32)],
        after(summed, own_grad, *early, *late), tokens_y, mlp_g,
    )
    hidden_all = after(gather_rows(hidden), grad_all)
    thin = ((group, block), BF)
    act0, d_gate0, d_up0, act1, d_gate1, d_up1, partial = call(
        glu_kernel, [thin] * 6 + [((group, 2 * width), BF)],
        hidden_all, grad_all, *gate_up_w, *down_w, late=0, scratch=[pltpu.VMEM((group, 2 * width), F32)],
    )
    acts = [act0, act1]

    def weight_pieces(terms, lefts, *rights):
        height = len(terms) * block
        shapes = [((height, width), BF)] * 2
        if pair:
            shapes = [((2, height // 2, width // 2), BF)] * 4
        return call(
            functools.partial(glu_weights_kernel, parts, terms), shapes, *lefts, *rights,
        )

    def first_swaps(pieces):
        upper, upper_sent, lower, lower_sent = pieces
        return upper, swap(upper_sent, "x"), lower, swap(lower_sent, "y")

    def first_sums(pieces):
        height = pieces[0].shape[1]
        shapes = [((height, width // 2), F32), ((height, width // 2), BF)] * 2
        return call(first_sums_kernel, shapes, *pieces)

    def last_swaps(pieces):
        upper, upper_sent, lower, lower_sent = pieces
        return upper, swap(upper_sent, "y"), lower, swap(lower_sent, "x")

    def last_sums(*pieces):
        height = sum(p.shape[0] for p in pieces[::2])
        return call(last_sums_kernel, [((CHUNKS, height, sub), BF)], *pieces)[0]

    def to_blocks(value):
        return value.reshape(value.shape[0], -1, sub).transpose(1, 0, 2)

    def total_blocks(pieces):
        blocks = to_blocks(both(*pieces, "x").astype(BF))
        return lax.psum_scatter(blocks, "y", scatter_dimension=0, tiled=True)

    summed = scatter_rows(partial)
    gate_up = weight_pieces((0, 0), [d_gate0, d_up0, d_gate1, d_up1], hidden_all)
    down = weight_pieces((0,), acts, grad_all)
    if pair:
        gate_up = first_sums(first_swaps(gate_up))
        down = first_swaps(down)
        summed, *gate_up = lax.optimization_barrier((summed, *gate_up))
    d_resid, piece, result_y = call(
        d_resid_kernel, [((rows, width), F32), ((rows, width + LANES), BF), ((rows, width), BF)],
        summed, resid, tokens_y, grad_y, mlp_g, scale,
    )
    if pair:
        piece, *down = lax.optimization_barrier((piece, *down))
    d_mixed = gather_rows(piece)
    if pair:
        gate_up = last_swaps(gate_up)
        down = last_swaps(first_sums(down))
        glu_grad = last_sums(*gate_up, *down)
        d_mixed, glu_grad = lax.optimization_barrier((d_mixed, glu_grad))

    mixed_in, d_gate_raw, adjoint, passed, first = call(
        mixer_back_kernel,
        [((group, feats), BF)] * 2 + [featured] * 2 + [((CHUNKS, feats), F32)],
        d_mixed, out_rows, raw, states, mix_g, decay,
        scratch=[pltpu.VMEM((group, feats), F32), pltpu.VMEM(*featured)], late=2,
    )
    firsts = parties(first)
    grad_out = mixed_in
    if pair:
        out_pieces = call(
            out_weights_kernel, [((sub, width // 2), BF)] * 4,
            near_y, near_x, mixed_in, d_mixed, smem=2, scratch=[pltpu.VMEM((sub, width), F32)],
        )
        out_pieces = after(out_pieces, *firsts)
        grad_out = sum(
            p.astype(F32)
            for p in (
                out_pieces[0],
                swap(out_pieces[1], "x"),
                swap(out_pieces[2], "y"),
                lax.ppermute(out_pieces[3], ("y", "x"), [(i, 3 - i) for i in range(4)]),
            )
        ).astype(BF)
    if pair:
        glu_grad = after(glu_grad, first)
    else:
        glu_grad = jnp.concatenate([total_blocks(gate_up), total_blocks(down)], axis=1)
    glu_grad = spread(glu_grad)
    *d_raw, part_bound = call(
        functools.partial(d_mixer_kernel, crowd, parts, count),
        [((group, 3 * feats // parts), BF)] * parts
        + [((1, feats), F32)],
        near_x, order, *edges, *firsts, adjoint, passed, states, entry, raw, keep, bound, d_gate_raw,
        smem=2, scratch=carries + [pltpu.VMEM((group, 3 * feats), BF)], late=2 * crowd,
    )

    pieces = call(
        functools.partial(mixer_weights_kernel, parts),
        [((width // parts, 3 * feats // parts), BF)] * parts**2,
        normed, *d_raw,
    )
    (partial,) = call(
        functools.partial(d_normed_kernel, parts), [((group, width), BF)],
        *after(d_raw, grad_out, *pieces), *mixer, late=parts,
    )
    (token_grad_y,) = call(
        token_grad_kernel, [((rows, width), F32)],
        scatter_rows(partial), tokens_y, d_resid, attn_g,
    )
    result, token_grad = z_first(result_y, token_grad_y)

    part_bound = part_bound.reshape(feats)
    if pair:
        pieces = [
            pieces[0],
            swap(pieces[1], "x"),
            swap(pieces[2], "y"),
            lax.ppermute(pieces[3], ("y", "x"), [(i, 3 - i) for i in range(4)]),
        ]
        top, bottom = jnp.split(part_bound, 2)
        d_bound = jnp.where(y == 0, top, bottom) + swap(jnp.where(y == 0, bottom, top), "y")
        pieces = after(pieces, d_bound)
        shape = (2, sub, 3 * feats // 2)
        theirs, *mine = call(
            mixer_sums_kernel, [((Z, *shape[1:]), BF)] + [(shape, BF)] * Z, z_c, *pieces, smem=1
        )
        got = swap(theirs, "c")
        d_bound = after(d_bound, got)
        mine = [v.at[1].set(got[k]) for k, v in enumerate(mine)]
        mixer_grad = [mine[0]] + [lax.ppermute(mine[k], "z", [(i, i ^ k) for i in range(Z)]) for k in range(1, Z)]
    else:
        d_bound = lax.psum_scatter(part_bound, "y", scatter_dimension=0, tiled=True)
        mixer_grad = lax.psum_scatter(pieces[0], "y", scatter_dimension=0, tiled=True)
        mixer_grad = both(mixer_grad, mixer_grad, "x").astype(BF)
        mixer_grad = spread(mixer_grad.reshape(CHUNKS, sub, 3 * feats))
    if pair:
        grad_gate_ff, grad_up_ff, grad_down, along_ff = call(
            glu_grads_kernel,
            [((sub, CHUNKS * block), F32)] * 2 + [((CHUNKS * block, sub), F32), ((sub, LANES), F32)],
            glu_grad, ff_gate, ff_up,
        )
        grad_mlp = along_ff[:, 0]
        grad_mlp = grad_mlp + swap(grad_mlp, "x")
        d_bound = d_bound + swap(d_bound, "x")
        mixer_grad[-1] = after(mixer_grad[-1], grad_out, d_bound, grad_mlp)
        mixer_grad = mixer_grad + [swap(v, "x") for v in mixer_grad]
        other = swap(grad_out, "x")
        grad_out = jnp.concatenate(
            [jnp.where(x == 0, grad_out, other), jnp.where(x == 0, other, grad_out)], axis=1
        ).astype(F32)
    else:
        (grad_out,) = z_first(contract_rows(mixed_in, d_mixed[:, :width]).astype(BF))
        grad_out = lax.psum_scatter(grad_out, "y", scatter_dimension=0, tiled=True)
        grad_out = both(grad_out, grad_out, "x")
        d_bound = d_bound + swap(d_bound, "x")
    row_ids = jnp.arange(bound_table.shape[0])[:, None]
    member = jnp.logical_and(row_ids >= 1, row_ids <= LAYER).astype(F32)
    grad_table = soft * (member - own_bound[None, :]) * d_bound[None, :]

    def along(weight, grad):
        return jnp.sum(weight.astype(F32) * grad, axis=1)

    square = ((sub, width), F32)
    if pair:
        grad_in, grad_forget, grad_gate, grad_attn = call(
            mixer_grads_kernel, [square] * 3 + [((sub, LANES), F32)],
            jnp.concatenate([near_x, z_c]), *mixer_grad, w_in, w_forget, w_gate, smem=1,
        )
        grad_attn = grad_attn[:, 0]
    else:
        mixer_grad = mixer_grad.reshape(Z, C, sub, 3, Y, sub).transpose(3, 2, 0, 4, 1, 5)
        grad_in, grad_forget, grad_gate = mixer_grad.reshape(3, sub, width).astype(F32)
        grad_attn = along(w_in, grad_in) + along(w_forget, grad_forget) + along(w_gate, grad_gate)
        grad_gate_ff, grad_up_ff = (
            glu_grad[:, k * block : (k + 1) * block].astype(F32).reshape(CHUNKS * block, sub).T for k in range(2)
        )
        grad_down = glu_grad[:, 2 * block :].reshape(CHUNKS * block, sub).astype(F32)
        grad_mlp = along(ff_gate, grad_gate_ff) + along(ff_up, grad_up_ff)
        grad_mlp = grad_mlp + swap(grad_mlp, "x")
    grad_attn = grad_attn / attn_gain.astype(F32)
    grad_mix = along(w_out, grad_out) / mix_gain.astype(F32)
    grad_mlp = grad_mlp / mlp_gain.astype(F32)
    return (
        result, token_grad, grad_in, grad_forget, grad_gate, grad_out, grad_attn, grad_mix,
        grad_table, grad_gate_ff, grad_up_ff, grad_down, grad_mlp,
    )


def solution(mesh):
    dp, mp = mesh.devices.shape
    grid = Mesh(mesh.devices.reshape(Z, dp // CHUNKS, C, mp), ("z", "y", "c", "x"))
    dp_axes = ("z", "y", "c")
    every = ("z", "y", "c", "x")
    mat, row, gain = P(dp_axes, None), P(every, None), P(dp_axes)
    table, glu, glu_down = P(None, dp_axes), P(dp_axes, "x"), P("x", dp_axes)
    return jax.shard_map(
        per_device,
        mesh=grid,
        in_specs=(
            row, P(), mat, mat, mat, mat, gain, gain, table, glu, glu, glu_down, gain, row,
        ),
        out_specs=(
            row, row, mat, mat, mat, mat, gain, gain, table, glu, glu, glu_down, gain,
        ),
        check_vma=False,
    )
```

```python
import functools

import jax
import jax.numpy as jnp
from jax import lax
from jax.experimental import pallas as pl
from jax.experimental.pallas import tpu as pltpu
from jax.sharding import Mesh, PartitionSpec as P

LAYER = 12
Z, C, X = 4, 2, 2
CHUNKS = Z * C
LANES = 128
epsilon = 1e-06
VMEM_LIMIT = 56 << 20
BF, F32 = jnp.bfloat16, jnp.float32


def swap(value, axis):
    return lax.ppermute(value, axis, [(0, 1), (1, 0)])


def dot(left, right):
    return jnp.dot(left, right, preferred_element_type=F32)


def contract_rows(left, right):
    return lax.dot_general(left, right, (((0,), (0,)), ((), ())), preferred_element_type=F32)


def times_transposed(left, right):
    return lax.dot_general(left, right, (((1,), (1,)), ((), ())), preferred_element_type=F32)


def mean_last(value):
    return jnp.mean(value, axis=-1, keepdims=True)


def inverse_rms(value):
    return lax.rsqrt(mean_last(value * value) + epsilon)


def sigmoid_slope(raw, sig):
    return sig * (1.0 + raw * (1.0 - sig))


class Copies:
    def __init__(self, inputs, outputs):
        self.inputs, self.outputs, self.waited, self.flushed = inputs, outputs, set(), set()
        for copy in inputs:
            copy.start()

    def wait(self, *numbers):
        for k in numbers:
            if k not in self.waited:
                self.waited.add(k)
                self.inputs[k].wait()

    def flush(self, *numbers):
        for k in numbers:
            if k not in self.flushed:
                self.flushed.add(k)
                self.outputs[k].start()


def call(kernel, outs, *ins, smem=0, scratch=(), late=None):
    n_in, n_out = len(ins) - smem, len(outs)

    def body(*refs):
        scalars, refs = refs[:smem], refs[smem:]
        far_in, far_out, refs = refs[:n_in], refs[n_in : n_in + n_out], refs[n_in + n_out :]
        near_in, near_out, refs = refs[:n_in], refs[n_in : n_in + n_out], refs[n_in + n_out :]
        *own, in_sems, out_sems = refs
        copies = Copies(
            [pltpu.make_async_copy(f, n, in_sems.at[k]) for k, (f, n) in enumerate(zip(far_in, near_in))],
            [pltpu.make_async_copy(n, f, out_sems.at[k]) for k, (f, n) in enumerate(zip(far_out, near_out))],
        )
        copies.wait(*range(n_in if late is None else late))
        kernel(*([] if late is None else [copies]), *scalars, *near_in, *near_out, *own)
        copies.wait(*range(n_in))
        copies.flush(*range(n_out))
        for copy in copies.outputs:
            copy.wait()

    shapes = [jax.ShapeDtypeStruct(s, t) for s, t in outs]
    near = [pltpu.VMEM(v.shape, v.dtype) for v in list(ins[smem:]) + shapes]
    return pl.pallas_call(
        body,
        out_shape=shapes,
        in_specs=[pl.BlockSpec(memory_space=pltpu.SMEM)] * smem + [pl.BlockSpec(memory_space=pl.ANY)] * n_in,
        out_specs=[pl.BlockSpec(memory_space=pl.ANY)] * n_out,
        scratch_shapes=near
        + list(scratch)
        + [pltpu.SemaphoreType.DMA((n_in,)), pltpu.SemaphoreType.DMA((n_out,))],
        compiler_params=pltpu.CompilerParams(vmem_limit_bytes=VMEM_LIMIT),
        cost_estimate=pl.CostEstimate(flops=0, bytes_accessed=1024, transcendentals=0),
    )(*ins)


def stat_block(columns, first=0):
    rows = columns[0].shape[0]
    lane = lax.broadcasted_iota(jnp.int32, (rows, LANES), 1) - first
    block = jnp.zeros((rows, LANES), F32)
    for k, column in enumerate(columns):
        high = column.astype(BF).astype(F32)
        block = jnp.where(lane == 2 * k, high, block)
        block = jnp.where(lane == 2 * k + 1, column - high, block)
    return block


def stat(block, k):
    lane = lax.broadcasted_iota(jnp.int32, block.shape, 1)
    picked = jnp.where((lane == 2 * k) | (lane == 2 * k + 1), block.astype(F32), 0.0)
    return jnp.sum(picked, axis=1, keepdims=True)


def reorder_kernel(back, y_ref, *refs):
    y = y_ref[0]
    half = len(refs) // 2
    for in_ref, out_ref in zip(refs[:half], refs[half:]):
        width = in_ref.shape[1] // CHUNKS
        for k in range(2):
            there = k + y - 2 * k * y
            for z in range(Z):
                near = slice((k * Z + z) * width, (k * Z + z + 1) * width)
                far = pl.ds(pl.multiple_of((z * 2 + there) * width, width), width)
                if back:
                    out_ref[:, far] = in_ref[:, near]
                else:
                    out_ref[:, near] = in_ref[:, far]


def token_piece_kernel(y_ref, tokens, gains, piece):
    width = tokens.shape[1]
    reorder_kernel(False, y_ref, tokens, piece.at[:, :width])
    row = lax.broadcasted_iota(jnp.int32, (tokens.shape[0], LANES), 0)
    block = jnp.zeros((tokens.shape[0], LANES), F32)
    for k in range(gains.shape[0]):
        block = jnp.where(row == k, gains[k : k + 1, :], block)
    piece[:, width:] = block.astype(BF)


def mixer_blocks_kernel(x_ref, *refs):
    *weights, out_ref = refs
    half = len(weights)
    x = x_ref[0]
    for z in range(Z):
        for c in range(C):
            for k in range(half):
                pieces = []
                for j in (k, half + k):
                    at = ((z * 2 + j % 2) * C + c) * LANES
                    pieces.append(weights[j // 2][:, at : at + LANES])
                out_ref[z * C + c, :, k * LANES : (k + 1) * LANES] = jnp.where(x == 0, *pieces)


def mixer_sums_kernel(at_ref, *refs):
    pieces, theirs, mine = refs[:4], refs[4], refs[5:]
    z, c = at_ref[0], at_ref[1]
    sub = theirs.shape[1]
    for k in range(Z):
        bits = [(z // 2 + k // 2) % 2, (z + k) % 2]
        for other in range(2):
            core = c + other - 2 * c * other
            row = pl.ds(pl.multiple_of(((bits[0] * 2 + bits[1]) * 2 + core) * sub, sub), sub)
            total = pieces[0][row, :].astype(F32)
            for p in pieces[1:]:
                total = total + p[row, :].astype(F32)
            if other:
                theirs[k] = total.astype(BF)
            else:
                mine[k][0] = total.astype(BF)
                mine[k][1] = jnp.zeros(theirs.shape[1:], BF)


def mixer_grads_kernel(copies, at_ref, *refs):
    mine, theirs, refs = refs[:Z], refs[Z : 2 * Z], refs[2 * Z :]
    w_in, w_forget, w_gate, grad_in, grad_forget, grad_gate, along_ref = refs
    x, z, c = at_ref[0], at_ref[1], at_ref[2]
    total = jnp.zeros((w_in.shape[0], 1), F32)
    for m, (w_ref, g_ref) in enumerate(((w_in, grad_in), (w_forget, grad_forget), (w_gate, grad_gate))):
        for k in range(Z):
            there = (z // 2 + k // 2) % 2 * 2 + (z + k) % 2
            for y in range(2):
                for other in range(2):
                    core = c + other - 2 * c * other
                    j = m * 2 + y
                    to = pl.ds(pl.multiple_of(((there * 2 + y) * C + core) * LANES, LANES), LANES)
                    at = j % 3 * LANES
                    piece = jnp.where(
                        x == j // 3,
                        mine[k][other, :, at : at + LANES],
                        theirs[k][other, :, at : at + LANES],
                    ).astype(F32)
                    g_ref[:, to] = piece
                    weight = w_ref[:, to].astype(F32)
                    total = total + jnp.sum(piece * weight, axis=1, keepdims=True)
        copies.flush(m)
    along_ref[...] = jnp.broadcast_to(total, along_ref.shape)


def glu_blocks_kernel(gate_ref, up_ref, down_ref, out_ref):
    block = down_ref.shape[0] // CHUNKS
    for s in range(CHUNKS):
        at = slice(s * block, (s + 1) * block)
        out_ref[s, :block] = gate_ref[:, at].astype(F32).T.astype(BF)
        out_ref[s, block : 2 * block] = up_ref[:, at].astype(F32).T.astype(BF)
        out_ref[s, 2 * block :] = down_ref[at, :]


def glu_grads_kernel(blocks_ref, w_gate, w_up, grad_gate, grad_up, grad_down, along_ref):
    block = blocks_ref.shape[1] // 3
    total = jnp.zeros((w_gate.shape[0], 1), F32)
    for s in range(CHUNKS):
        at = slice(s * block, (s + 1) * block)
        for m, (w_ref, g_ref) in enumerate(((w_gate, grad_gate), (w_up, grad_up))):
            piece = blocks_ref[s, m * block : (m + 1) * block].astype(F32).T
            g_ref[:, at] = piece
            total = total + jnp.sum(piece * w_ref[:, at].astype(F32), axis=1, keepdims=True)
        grad_down[at, :] = blocks_ref[s, 2 * block :].astype(F32)
    along_ref[...] = jnp.broadcast_to(total, along_ref.shape)


def columns_of(x_ref, parts, k, span):
    if parts == 1:
        return slice(0, span)
    return pl.ds(pl.multiple_of((k + x_ref[0] - 2 * k * x_ref[0]) * span, LANES), span)


def mixer_forward_kernel(parts, copies, x_ref, *refs):
    gain, tokens, bound, keep = refs[:4]
    weights = refs[4 : 4 + parts * parts]
    normed, raw, decay, local, through, edge, drive = refs[4 + parts * parts :]
    group, feats = raw.shape[0], bound.shape[1]
    width = gain.shape[1]
    rows = group // CHUNKS

    @pl.loop(0, group // 32)
    def _(i):
        at = pl.ds(i * 32, 32)
        value = tokens[at, :width].astype(F32)
        normed[at, :] = (value * inverse_rms(value) * gain[...]).astype(BF)

    copies.flush(0)
    copies.wait(*range(2, 4 + parts * parts))

    @pl.loop(0, 2)
    def _(i):
        at = pl.ds(i * (group // 2), group // 2)
        deep, span = width // parts, 3 * feats // parts
        for k in range(parts):
            total = None
            for d in range(parts):
                part = dot(normed[at, d * deep : (d + 1) * deep], weights[d * parts + k][...])
                total = part if total is None else total + part
            raw[at, columns_of(x_ref, parts, k, span)] = total

    copies.flush(1)
    count = feats // LANES

    @pl.loop(0, CHUNKS)
    def _(i):
        at = pl.ds(i * rows, rows)
        for j in range(count):
            lanes = slice(j * LANES, (j + 1) * LANES)
            inner = raw[at, lanes]
            forget_raw = raw[at, feats + j * LANES : feats + (j + 1) * LANES]
            low = bound[:, lanes]
            forget = low + (1.0 - low) * jax.nn.sigmoid(forget_raw)
            drive[j, at, :] = inner * jax.nn.sigmoid(inner) * (1.0 - forget)
            decay[j, at, :] = forget * keep[at, :]

    copies.flush(2)

    def step(t, carry):
        out = []
        at = pl.ds(t, CHUNKS, stride=rows)
        for j in range(count):
            state, passed = carry[2 * j], carry[2 * j + 1]
            here = decay[j, at, :]
            state = here * state + drive[j, at, :]
            passed = here * passed
            local[j, at, :] = state
            through[j, at, :] = passed
            out += [state, passed]
        return tuple(out)

    zero, one = jnp.zeros((CHUNKS, LANES), F32), jnp.ones((CHUNKS, LANES), F32)
    last = lax.fori_loop(0, rows, step, (zero, one) * count, unroll=8)
    for j in range(count):
        edge[:CHUNKS, j * LANES : (j + 1) * LANES] = last[2 * j + 1]
        edge[CHUNKS:, j * LANES : (j + 1) * LANES] = last[2 * j]


def entries(order, backwards, count, passed, last, entry):
    def step(n, running):
        row = pl.ds(order[count - 1 - n if backwards else n], 1)
        entry[row, :] = running
        return passed[row, :] * running + last[row, :]

    lax.fori_loop(0, count, step, jnp.zeros((1, last.shape[1]), F32))


def collect(parties, at, to):
    base = 0
    for p in parties:
        for g in range(p.shape[0] // (at[1] * CHUNKS)):
            begin = (g * at[1] + at[0]) * CHUNKS
            to[base : base + CHUNKS, :] = p[begin : begin + CHUNKS, :]
            base += CHUNKS


def mixer_out_kernel(parties, count, copies, order, *refs):
    edges = refs[:parties]
    local, through, raw, mix_gain, out_w = refs[parties : parties + 5]
    states, entry_own, partial, passed, last, entry, mixed = refs[parties + 5 :]
    group, feats = raw.shape[0], mix_gain.shape[1]
    width = out_w.shape[1]
    rows = group // CHUNKS
    collect(edges, (0, 2), passed)
    collect(edges, (1, 2), last)
    entries(order, False, count, passed, last, entry)
    base = order[count]
    entry_own[...] = entry[pl.ds(pl.multiple_of(base, CHUNKS), CHUNKS), :]
    copies.wait(*range(parties, parties + 4))
    for s in range(CHUNKS):
        at = slice(s * rows, (s + 1) * rows)
        total = jnp.zeros((rows, LANES), F32)
        for j in range(feats // LANES):
            lanes = slice(j * LANES, (j + 1) * LANES)
            state = local[j, at, :] + through[j, at, :] * entry_own[s : s + 1, lanes]
            gate = raw[at, 2 * feats + j * LANES : 2 * feats + (j + 1) * LANES]
            mixed[at, lanes] = (state * (mix_gain[:, lanes] * (gate * jax.nn.sigmoid(gate)))).astype(BF)
            states[j, at, :] = state
            total = total + state * state
        squares = jnp.sum(total, axis=1, keepdims=True)
        partial[at, width:] = stat_block([squares], 2 * order[count + 1]).astype(BF)
    copies.flush(0)
    copies.wait(parties + 4)
    for k in range(2):
        at = slice(k * group // 2, (k + 1) * group // 2)
        partial[at, :width] = dot(mixed[at, :], out_w[...]).astype(BF)


STEP = 16


def resid_kernel(summed, tokens, gain, resid, hidden, scale):
    width = tokens.shape[1]

    @pl.loop(0, tokens.shape[0] // STEP)
    def _(i):
        at = pl.ds(i * STEP, STEP)
        squares = jnp.sum(summed[at, width:].astype(F32), axis=1, keepdims=True)
        q = lax.rsqrt(squares / width + epsilon)
        value = tokens[at, :].astype(F32) + q * summed[at, :width].astype(F32)
        resid[at, :] = value
        hidden[at, :] = (value * inverse_rms(value) * gain[...]).astype(BF)
        scale[at, :] = jnp.broadcast_to(q, (STEP, LANES))


def glu_kernel(copies, hidden, grad, *refs):
    weights, outs, partial, total = refs[:4], refs[4:10], refs[10], refs[11]
    group, block = outs[0].shape
    width = hidden.shape[1]
    for k in range(2):
        gate_up, down = weights[k], weights[2 + k]
        act, d_gate, d_up = outs[3 * k : 3 * k + 3]
        w_gate, w_up = gate_up.at[:block, :], gate_up.at[block:, :]
        copies.wait(0, 2 + k)
        for i in range(2):
            at = slice(i * group // 2, (i + 1) * group // 2)
            gate = times_transposed(hidden[at, :], w_gate[...])
            up = times_transposed(hidden[at, :], w_up[...])
            copies.wait(1, 4 + k)
            d_act = times_transposed(grad[at, :], down[...])
            sig = jax.nn.sigmoid(gate)
            silu = gate * sig
            act[at, :] = (silu * up).astype(BF)
            d_gate[at, :] = (d_act * up * sigmoid_slope(gate, sig)).astype(BF)
            d_up[at, :] = (d_act * silu).astype(BF)
            back = dot(d_gate[at, :], w_gate[...]) + dot(d_up[at, :], w_up[...])
            for cols, value in ((slice(0, width), back), (slice(width, None), dot(act[at, :], down[...]))):
                if k == 0:
                    total[at, cols] = value
                else:
                    partial[at, cols] = (total[at, cols] + value).astype(BF)
        copies.flush(3 * k, 3 * k + 1, 3 * k + 2)


def glu_weights_kernel(parts, terms, copies, *refs):
    count = len(terms)
    lefts, rights, outs = refs[: 2 * count], refs[2 * count : 2 * count + max(terms) + 1], None
    outs = refs[2 * count + max(terms) + 1 :]
    block = lefts[0].shape[1]
    part = rights[0].shape[1] // parts
    cut = count * block // 2
    for k in range(2):
        for m, right in enumerate(terms):
            begin, end = m * block, (m + 1) * block
            for d in range(parts):
                value = contract_rows(lefts[k * count + m][...], rights[right][:, d * part : (d + 1) * part])
                value = value.astype(BF)
                if parts == 1:
                    outs[k][begin:end, :] = value
                    continue
                upper, lower = outs[k], outs[2 + d]
                if begin < cut:
                    upper[d, begin : min(end, cut)] = value[: min(end, cut) - begin]
                if d == parts - 1 and cut <= end and begin < cut:
                    copies.flush(k)
                if end > cut:
                    lower[k, max(begin, cut) - cut : end - cut] = value[max(begin, cut) - begin :]


def first_sums_kernel(upper, upper_got, lower, lower_got, upper_keep, upper_send, lower_keep, lower_send):
    for mine, got, keep, send in (
        (upper, upper_got, upper_keep, upper_send),
        (lower, lower_got, lower_keep, lower_send),
    ):
        keep[...] = mine[0].astype(F32) + got[0].astype(F32)
        send[...] = (mine[1].astype(F32) + got[1].astype(F32)).astype(BF)


def last_sums_kernel(*refs):
    *pieces, blocks = refs
    begin = 0
    for mine, got in zip(pieces[::2], pieces[1::2]):
        for s in range(CHUNKS):
            cols = slice(s * LANES, (s + 1) * LANES)
            blocks[s, begin : begin + mine.shape[0]] = (mine[:, cols] + got[:, cols].astype(F32)).astype(BF)
        begin += mine.shape[0]


def d_resid_kernel(summed, resid, tokens, grad, gain, scale, d_resid, piece, result):
    width = tokens.shape[1]

    @pl.loop(0, tokens.shape[0] // STEP)
    def _(i):
        at = pl.ds(i * STEP, STEP)
        d_hidden = summed[at, :width].astype(F32) * gain[...]
        value = resid[at, :]
        inv = inverse_rms(value)
        hat = value * inv
        d_value = grad[at, :].astype(F32) + inv * (d_hidden - hat * mean_last(d_hidden * hat))
        d_resid[at, :] = d_value
        result[at, :] = (value + summed[at, width:].astype(F32)).astype(BF)
        low = d_value.astype(BF)
        piece[at, :width] = low
        mean = mean_last(low.astype(F32) * (value - tokens[at, :].astype(F32)))
        piece[at, width:] = stat_block([scale[at, :1], mean]).astype(BF)


def mixer_back_kernel(copies, d_mixed, out_w, raw, states, mix_gain, decay, *refs):
    mixed, d_gate_raw, local, after, first, d_mixin, d_states = refs
    width = out_w.shape[1]
    group, feats = raw.shape[0], mix_gain.shape[1]
    rows = group // CHUNKS
    count = feats // LANES
    for k in range(2):
        at = slice(k * group // 2, (k + 1) * group // 2)
        d_mixin[at, :] = times_transposed(d_mixed[at, :width], out_w[...])
    copies.wait(2, 3, 4, 5)
    for s in range(CHUNKS):
        at = slice(s * rows, (s + 1) * rows)
        stats = d_mixed[at, width:]
        q, mean = stat(stats, 0), stat(stats, 1)
        for j in range(count):
            lanes = slice(j * LANES, (j + 1) * LANES)
            hat = states[j, at, :] * q
            gate = raw[at, 2 * feats + j * LANES : 2 * feats + (j + 1) * LANES]
            sig = jax.nn.sigmoid(gate)
            silu = gate * sig
            gain = mix_gain[:, lanes]
            d = d_mixin[at, lanes] * gain
            mixed[at, lanes] = (hat * gain * silu).astype(BF)
            d_gate_raw[at, lanes] = (d * hat * sigmoid_slope(gate, sig)).astype(BF)
            d_states[j, at, :] = q * (d * silu - hat * mean)
    copies.flush(0, 1)

    def step(t, carry):
        out = []
        at = pl.ds(rows - 1 - t, CHUNKS, stride=rows)
        for j in range(count):
            coming, passed = carry[2 * j], carry[2 * j + 1]
            here = decay[j, at, :]
            adjoint = d_states[j, at, :] + coming
            local[j, at, :] = adjoint
            after[j, at, :] = passed
            out += [here * adjoint, here * passed]
        return tuple(out)

    zero, one = jnp.zeros((CHUNKS, LANES), F32), jnp.ones((CHUNKS, LANES), F32)
    last = lax.fori_loop(0, rows, step, (zero, one) * count, unroll=8)
    for j in range(count):
        first[:, j * LANES : (j + 1) * LANES] = last[2 * j]


def mixer_weights_kernel(parts, copies, normed, *refs):
    d_raw, outs = refs[:parts], refs[parts:]
    deep = normed.shape[1] // parts
    for d in range(parts):
        for k in range(parts):
            outs[d * parts + k][...] = contract_rows(normed[:, d * deep : (d + 1) * deep], d_raw[k][...]).astype(BF)
            copies.flush(d * parts + k)


def out_weights_kernel(y_ref, x_ref, mixed, d_mixed, *refs):
    *outs, full = refs
    y, x = y_ref[0], x_ref[0]
    width = full.shape[1]
    sub, part = mixed.shape[1] // 2, width // CHUNKS
    for k in range(2):
        row = pl.multiple_of((k + y - 2 * k * y) * sub, sub)
        full[...] = contract_rows(mixed[:, pl.ds(row, sub)], d_mixed[:, :width])
        for m in range(2):
            half = m + x - 2 * m * x
            for z in range(Z // 2):
                for there in range(2):
                    near = (there + y - 2 * there * y) * Z + half * (Z // 2) + z
                    at = pl.ds(pl.multiple_of(near * part, part), part)
                    to = (z * 2 + there) * part
                    outs[k * 2 + m][:, to : to + part] = full[:, at].astype(BF)


def d_mixer_kernel(parties, parts, count, copies, x_ref, order, *refs):
    edges, firsts = refs[:parties], refs[parties : 2 * parties]
    refs = refs[2 * parties :]
    local, after, states, entry_own, raw, keep_mask, bound, d_gate_raw = refs[:8]
    refs = refs[8:]
    d_parts, (d_bound, passed, last, entry, d_raw) = refs[:parts], refs[parts:]
    group, feats = raw.shape[0], bound.shape[1]
    rows = group // CHUNKS
    collect(edges, (0, 2), passed)
    collect(firsts, (0, 1), last)
    entries(order, True, count, passed, last, entry)
    base = pl.multiple_of(order[count], CHUNKS)
    copies.wait(*range(2 * parties, 2 * parties + 8))
    top = lax.broadcasted_iota(jnp.int32, (rows, LANES), 0) == 0
    for j in range(feats // LANES):
        lanes = slice(j * LANES, (j + 1) * LANES)
        coming = entry[pl.ds(base, CHUNKS), lanes]
        low = bound[:, lanes]
        total = jnp.zeros((1, LANES), F32)
        for s in range(CHUNKS):
            at = slice(s * rows, (s + 1) * rows)
            adjoint = local[j, at, :] + after[j, at, :] * coming[s : s + 1, :]
            previous = jnp.where(top, entry_own[s : s + 1, lanes], pltpu.roll(states[j, at, :], 1, 0))
            inner = raw[at, lanes]
            sig_inner = jax.nn.sigmoid(inner)
            sig = jax.nn.sigmoid(raw[at, feats + j * LANES : feats + (j + 1) * LANES])
            open_part = (1.0 - low) * (1.0 - sig)
            d_forget = adjoint * (previous * keep_mask[at, :] - inner * sig_inner)
            d_inner = adjoint * open_part * sigmoid_slope(inner, sig_inner)
            d_raw[at, lanes] = d_inner.astype(BF)
            d_raw[at, feats + j * LANES : feats + (j + 1) * LANES] = (d_forget * open_part * sig).astype(BF)
            total = total + jnp.sum(d_forget * (1.0 - sig), axis=0, keepdims=True)
        d_bound[:, lanes] = total
    d_raw[:, 2 * feats :] = d_gate_raw[...]
    for k, d_part in enumerate(d_parts):
        d_part[...] = d_raw[:, columns_of(x_ref, parts, k, 3 * feats // parts)]


def d_normed_kernel(parts, copies, *refs):
    d_parts, weights, partial = refs[:parts], refs[parts:-1], refs[-1]
    group, deep = partial.shape[0], partial.shape[1] // parts
    for d in range(parts):
        copies.wait(*range(parts + d * parts, parts + (d + 1) * parts))
        for i in range(2):
            at = slice(i * group // 2, (i + 1) * group // 2)
            total = None
            for k, d_part in enumerate(d_parts):
                part = times_transposed(d_part[at, :], weights[d * parts + k][...])
                total = part if total is None else total + part
            partial[at, d * deep : (d + 1) * deep] = total.astype(BF)


def token_grad_kernel(summed, tokens, d_resid, gain, out):
    @pl.loop(0, tokens.shape[0] // STEP)
    def _(i):
        at = pl.ds(i * STEP, STEP)
        value = tokens[at, :].astype(F32)
        inv = inverse_rms(value)
        hat = value * inv
        d = summed[at, :].astype(F32) * gain[...]
        out[at, :] = d_resid[at, :] + inv * (d - hat * mean_last(d * hat))


def after(value, *others):
    return lax.optimization_barrier((value, *others))[0]


def gather_rows(own):
    return lax.all_gather(own, ("z", "c"), axis=0, tiled=True)


def scatter_rows(partial):
    return lax.psum_scatter(partial, ("z", "c"), scatter_dimension=0, tiled=True)


def per_device(
    tokens, lengths, w_in, w_forget, w_gate, w_out, attn_gain, mix_gain, bound_table,
    ff_gate, ff_up, ff_down, mlp_gain, out_grad,
):
    Y = lax.axis_size("y")
    pair = Y == 2
    parts = 2 if pair else 1
    z, y, c, x = (lax.axis_index(a) for a in "zycx")
    rows, width = tokens.shape
    sub = w_in.shape[0]
    feats = Y * sub
    block = ff_gate.shape[1] // CHUNKS
    tall = 3 * block
    group = rows * CHUNKS
    near_y = y[None].astype(jnp.int32)

    def y_first(*values):
        if pair:
            return call(
                functools.partial(reorder_kernel, False),
                [(v.shape, v.dtype) for v in values], near_y, *values, smem=1,
            )
        return [
            v.reshape(v.shape[0], Z, Y, C * sub).transpose(0, 2, 1, 3).reshape(v.shape) for v in values
        ]

    def z_first(*values):
        if pair:
            return call(
                functools.partial(reorder_kernel, True),
                [(v.shape, v.dtype) for v in values], near_y, *values, smem=1,
            )
        return [
            v.reshape(v.shape[0], Y, Z, C * sub).transpose(0, 2, 1, 3).reshape(v.shape) for v in values
        ]

    def over_y(value):
        if pair:
            return [value, swap(value, "y")]
        return [lax.all_gather(value, "y", axis=0, tiled=True)]

    def in_order(value):
        if pair:
            other = swap(value, "y")
            return jnp.concatenate(
                [jnp.where(y == 0, value, other), jnp.where(y == 0, other, value)], axis=0
            )
        return lax.all_gather(value, "y", axis=0, tiled=True)

    def spread(value):
        return lax.all_to_all(value, ("z", "c"), 0, 0, tiled=True)

    def both(own, sent, axis):
        return own.astype(BF).astype(F32) + swap(sent.astype(BF), axis).astype(F32)

    near_x = x[None].astype(jnp.int32)
    z_c = jnp.stack([z, c]).astype(jnp.int32)

    def own_and_neighbours(value):
        corner = lax.ppermute(value, ("y", "x"), [(i, 3 - i) for i in range(4)])
        return [value, swap(value, "x"), swap(value, "y"), corner]

    table_f = bound_table.astype(F32)
    soft = jax.nn.softmax(table_f, axis=0)
    own_bound = jnp.sum(soft[1 : LAYER + 1], axis=0)

    if pair:
        (glu,) = call(glu_blocks_kernel, [((CHUNKS, tall, sub), BF)], ff_gate, ff_up, ff_down)
    else:
        glu = jnp.concatenate([w.T.reshape(CHUNKS, block, sub) for w in (ff_gate, ff_up)], axis=1)
        glu = jnp.concatenate([glu, ff_down.reshape(CHUNKS, block, sub)], axis=1)
    (out_rows,) = y_first(in_order(w_out))

    tokens_y, grad_y = y_first(tokens, out_grad)
    if pair:
        (blocks,) = call(
            mixer_blocks_kernel, [((CHUNKS, sub, 3 * feats // 2), BF)], near_x, w_in, w_forget, w_gate, smem=1
        )
        moved = after(spread(blocks), glu, out_rows)
        small = jnp.stack([attn_gain.astype(F32), mlp_gain.astype(F32), own_bound, mix_gain.astype(F32)])
        small = [small, swap(small, "y")]
        (piece,) = call(
            token_piece_kernel, [((rows, width + LANES), BF)],
            near_y, tokens, jnp.concatenate([v[:2] for v in small]), smem=1,
        )
        tokens_all = gather_rows(after(piece, moved))
        gains = tokens_all.reshape(CHUNKS, rows, -1)[:, :4, width:].astype(F32)
        attn_g, mlp_g = (
            jnp.concatenate([gains[:, k].reshape(1, -1), gains[:, 2 + k].reshape(1, -1)], axis=1) for k in range(2)
        )
        small = jnp.stack([v[2:] for v in small])
        small = jnp.where(y == 0, small, small[::-1])
        mixer = own_and_neighbours(moved.reshape(CHUNKS * sub, 3 * feats // 2))
    else:
        gains = lax.all_gather(jnp.stack([attn_gain, mlp_gain]), ("z", "y", "c"), axis=1, tiled=True)
        attn_g, mlp_g = y_first(gains[:1].astype(F32), gains[1:].astype(F32))
        tokens_all = gather_rows(tokens_y)
        small = in_order(jnp.stack([own_bound, mix_gain.astype(F32)])[None])
        mixer = [
            w.reshape(sub, Z, Y, C, sub).transpose(1, 3, 0, 2, 4).reshape(CHUNKS, sub, feats)
            for w in (w_in, w_forget, w_gate)
        ]
        moved = spread(jnp.concatenate(mixer, axis=2))
        mixer = over_y(moved.reshape(CHUNKS * sub, 3 * feats))
    glu = spread(after(glu, moved))
    bound = small[:, 0].reshape(1, feats)
    mix_g = small[:, 1].reshape(1, feats)

    slot = jnp.arange(lengths.shape[0])
    starts = jnp.sum(jnp.where(slot[None, :] < slot[:, None], lengths[None, :], 0), axis=1)
    slot = jnp.arange(CHUNKS)
    chunk = (slot // C * Y + y) * (C * X) + slot % C * X + x
    position = (chunk[:, None] * rows + jnp.arange(rows)[None, :]).reshape(group)
    keep = 1.0 - jnp.any(position[:, None] == starts[None, :], axis=1).astype(F32)[:, None]
    count = Z * Y * C * X
    number = jnp.arange(count)
    xn, cn = number % X, number // X % C
    yn, zn = number // (X * C) % Y, number // (X * C * Y)
    party = (yn ^ y) * X + (xn ^ x) if pair else yn * X + xn
    order = party * CHUNKS + zn * C + cn
    base = 0 * y if pair else (y * X + x) * CHUNKS
    order = jnp.concatenate([order, jnp.stack([base, z * C + c])]).astype(jnp.int32)

    def parties(value):
        if pair:
            return own_and_neighbours(value)
        return [lax.all_gather(value, ("y", "x"), axis=0, tiled=True)]

    crowd = 4 if pair else 1
    featured = ((feats // LANES, group, LANES), F32)
    normed, raw, decay, local, through, edge = call(
        functools.partial(mixer_forward_kernel, parts),
        [((group, width), BF), ((group, 3 * feats), F32)] + [featured] * 3 + [((2 * CHUNKS, feats), F32)],
        near_x, attn_g, tokens_all, bound, keep, *mixer,
        smem=1, scratch=[pltpu.VMEM(*featured)], late=2,
    )
    edges = parties(edge)
    def assemble(pieces):
        return jnp.concatenate([p.transpose(1, 0, 2).reshape(p.shape[1], -1) for p in pieces], axis=1)

    def around(blocks):
        cut = blocks.shape[1] // 2
        side, up_y = swap(blocks, "x"), swap(blocks, "y")
        corner = [swap(up_y[:, :cut], "x"), swap(side[:, cut:], "y")]
        near, far = assemble([blocks, up_y]), assemble([side, jnp.concatenate(corner, axis=1)])
        return [near, far], (side, up_y), corner

    early, late, last = (), (), ()
    gate_up, down = glu[:, : 2 * block], glu[:, 2 * block :]
    if pair:
        gate_up_w, early, _ = around(after(gate_up, edges[0]))
        down_w, late, last = around(after(down, *early))
    else:
        gate_up_w, down_w = (assemble(over_y(v)) for v in (gate_up, down))
        gate_up_w, down_w = ([v, swap(v, "x")] for v in (gate_up_w, down_w))
    carries = [pltpu.VMEM((Y * X * CHUNKS, feats), F32)] * 3
    states, entry, partial = call(
        functools.partial(mixer_out_kernel, crowd, count),
        [featured, ((CHUNKS, feats), F32), ((group, width + LANES), BF)],
        order, *edges, local, through, raw, mix_g, out_rows,
        smem=1, scratch=carries + [pltpu.VMEM((group, feats), BF)], late=crowd,
    )
    summed = scatter_rows(after(partial, glu))
    own_grad = lax.all_to_all(jnp.broadcast_to(after(grad_y, glu)[None], (Z, rows, width)), "z", 0, 0, tiled=False)
    other_grad = swap(own_grad, "c")
    grad_all = jnp.where(
        c == 0, jnp.stack([own_grad, other_grad], axis=1), jnp.stack([other_grad, own_grad], axis=1)
    ).reshape(group, width)
    resid, hidden, scale = call(
        resid_kernel,
        [((rows, width), F32), ((rows, width), BF), ((rows, LANES), F32)],
        after(summed, own_grad, *early, *late), tokens_y, mlp_g,
    )
    hidden_all = after(gather_rows(hidden), grad_all)
    thin = ((group, block), BF)
    act0, d_gate0, d_up0, act1, d_gate1, d_up1, partial = call(
        glu_kernel, [thin] * 6 + [((group, 2 * width), BF)],
        hidden_all, grad_all, *gate_up_w, *down_w, late=0, scratch=[pltpu.VMEM((group, 2 * width), F32)],
    )
    acts = [act0, act1]

    def weight_pieces(terms, lefts, *rights):
        height = len(terms) * block
        shapes = [((height, width), BF)] * 2
        if pair:
            shapes = [((2, height // 2, width // 2), BF)] * 4
        return call(
            functools.partial(glu_weights_kernel, parts, terms), shapes, *lefts, *rights,
            late=len(lefts) + len(rights),
        )

    def first_swaps(pieces):
        upper, upper_sent, lower, lower_sent = pieces
        return upper, swap(upper_sent, "x"), lower, swap(lower_sent, "y")

    def first_sums(pieces):
        height = pieces[0].shape[1]
        shapes = [((height, width // 2), F32), ((height, width // 2), BF)] * 2
        return call(first_sums_kernel, shapes, *pieces)

    def last_swaps(pieces):
        upper, upper_sent, lower, lower_sent = pieces
        return upper, swap(upper_sent, "y"), lower, swap(lower_sent, "x")

    def last_sums(*pieces):
        height = sum(p.shape[0] for p in pieces[::2])
        return call(last_sums_kernel, [((CHUNKS, height, sub), BF)], *pieces)[0]

    def to_blocks(value):
        return value.reshape(value.shape[0], -1, sub).transpose(1, 0, 2)

    def total_blocks(pieces):
        blocks = to_blocks(both(*pieces, "x").astype(BF))
        return lax.psum_scatter(blocks, "y", scatter_dimension=0, tiled=True)

    summed = scatter_rows(partial)
    gate_up = weight_pieces((0, 0), [d_gate0, d_up0, d_gate1, d_up1], hidden_all)
    down = weight_pieces((0,), acts, grad_all)
    if pair:
        gate_up = first_sums(first_swaps(gate_up))
        down = first_swaps(down)
        summed, *gate_up = lax.optimization_barrier((summed, *gate_up))
    d_resid, piece, result_y = call(
        d_resid_kernel, [((rows, width), F32), ((rows, width + LANES), BF), ((rows, width), BF)],
        summed, resid, tokens_y, grad_y, mlp_g, scale,
    )
    if pair:
        piece, *down = lax.optimization_barrier((piece, *down))
    d_mixed = gather_rows(piece)
    if pair:
        gate_up = last_swaps(gate_up)
        down = last_swaps(first_sums(down))
        glu_grad = last_sums(*gate_up, *down)
        d_mixed, glu_grad = lax.optimization_barrier((d_mixed, glu_grad))

    mixed_in, d_gate_raw, adjoint, passed, first = call(
        mixer_back_kernel,
        [((group, feats), BF)] * 2 + [featured] * 2 + [((CHUNKS, feats), F32)],
        d_mixed, out_rows, raw, states, mix_g, decay,
        scratch=[pltpu.VMEM((group, feats), F32), pltpu.VMEM(*featured)], late=2,
    )
    firsts = parties(first)
    grad_out = mixed_in
    if pair:
        out_pieces = call(
            out_weights_kernel, [((sub, width // 2), BF)] * 4,
            near_y, near_x, mixed_in, d_mixed, smem=2, scratch=[pltpu.VMEM((sub, width), F32)],
        )
        out_pieces = after(out_pieces, *firsts)
        grad_out = sum(
            p.astype(F32)
            for p in (
                out_pieces[0],
                swap(out_pieces[1], "x"),
                swap(out_pieces[2], "y"),
                lax.ppermute(out_pieces[3], ("y", "x"), [(i, 3 - i) for i in range(4)]),
            )
        ).astype(BF)
    if pair:
        glu_grad = after(glu_grad, first)
    else:
        glu_grad = jnp.concatenate([total_blocks(gate_up), total_blocks(down)], axis=1)
    glu_grad = spread(glu_grad)
    *d_raw, part_bound = call(
        functools.partial(d_mixer_kernel, crowd, parts, count),
        [((group, 3 * feats // parts), BF)] * parts
        + [((1, feats), F32)],
        near_x, order, *edges, *firsts, adjoint, passed, states, entry, raw, keep, bound, d_gate_raw,
        smem=2, scratch=carries + [pltpu.VMEM((group, 3 * feats), BF)], late=2 * crowd,
    )

    pieces = call(
        functools.partial(mixer_weights_kernel, parts),
        [((width // parts, 3 * feats // parts), BF)] * parts**2,
        normed, *d_raw, late=1 + parts,
    )
    (partial,) = call(
        functools.partial(d_normed_kernel, parts), [((group, width), BF)],
        *after(d_raw, grad_out, *pieces), *mixer, late=parts,
    )
    (token_grad_y,) = call(
        token_grad_kernel, [((rows, width), F32)],
        scatter_rows(partial), tokens_y, d_resid, attn_g,
    )
    result, token_grad = z_first(result_y, token_grad_y)

    part_bound = part_bound.reshape(feats)
    if pair:
        pieces = [
            pieces[0],
            swap(pieces[1], "x"),
            swap(pieces[2], "y"),
            lax.ppermute(pieces[3], ("y", "x"), [(i, 3 - i) for i in range(4)]),
        ]
        top, bottom = jnp.split(part_bound, 2)
        d_bound = jnp.where(y == 0, top, bottom) + swap(jnp.where(y == 0, bottom, top), "y")
        pieces = after(pieces, d_bound)
        shape = (2, sub, 3 * feats // 2)
        theirs, *mine = call(
            mixer_sums_kernel, [((Z, *shape[1:]), BF)] + [(shape, BF)] * Z, z_c, *pieces, smem=1
        )
        got = swap(theirs, "c")
        d_bound = after(d_bound, got)
        mine = [v.at[1].set(got[k]) for k, v in enumerate(mine)]
        mixer_grad = [mine[0]] + [lax.ppermute(mine[k], "z", [(i, i ^ k) for i in range(Z)]) for k in range(1, Z)]
    else:
        d_bound = lax.psum_scatter(part_bound, "y", scatter_dimension=0, tiled=True)
        mixer_grad = lax.psum_scatter(pieces[0], "y", scatter_dimension=0, tiled=True)
        mixer_grad = both(mixer_grad, mixer_grad, "x").astype(BF)
        mixer_grad = spread(mixer_grad.reshape(CHUNKS, sub, 3 * feats))
    if pair:
        grad_gate_ff, grad_up_ff, grad_down, along_ff = call(
            glu_grads_kernel,
            [((sub, CHUNKS * block), F32)] * 2 + [((CHUNKS * block, sub), F32), ((sub, LANES), F32)],
            glu_grad, ff_gate, ff_up,
        )
        grad_mlp = along_ff[:, 0]
        grad_mlp = grad_mlp + swap(grad_mlp, "x")
        d_bound = d_bound + swap(d_bound, "x")
        mixer_grad[-1] = after(mixer_grad[-1], grad_out, d_bound, grad_mlp)
        mixer_grad = mixer_grad + [swap(v, "x") for v in mixer_grad]
        other = swap(grad_out, "x")
        grad_out = jnp.concatenate(
            [jnp.where(x == 0, grad_out, other), jnp.where(x == 0, other, grad_out)], axis=1
        ).astype(F32)
    else:
        (grad_out,) = z_first(contract_rows(mixed_in, d_mixed[:, :width]).astype(BF))
        grad_out = lax.psum_scatter(grad_out, "y", scatter_dimension=0, tiled=True)
        grad_out = both(grad_out, grad_out, "x")
        d_bound = d_bound + swap(d_bound, "x")
    row_ids = jnp.arange(bound_table.shape[0])[:, None]
    member = jnp.logical_and(row_ids >= 1, row_ids <= LAYER).astype(F32)
    grad_table = soft * (member - own_bound[None, :]) * d_bound[None, :]

    def along(weight, grad):
        return jnp.sum(weight.astype(F32) * grad, axis=1)

    square = ((sub, width), F32)
    if pair:
        grad_in, grad_forget, grad_gate, grad_attn = call(
            mixer_grads_kernel, [square] * 3 + [((sub, LANES), F32)],
            jnp.concatenate([near_x, z_c]), *mixer_grad, w_in, w_forget, w_gate, smem=1, late=2 * Z + 3,
        )
        grad_attn = grad_attn[:, 0]
    else:
        mixer_grad = mixer_grad.reshape(Z, C, sub, 3, Y, sub).transpose(3, 2, 0, 4, 1, 5)
        grad_in, grad_forget, grad_gate = mixer_grad.reshape(3, sub, width).astype(F32)
        grad_attn = along(w_in, grad_in) + along(w_forget, grad_forget) + along(w_gate, grad_gate)
        grad_gate_ff, grad_up_ff = (
            glu_grad[:, k * block : (k + 1) * block].astype(F32).reshape(CHUNKS * block, sub).T for k in range(2)
        )
        grad_down = glu_grad[:, 2 * block :].reshape(CHUNKS * block, sub).astype(F32)
        grad_mlp = along(ff_gate, grad_gate_ff) + along(ff_up, grad_up_ff)
        grad_mlp = grad_mlp + swap(grad_mlp, "x")
    grad_attn = grad_attn / attn_gain.astype(F32)
    grad_mix = along(w_out, grad_out) / mix_gain.astype(F32)
    grad_mlp = grad_mlp / mlp_gain.astype(F32)
    return (
        result, token_grad, grad_in, grad_forget, grad_gate, grad_out, grad_attn, grad_mix,
        grad_table, grad_gate_ff, grad_up_ff, grad_down, grad_mlp,
    )


def solution(mesh):
    dp, mp = mesh.devices.shape
    grid = Mesh(mesh.devices.reshape(Z, dp // CHUNKS, C, mp), ("z", "y", "c", "x"))
    dp_axes = ("z", "y", "c")
    every = ("z", "y", "c", "x")
    mat, row, gain = P(dp_axes, None), P(every, None), P(dp_axes)
    table, glu, glu_down = P(None, dp_axes), P(dp_axes, "x"), P("x", dp_axes)
    return jax.shard_map(
        per_device,
        mesh=grid,
        in_specs=(
            row, P(), mat, mat, mat, mat, gain, gain, table, glu, glu, glu_down, gain, row,
        ),
        out_specs=(
            row, row, mat, mat, mat, mat, gain, gain, table, glu, glu, glu_down, gain,
        ),
        check_vma=False,
    )
```
